32 devices in a mesh: wide: 8 (over z, x), narrow: 4 (over y, core).
Axes of the slice: x: 2, y: 2, z: 4, core: 2. Of those that a mesh axis runs over, the one named last changes fastest.
Arguments:
- hidden_in: bfloat16 [16384, 1024], P(('wide', 'narrow')), may hold values from -6 to 6
- grad_out: bfloat16 [16384, 1024], P(('wide', 'narrow')), may hold values from -6 to 6
- gain_attn: bfloat16 [1024], replicated, may hold values from 0.5 to 1.5
- gain_ffn: bfloat16 [1024], replicated, may hold values from 0.5 to 1.5
- w_query: bfloat16 [1024, 1024], P(None, 'narrow'), may hold values from -0.046875 to 0.046875
- w_key: bfloat16 [1024, 1024], P(None, 'narrow'), may hold values from -0.1875 to 0.1875
- w_value: bfloat16 [1024, 1024], P(None, 'narrow'), may hold values from -0.1875 to 0.1875
- w_output: bfloat16 [1024, 1024], P('narrow'), may hold values from -0.75 to 0.75
- table_rel: bfloat16 [32, 16], P(None, 'narrow'), may hold values from -4 to 4
- table_horiz: bfloat16 [32, 16], P(None, 'narrow'), may hold values from -4 to 4
- table_vert: bfloat16 [32, 16], P(None, 'narrow'), may hold values from -4 to 4
- wi_gate: bfloat16 [1024, 2816], P(None, 'narrow'), may hold values from -0.1875 to 0.1875
- wi_up: bfloat16 [1024, 2816], P(None, 'narrow'), may hold values from -0.1875 to 0.1875
- wo_ffn: bfloat16 [2816, 1024], P('narrow'), may hold values from -0.21875 to 0.21875
- counts: int32 [32], P('wide'), may hold values from 1 to 256
- patch_mask: int32 [32, 256], P('wide'), may hold values 0 or 1
- bucket_rel: int32 [32, 512, 512], P('wide'), may hold values from 0 to 31
- bucket_horiz: int32 [32, 512, 512], P('wide'), may hold values from 0 to 31
- bucket_vert: int32 [32, 512, 512], P('wide'), may hold values from 0 to 31
Outputs:
- block_out: bfloat16 [16384, 1024], P(('wide', 'narrow'))
- grad_input: float32 [16384, 1024], P(('wide', 'narrow'))
- grad_gain_attn: float32 [1024], P(('wide', 'narrow'))
- grad_gain_ffn: float32 [1024], P(('wide', 'narrow'))
- grad_w_query: float32 [1024, 1024], P('wide', 'narrow')
- grad_w_key: float32 [1024, 1024], P('wide', 'narrow')
- grad_w_value: float32 [1024, 1024], P('wide', 'narrow')
- grad_w_output: float32 [1024, 1024], P('narrow', 'wide')
- grad_table_rel: float32 [32, 16], P('wide', 'narrow')
- grad_table_horiz: float32 [32, 16], P('wide', 'narrow')
- grad_table_vert: float32 [32, 16], P('wide', 'narrow')
- grad_wi_gate: float32 [1024, 2816], P('wide', 'narrow')
- grad_wi_up: float32 [1024, 2816], P('wide', 'narrow')
- grad_wo_ffn: float32 [2816, 1024], P('narrow', 'wide')
The draws below stay inside these ranges and needn't reach their ends.
All inputs are finite; a program needn't handle non-finite values. No bound on the sum of `patch_mask` on one device may be relied on, other than what follows from the above.
Results may differ from the reference program's by a relative error of at most 0.02.
Values may be sent and summed in bfloat16 or wider, within the bound.
A program may use at most 256 MiB of HBM per device.

```python
import jax
import jax.numpy as jnp
from jax import lax

D = 1024
HEADS = 16
HEAD_DIM = 64
FF = 2816
BUCKETS = 32
SLOTS = 512
TEXT = 256
PATCHES = 256
PAGES_ALL = 32
TOKENS = 16384


def place_ends(entries, rng, low, largest):
    longest = entries.shape.index(max(entries.shape))
    spots = []
    for shift in (0, 1):
        where = [jax.random.randint(jax.random.fold_in(rng, axis), (), 0, length) for axis, length in enumerate(entries.shape)]
        where[longest] = (where[longest] + shift) % entries.shape[longest]
        spots.append(tuple(where))
    return entries.at[spots[0]].set(low).at[spots[1]].set(largest)


def strengthened(values, stream_key, source, target, parts, factor):
    owner, partner = [(jnp.arange(values.shape[position]) // (values.shape[position] // parts)).reshape([-1 if axis == position else 1 for axis in range(values.ndim)]) for position in (source, target)]
    chosen = jax.random.permutation(stream_key, parts)[partner]
    strong = (owner == chosen) | (owner == (partner + parts // 2) % parts)
    return jnp.where(strong, factor * values, values)


def levels(rng, extent, shards, low, top_value):
    factor_of = 1.0
    for axis_at, parts in shards:
        heights = jax.random.uniform(jax.random.fold_in(jax.random.fold_in(rng, 6), axis_at), (parts,), jnp.float32, low / len(shards), top_value / len(shards))
        factor_of = factor_of * jnp.repeat(jnp.exp(heights), extent[axis_at] // parts).reshape((-1,) + (1,) * (len(extent) - 1 - axis_at))
    return factor_of


def scatter_about(rng, shape, scale, limit, pieces=(), kind=jnp.bfloat16):
    array = jax.random.normal(rng, shape, jnp.float32) * scale
    if len(pieces) > 0:
        array = levels(rng, shape, pieces, -0.22, 0.18) * array
    return jnp.clip(array, min=-limit, max=limit).astype(kind)


def noise_with(rng, shape, deviation, limit, cuts, heavy, kind=jnp.bfloat16):
    drawn = deviation * jax.random.normal(rng, shape, jnp.float32)
    if cuts:
        drawn = drawn * levels(rng, shape, cuts, -0.22, 0.18)
    return jnp.clip(strengthened(drawn, jax.random.fold_in(rng, 3), *heavy), -limit, limit).astype(kind)


def setup_inputs(seed: int = 0) -> dict:
    arg_keys = jax.random.split(jax.random.key(seed), 20)
    hidden_in = noise_with(arg_keys[0], (TOKENS, D), 1.0, 6.0, ((0, 32),), (0, 1, 32, 2.75))
    grad_out = noise_with(arg_keys[1], (TOKENS, D), 1.0, 6.0, ((0, 32),), (0, 1, 32, 2.75))
    gain_attn = jnp.clip(1.0 + 0.1 * jax.random.normal(arg_keys[2], (D,), jnp.float32), 0.5, 1.5).astype(jnp.bfloat16)
    gain_ffn = jnp.clip(1.0 + 0.1 * jax.random.normal(arg_keys[3], (D,), jnp.float32), 0.5, 1.5).astype(jnp.bfloat16)
    w_query = scatter_about(arg_keys[4], (D, HEADS * HEAD_DIM), (16 * D) ** -0.5, 0.046875, ((1, 4),))
    w_key = scatter_about(arg_keys[5], (D, HEADS * HEAD_DIM), D ** -0.5, 0.1875, ((1, 4),))
    w_value = scatter_about(arg_keys[6], (D, HEADS * HEAD_DIM), D ** -0.5, 0.1875, ((1, 4),))
    w_output = scatter_about(arg_keys[7], (HEADS * HEAD_DIM, D), (HEADS * HEAD_DIM // 16) ** -0.5, 0.75, ((0, 4),))
    table_rel = scatter_about(arg_keys[8], (BUCKETS, HEADS), 1.0, 4.0, ((1, 4),))
    table_horiz = scatter_about(arg_keys[9], (BUCKETS, HEADS), 1.0, 4.0, ((1, 4),))
    table_vert = scatter_about(arg_keys[10], (BUCKETS, HEADS), 1.0, 4.0, ((1, 4),))
    wi_gate = scatter_about(arg_keys[11], (D, FF), D ** -0.5, 0.1875, ((1, 4),))
    wi_up = scatter_about(arg_keys[12], (D, FF), D ** -0.5, 0.1875, ((1, 4),))
    wo_ffn = scatter_about(arg_keys[13], (FF, D), (FF // 4) ** -0.5, 0.21875, ((0, 4),))
    counts = place_ends(jax.random.randint(arg_keys[14], (PAGES_ALL,), 1, TEXT + 1), jax.random.fold_in(arg_keys[14], 1), 1, TEXT).astype(jnp.int32)
    patch_mask = place_ends((jax.random.randint(arg_keys[15], (PAGES_ALL, PATCHES), 0, 4) < 3).astype(jnp.int32), jax.random.fold_in(arg_keys[15], 1), 0, 1)
    bucket_rel = place_ends(jax.random.randint(arg_keys[16], (PAGES_ALL, SLOTS, SLOTS), 0, BUCKETS), jax.random.fold_in(arg_keys[16], 1), 0, BUCKETS - 1).astype(jnp.int32)
    bucket_horiz = place_ends(jax.random.randint(arg_keys[17], (PAGES_ALL, SLOTS, SLOTS), 0, BUCKETS), jax.random.fold_in(arg_keys[17], 1), 0, BUCKETS - 1).astype(jnp.int32)
    bucket_vert = place_ends(jax.random.randint(arg_keys[18], (PAGES_ALL, SLOTS, SLOTS), 0, BUCKETS), jax.random.fold_in(arg_keys[18], 1), 0, BUCKETS - 1).astype(jnp.int32)
    return dict(hidden_in=hidden_in, grad_out=grad_out, gain_attn=gain_attn, gain_ffn=gain_ffn, w_query=w_query, w_key=w_key, w_value=w_value, w_output=w_output, table_rel=table_rel, table_horiz=table_horiz, table_vert=table_vert, wi_gate=wi_gate, wi_up=wi_up, wo_ffn=wo_ffn, counts=counts, patch_mask=patch_mask, bucket_rel=bucket_rel, bucket_horiz=bucket_horiz, bucket_vert=bucket_vert)


EPS = 1e-06

@jax.custom_vjp
def low(v):
    return lax.optimization_barrier(v.astype(jnp.bfloat16)).astype(jnp.float32)

@jax.custom_vjp
def low_back(v):
    return v

def low_keep(v):
    return (low(v), None)

def low_pass(kept, grad):
    return (grad,)

def back_keep(v):
    return (v, None)

def back_low(kept, grad):
    return (low(grad),)
low.defvjp(low_keep, low_pass)
low_back.defvjp(back_keep, back_low)

def round_both(value):
    return low(low_back(value))

def exact_dot(left, right):
    return jnp.dot(left, right, precision=lax.Precision.HIGHEST)

def rms_norm(row_data, gain_vec):
    return row_data * lax.rsqrt(lax.optimization_barrier(jnp.mean(row_data * row_data, axis=-1, keepdims=True)) + EPS) * gain_vec

def page_attention(tables, page_data):
    table_rel, table_horiz, table_vert = tables
    queries, key_rows, values, bucket_rel, bucket_horiz, bucket_vert, valid = page_data
    scores = jnp.einsum('ihd,jhd->hij', queries, key_rows, precision=lax.Precision.HIGHEST)
    bias = table_rel[bucket_rel] + table_horiz[bucket_horiz] + table_vert[bucket_vert]
    scores = low_back(scores + jnp.transpose(bias, (2, 0, 1)))
    scores = jnp.where(valid[None, None, :] == 1, scores, -1000000000.0)
    probs = low(jax.nn.softmax(scores, axis=-1))
    context = jnp.einsum('hij,jhd->ihd', probs, values, precision=lax.Precision.HIGHEST)
    return context.reshape(context.shape[0], -1)

def forward_block(params, resid, bucket_rel, bucket_horiz, bucket_vert, valid):
    gain_attn, gain_ffn, w_query, w_key, w_value, w_output, table_rel, table_horiz, table_vert, wi_gate, wi_up, wo_ffn = params
    page_count = bucket_rel.shape[0]
    normed = low(rms_norm(resid, gain_attn))
    queries = round_both(exact_dot(normed, w_query)).reshape(page_count, SLOTS, HEADS, HEAD_DIM)
    key_rows = round_both(exact_dot(normed, w_key)).reshape(page_count, SLOTS, HEADS, HEAD_DIM)
    values = round_both(exact_dot(normed, w_value)).reshape(page_count, SLOTS, HEADS, HEAD_DIM)
    tables = (table_rel, table_horiz, table_vert)
    context = lax.map(lambda page_data: jax.checkpoint(page_attention)(tables, page_data), (queries, key_rows, values, bucket_rel, bucket_horiz, bucket_vert, valid))
    context = round_both(context.reshape(resid.shape[0], -1))
    middle = resid + low_back(exact_dot(context, w_output))
    normed_ffn = low(rms_norm(middle, gain_ffn))
    gate = low_back(exact_dot(normed_ffn, wi_gate))
    upper = low_back(exact_dot(normed_ffn, wi_up))
    hidden = low(jax.nn.gelu(gate, approximate=True) * upper)
    return middle + low_back(exact_dot(hidden, wo_ffn))

def reference(hidden_in, grad_out, gain_attn, gain_ffn, w_query, w_key, w_value, w_output, table_rel, table_horiz, table_vert, wi_gate, wi_up, wo_ffn, counts, patch_mask, bucket_rel, bucket_horiz, bucket_vert):
    params = tuple((item.astype(jnp.float32) for item in (gain_attn, gain_ffn, w_query, w_key, w_value, w_output, table_rel, table_horiz, table_vert, wi_gate, wi_up, wo_ffn)))
    positions = jnp.arange(SLOTS, dtype=jnp.int32)
    text_valid = (positions[None, :TEXT] < counts[:, None]).astype(jnp.int32)
    valid = jnp.concatenate([text_valid, patch_mask.astype(jnp.int32)], axis=1)
    step_pages = 1
    for candidate in range(1, PAGES_ALL + 1):
        if PAGES_ALL % candidate == 0 and candidate * SLOTS <= 4096:
            step_pages = candidate
    rounds = PAGES_ALL // step_pages
    inputs = hidden_in.astype(jnp.float32).reshape(rounds, step_pages * SLOTS, D)
    cotangents = grad_out.astype(jnp.float32).reshape(rounds, step_pages * SLOTS, D)
    shaped_ids = tuple((item.reshape(rounds, step_pages, SLOTS, SLOTS) for item in (bucket_rel, bucket_horiz, bucket_vert)))
    shaped_valid = valid.reshape(rounds, step_pages, SLOTS)

    def one_round(totals, item):
        resid, cotangent, ids_rel, ids_horiz, ids_vert, valid_now = item
        block_out, pull = jax.vjp(lambda prm, rows: forward_block(prm, rows, ids_rel, ids_horiz, ids_vert, valid_now), params, resid)
        grad_params, grad_rows = pull(cotangent)
        return (tuple((total + grad for total, grad in zip(totals, grad_params))), (block_out, grad_rows))
    zeros = tuple((jnp.zeros_like(item) for item in params))
    totals, (outputs, grad_rows) = lax.scan(one_round, zeros, (inputs, cotangents) + shaped_ids + (shaped_valid,))
    return (outputs.reshape(TOKENS, D).astype(jnp.bfloat16), grad_rows.reshape(TOKENS, D), totals[0], totals[1], totals[2], totals[3], totals[4], totals[5], totals[6], totals[7], totals[8], totals[9], totals[10], totals[11])
```

```python
import functools
import math

import jax
import jax.numpy as jnp
from jax import lax
from jax.experimental import pallas as pl
from jax.experimental.pallas import tpu as pltpu
from jax.sharding import PartitionSpec as P

F32 = jnp.float32
BF = jnp.bfloat16
I32 = jnp.int32
HEAD_DIM = 64
LANES = 128
EPS = 1e-06
NT = (((1,), (1,)), ((), ()))
TN = (((0,), (0,)), ((), ()))

FIXED = 2048.0
OFFSET = 8192
MASKED = -3.0e12
VMEM_LIMIT = 56 << 20


def lookup(table_row, ids):
    return jnp.take_along_axis(table_row, ids, axis=1, mode="promise_in_bounds")


def attn_fwd_body(
    heads, chunk, page_ref, normed_ref, w_ref, tab_ref, ir_ref, ih_ref, iv_ref, valid_ref,
    qkv_ref, p_ref, ctx_ref, linv_ref, kx_ref, vx_ref,
):
    hd = HEAD_DIM
    rows, slots = ir_ref.shape[1], ir_ref.shape[2]
    hw, pw = heads * hd, 2 * hd

    @pl.when(pl.program_id(0) == 0)
    def _():
        qkv_ref[...] = jnp.dot(normed_ref[...], w_ref[...], preferred_element_type=F32).astype(BF)
        lane = lax.broadcasted_iota(I32, (slots, pw), 1)
        shown = jnp.broadcast_to(valid_ref[...], (slots, pw)) > 0.5
        mask_col = jnp.where(lane == 0, jnp.where(shown, 0.0, MASKED), 0.0).astype(BF)
        ones = jnp.ones((slots, pw), BF)
        for pair in range(heads // 2):
            kx_ref[pair, :, :pw] = qkv_ref[:, hw + pair * pw : hw + (pair + 1) * pw]
            kx_ref[pair, :, pw:] = mask_col
            vx_ref[pair, :, :pw] = qkv_ref[:, 2 * hw + pair * pw : 2 * hw + (pair + 1) * pw]
            vx_ref[pair, :, pw:] = ones

    base = pl.program_id(0) * rows
    lane = lax.broadcasted_iota(I32, (chunk, pw), 1)
    low = lane < hd
    first = jnp.where(lane == 0, 1.0, 0.0).astype(BF)
    to_log2 = math.log2(math.e) / FIXED

    def step(c, carry):
        r0 = pl.multiple_of(c * chunk, chunk)
        g0 = pl.multiple_of(base + c * chunk, chunk)
        for pair in range(heads // 2):
            q2 = qkv_ref[pl.ds(g0, chunk), pair * pw : (pair + 1) * pw] * jnp.bfloat16(FIXED)
            zero = jnp.zeros_like(q2)
            kx, vx = kx_ref[pair], vx_ref[pair]
            scores = []
            for sub in range(2):
                q = jnp.where(low, q2, zero) if sub == 0 else jnp.where(low, zero, q2)
                q = jnp.concatenate([q, first], axis=1)
                scores.append(lax.dot_general(q, kx, NT, preferred_element_type=F32))
            tabs = [jnp.broadcast_to(tab_ref[t, pair : pair + 1, :], (chunk, LANES)) for t in range(3)]
            parts = ([], [])
            for j in range(slots // LANES):
                sl = slice(j * LANES, (j + 1) * LANES)
                bias = (
                    lookup(tabs[0], ir_ref[0, pl.ds(r0, chunk), sl])
                    + lookup(tabs[1], ih_ref[0, pl.ds(r0, chunk), sl])
                    + lookup(tabs[2], iv_ref[0, pl.ds(r0, chunk), sl])
                )
                parts[0].append(scores[0][:, sl] + (bias & 0xFFFF).astype(F32))
                parts[1].append(scores[1][:, sl] + (bias >> 16).astype(F32))
            outs = []
            for sub in range(2):
                s = jnp.concatenate(parts[sub], axis=1)
                peak = jnp.max(s, axis=1, keepdims=True)
                e = jnp.exp2((s - peak) * to_log2).astype(BF)
                p_ref[pair * 2 + sub, pl.ds(r0, chunk), :] = e
                outs.append(jnp.dot(e, vx, preferred_element_type=F32))
            linv = 1.0 / jnp.where(low, outs[0][:, pw:], outs[1][:, pw:])
            linv_ref[pl.ds(r0, chunk), pair * pw : (pair + 1) * pw] = linv
            ctx = jnp.where(low, outs[0][:, :pw], outs[1][:, :pw]) * linv
            ctx_ref[pl.ds(r0, chunk), pair * pw : (pair + 1) * pw] = ctx.astype(BF)
        return carry

    lax.fori_loop(0, rows // chunk, step, 0)


def attn_fwd(page, normed, w, tab, ids, valid, heads, rows=256, chunk=256):
    slots, d = normed.shape
    hw, pw = heads * HEAD_DIM, 2 * HEAD_DIM
    full = lambda *sh: pl.BlockSpec(sh, lambda i, n: (0,) * len(sh))
    id_spec = pl.BlockSpec((1, rows, slots), lambda i, n: (n[0], i, 0))
    row_spec = pl.BlockSpec((rows, hw), lambda i, n: (i, 0))
    grid_spec = pltpu.PrefetchScalarGridSpec(
        num_scalar_prefetch=1,
        grid=(slots // rows,),
        in_specs=[full(slots, d), full(d, 3 * hw), full(*tab.shape), id_spec, id_spec, id_spec, full(slots, 1)],
        out_specs=[
            full(slots, 3 * hw),
            pl.BlockSpec((heads, rows, slots), lambda i, n: (0, i, 0)),
            row_spec,
            row_spec,
        ],
        scratch_shapes=[pltpu.VMEM((heads // 2, slots, 2 * pw), BF)] * 2,
    )
    return pl.pallas_call(
        functools.partial(attn_fwd_body, heads, chunk),
        grid_spec=grid_spec,
        out_shape=[
            jax.ShapeDtypeStruct((slots, 3 * hw), BF),
            jax.ShapeDtypeStruct((heads, slots, slots), BF),
            jax.ShapeDtypeStruct((slots, hw), BF),
            jax.ShapeDtypeStruct((slots, hw), F32),
        ],
        compiler_params=pltpu.CompilerParams(vmem_limit_bytes=VMEM_LIMIT),
        cost_estimate=pl.CostEstimate(
            flops=10 * slots * d * hw, bytes_accessed=10 << 20, transcendentals=heads * slots * slots
        ),
        name="attn_fwd",
    )(page, normed, w, tab, *ids, valid)


def attn_bwd_body(
    heads, ga_ref, wo_ref, ctx_ref, linv_ref, q_ref, k_ref, v_ref, p_ref,
    dq_ref, dk_ref, dv_ref, ds_ref, do_ref,
):
    hd, pw = HEAD_DIM, 2 * HEAD_DIM
    slots = ga_ref.shape[0]
    pair = pl.program_id(0)

    @pl.when(pair == 0)
    def _():
        d = lax.dot_general(ga_ref[...], wo_ref[...], NT, preferred_element_type=F32)
        for p in range(heads // 2):
            do_ref[p] = (d[:, p * pw : (p + 1) * pw] * linv_ref[:, p * pw : (p + 1) * pw]).astype(BF)

    lane = lax.broadcasted_iota(I32, (slots, pw), 1)
    low = lane < hd
    do2 = do_ref[pair]
    prod = do2.astype(F32) * ctx_ref[...].astype(F32)
    q2, k2, v2 = q_ref[...], k_ref[...], v_ref[...]
    vx = jnp.concatenate([v2, jnp.where(lane < 2, 1.0, 0.0).astype(BF)], axis=1)
    do_t, q_t = do2.T, q2.T
    zero = jnp.zeros_like(do2)
    dq, dk, dv = [], [], []
    for sub in range(2):
        mine = low if sub == 0 else jnp.logical_not(low)
        row = -jnp.sum(jnp.where(mine, prod, 0.0), axis=1, keepdims=True)
        head_part = row.astype(BF).astype(F32)
        extra = jnp.where(lane == 0, head_part, jnp.where(lane == 1, row - head_part, 0.0)).astype(BF)
        dox = jnp.concatenate([jnp.where(mine, do2, zero), extra], axis=1)
        t = lax.dot_general(dox, vx, NT, preferred_element_type=F32)
        e = p_ref[sub]
        ds = (e.astype(F32) * t).astype(BF)
        ds_ref[sub] = ds
        dv.append(jnp.dot(do_t[sub * hd : (sub + 1) * hd], e, preferred_element_type=F32))
        dk.append(jnp.dot(q_t[sub * hd : (sub + 1) * hd], ds, preferred_element_type=F32))
        dq.append(jnp.dot(ds, k2, preferred_element_type=F32))
    dq_ref[...] = jnp.where(low, dq[0], dq[1]).astype(BF)
    dk_ref[...] = jnp.concatenate(dk, axis=0).T.astype(BF)
    dv_ref[...] = jnp.concatenate(dv, axis=0).T.astype(BF)


def attn_bwd(ga, wo, ctx, linv, qkv, p, heads):
    slots, d = ga.shape
    hw, pw, pairs = heads * HEAD_DIM, 2 * HEAD_DIM, heads // 2
    full = lambda *sh: pl.BlockSpec(sh, lambda i: (0,) * len(sh))
    col = lambda off: pl.BlockSpec((slots, pw), lambda i: (0, off + i))
    block = pl.BlockSpec((2, slots, slots), lambda i: (i, 0, 0))
    return pl.pallas_call(
        functools.partial(attn_bwd_body, heads),
        grid=(pairs,),
        in_specs=[full(slots, d), full(hw, d), col(0), full(slots, hw), col(0), col(pairs), col(2 * pairs), block],
        out_specs=[col(0), col(0), col(0), block],
        scratch_shapes=[pltpu.VMEM((pairs, slots, pw), BF)],
        out_shape=[jax.ShapeDtypeStruct((slots, hw), BF)] * 3 + [jax.ShapeDtypeStruct((heads, slots, slots), BF)],
        compiler_params=pltpu.CompilerParams(vmem_limit_bytes=VMEM_LIMIT),
        cost_estimate=pl.CostEstimate(flops=6 * slots * d * hw, bytes_accessed=8 << 20, transcendentals=0),
        name="attn_bwd",
    )(ga, wo, ctx, linv, qkv, qkv, qkv, p)


def table_body(heads, buckets, blk, page_ref, ir_ref, ih_ref, iv_ref, *rest):
    ds_refs, (out_ref, acc_ref) = rest[:-2], rest[-2:]

    @pl.when(pl.program_id(0) == 0)
    def _():
        acc_ref[...] = jnp.zeros_like(acc_ref)

    rows, slots = ir_ref.shape[1], ir_ref.shape[2]
    one, zero = jnp.ones((blk, slots), BF), jnp.zeros((blk, slots), BF)

    def step(c, carry):
        r0 = pl.multiple_of(c * blk, blk)
        g = jnp.concatenate([r[h, pl.ds(r0, blk), :] for r in ds_refs for h in range(r.shape[0])], axis=0)
        for t, ref in enumerate((ir_ref, ih_ref, iv_ref)):
            ids = ref[0, pl.ds(r0, blk), :].astype(F32).astype(BF)
            hot = jnp.concatenate([jnp.where(ids == jnp.bfloat16(b), one, zero) for b in range(buckets)], axis=0)
            span = slice(t * buckets * blk, (t + 1) * buckets * blk)
            acc_ref[span, :] += lax.dot_general(hot, g, NT, preferred_element_type=F32)
        return carry

    lax.fori_loop(0, rows // blk, step, 0)

    @pl.when(pl.program_id(0) == pl.num_programs(0) - 1)
    def _():
        n = heads * blk
        same = lax.broadcasted_iota(I32, (blk, n), 0) == (lax.broadcasted_iota(I32, (blk, n), 1) & (blk - 1))
        for b in range(3 * buckets):
            rows_b = jnp.where(same, acc_ref[b * blk : (b + 1) * blk, :], 0.0)
            out_ref[b : b + 1, :] = jnp.sum(rows_b, axis=0, keepdims=True)


def table_grads(page, ids, dss, buckets, rows=64, blk=16):
    heads = sum(d.shape[0] for d in dss)
    slots = ids[0].shape[1]
    id_spec = pl.BlockSpec((1, rows, slots), lambda i, n: (n[0], i, 0))
    grid_spec = pltpu.PrefetchScalarGridSpec(
        num_scalar_prefetch=1,
        grid=(slots // rows,),
        in_specs=[id_spec] * 3 + [pl.BlockSpec((d.shape[0], rows, slots), lambda i, n: (0, i, 0)) for d in dss],
        out_specs=pl.BlockSpec((3 * buckets, heads * blk), lambda i, n: (0, 0)),
        scratch_shapes=[pltpu.VMEM((3 * buckets * blk, heads * blk), F32)],
    )
    out = pl.pallas_call(
        functools.partial(table_body, heads, buckets, blk),
        grid_spec=grid_spec,
        out_shape=jax.ShapeDtypeStruct((3 * buckets, heads * blk), F32),
        compiler_params=pltpu.CompilerParams(vmem_limit_bytes=VMEM_LIMIT),
        cost_estimate=pl.CostEstimate(
            flops=6 * buckets * blk * heads * slots * slots, bytes_accessed=12 << 20, transcendentals=0
        ),
        name="table_grads",
    )(page, *ids, *dss)
    return out.reshape(3 * buckets, heads, blk).sum(-1)


def pack_tables(tab):
    fixed = jnp.round(tab.astype(F32) * FIXED).astype(I32)
    words = fixed[:, 1::2] * 65536 + fixed[:, 0::2] + OFFSET
    return jnp.pad(words, ((0, 0), (0, 8 - words.shape[1]), (0, LANES - words.shape[2])))


def swap(x, axis, bit, size):
    return lax.ppermute(x, axis, [(i, i ^ bit) for i in range(size)])


def after(x, *others):
    return lax.optimization_barrier((x,) + others)[0]


def scatter_wide(x, size, kind):
    left = size
    while left > 1:
        bit = size // left
        side = (lax.axis_index("wide") // bit) % 2
        view = x.reshape((left // 2, 2) + x.shape[1:])
        keep = lax.dynamic_index_in_dim(view, side, 1, False)
        send = lax.dynamic_index_in_dim(view, 1 - side, 1, False).astype(kind)
        x = keep.astype(F32) + swap(send, "wide", bit, size).astype(F32)
        left //= 2
        if left > 1:
            x = x.astype(kind)
    return x[0]


def rms_forward(row_data, gain_vec):
    inv_rms = lax.rsqrt(jnp.mean(row_data * row_data, axis=-1, keepdims=True) + EPS)
    return (row_data * inv_rms * gain_vec, inv_rms)


def rms_backward(upstream, row_data, inv_rms, gain_vec):
    lifted = upstream * gain_vec
    inner = jnp.mean(lifted * row_data, axis=-1, keepdims=True)
    grad_rows = inv_rms * lifted - row_data * inv_rms * inv_rms * inv_rms * inner
    grad_gain = jnp.sum(upstream * row_data * inv_rms, axis=0)
    return (grad_rows, grad_gain)


def gated(gate, upper):
    return jax.nn.gelu(gate, approximate=True) * upper


def dot(a, b):
    return jnp.dot(a, b, preferred_element_type=F32)


def dot_nt(a, b):
    return lax.dot_general(a, b, NT, preferred_element_type=F32)


def dot_tn(a, b):
    return lax.dot_general(a, b, TN, preferred_element_type=F32)


def shards(
    wide, narrow, hidden_in, grad_out, gain_attn, gain_ffn, w_query, w_key, w_value, w_output,
    table_rel, table_horiz, table_vert, wi_gate, wi_up, wo_ffn, counts, patch_mask,
    bucket_rel, bucket_horiz, bucket_vert,
):
    slots = bucket_rel.shape[1]
    rows, d = hidden_in.shape
    buckets, heads = table_rel.shape
    width = w_query.shape[1]
    ff = wi_gate.shape[1]
    assert rows == slots and narrow == 4 and heads * HEAD_DIM == width
    me = lax.axis_index("narrow").astype(I32)
    page = me[None]
    core = lambda x: swap(x, "narrow", 1, narrow)
    far = lambda x: swap(x, "narrow", 2, narrow)

    positions = jnp.arange(slots, dtype=I32)
    text = slots - patch_mask.shape[1]
    count = lax.dynamic_index_in_dim(counts, me, 0, False)
    patches = lax.dynamic_index_in_dim(patch_mask, me, 0, False)
    valid = jnp.concatenate([positions[:text] < count, patches == 1]).astype(F32)[:, None]
    ids = (bucket_rel, bucket_horiz, bucket_vert)

    tables = jnp.stack([table_rel, table_horiz, table_vert]).transpose(0, 2, 1)
    table_row = jnp.pad(tables.reshape(1, -1), ((0, 15), (0, 3 * width - tables.size)))
    pack_own = jnp.concatenate([jnp.concatenate([w_query, w_key, w_value], axis=1), table_row], axis=0)
    pack_far = far(pack_own)
    wo_far = far(after(w_output, pack_far))
    packs = [pack_own, core(pack_own), pack_far, core(pack_far)]
    wos = [w_output, core(w_output), wo_far, core(wo_far)]
    wi_own = jnp.concatenate([wi_gate, wi_up], axis=1)
    wi_core = core(wi_own)
    wo_core = core(wo_ffn)
    wg = jnp.concatenate([wi_own[:, :ff], wi_core[:, :ff]], axis=1)
    wu = jnp.concatenate([wi_own[:, ff:], wi_core[:, ff:]], axis=1)
    wd = jnp.concatenate([wo_ffn, wo_core], axis=0)
    grad_far = far(after(grad_out, wo_far))

    gain_first = gain_attn.astype(F32)
    gain_second = gain_ffn.astype(F32)
    resid = hidden_in.astype(F32)
    normed, inv_first = rms_forward(resid, gain_first)
    normed = normed.astype(BF)

    saved = []
    for pack in packs:
        tab = pack_tables(pack[d, : tables.size].reshape(3, heads, buckets))
        saved.append(attn_fwd(page, normed, pack, tab, ids, valid, heads))
    context = jnp.concatenate([s[2] for s in saved], axis=1)
    wo_all = jnp.concatenate(wos, axis=0)
    middle = resid + dot(context, wo_all)
    normed_ffn, inv_second = rms_forward(middle, gain_second)
    ffn_own = normed_ffn.astype(BF)
    ffn_far = far(ffn_own)

    def ffn(rows_in, g):
        gate, upper = dot(rows_in, wg), dot(rows_in, wu)
        hidden = gated(gate, upper).astype(BF)
        out = dot(hidden, wd)
        grad_hidden = dot_nt(g, wd)
        _, pull = jax.vjp(gated, gate, upper)
        dg, du = pull(grad_hidden)
        dg, du = dg.astype(BF), du.astype(BF)
        back = dot_nt(dg, wg) + dot_nt(du, wu)
        return hidden, out, dg, du, back

    hid_f, out_f, dg_f, du_f, back_f = ffn(ffn_far, grad_far)
    hid_o, out_o, dg_o, du_o, back_o = ffn(ffn_own, grad_out)
    back_in = far(back_f.astype(BF))
    out_in = far(after(out_f.astype(BF), back_in))
    block_out = (middle + (out_o + out_in.astype(F32))).astype(BF)
    grad_normed_ffn = back_o + back_in.astype(F32)

    grad_norm, grad_gain_second = rms_backward(grad_normed_ffn, middle, inv_second, gain_second)
    grad_middle = grad_out.astype(F32) + grad_norm
    grad_attn = grad_middle.astype(BF)

    both = lambda a, b: jnp.concatenate([a, b], axis=0)
    x2, g2 = both(ffn_own, ffn_far), both(grad_out, grad_far)
    dw = [dot_tn(x2, both(dg_o, dg_f)), dot_tn(x2, both(du_o, du_f)), dot_tn(g2, both(hid_o, hid_f))]
    dw = [x.astype(BF) for x in dw]
    keep = jnp.concatenate([x[:, :ff] for x in dw], axis=1)
    send = jnp.concatenate([x[:, ff:] for x in dw], axis=1)
    ffn_sum = (keep.astype(F32) + core(send).astype(F32)).astype(BF)
    ffn_sum = scatter_wide(ffn_sum.reshape(wide, d // wide, 3 * ff), wide, BF)

    grads, dss, dqkv = [None] * 4, [None] * 4, [None] * 4
    for r in (3, 2, 1, 0):
        qkv, p, ctx, linv = saved[r]
        dq, dk, dv, dss[r] = attn_bwd(grad_attn, wos[r], ctx, linv, qkv, p, heads)
        dqkv[r] = jnp.concatenate([dq, dk, dv], axis=1)
        grads[r] = jnp.concatenate([dot_tn(normed, dqkv[r]), dot_tn(grad_attn, ctx)], axis=1).astype(BF)
    far_sum = (grads[2].astype(F32) + core(grads[3]).astype(F32)).astype(BF)
    own_sum = grads[0].astype(F32) + core(grads[1]).astype(F32)
    attn_sum = (own_sum + far(far_sum).astype(F32)).astype(BF)
    attn_sum = scatter_wide(attn_sum.reshape(wide, d // wide, 4 * width), wide, BF)

    table_sum = table_grads(page, ids, dss, buckets)

    grad_normed = sum(dot_nt(dqkv[r], packs[r][:d]) for r in range(4))
    grad_norm, grad_gain_first = rms_backward(grad_normed, resid, inv_first, gain_first)
    grad_input = grad_middle + grad_norm

    per = d // (wide * narrow)
    gains = jnp.stack([grad_gain_first, grad_gain_second]).reshape(2, wide, narrow, per)
    gains = jnp.stack([lax.dynamic_index_in_dim(gains, me ^ r, 2, False) for r in range(4)], axis=2)
    gains = gains.transpose(2, 1, 0, 3).reshape(4, wide, 2 * per)
    tabs = table_sum.reshape(3, wide, buckets // wide, 4, heads).transpose(3, 1, 0, 2, 4)
    small = jnp.concatenate([gains, tabs.reshape(4, wide, -1)], axis=2)
    small = small[0::2] + core(small[1::2])
    small = small[0] + far(small[1])
    small = scatter_wide(small, wide, F32)
    small_gains = small[: 2 * per].reshape(2, per)
    small_tabs = small[2 * per :].reshape(3, buckets // wide, heads)

    return (
        block_out,
        grad_input,
        small_gains[0],
        small_gains[1],
        attn_sum[:, :width],
        attn_sum[:, width : 2 * width],
        attn_sum[:, 2 * width : 3 * width],
        attn_sum[:, 3 * width :].T,
        small_tabs[0],
        small_tabs[1],
        small_tabs[2],
        ffn_sum[:, :ff],
        ffn_sum[:, ff : 2 * ff],
        ffn_sum[:, 2 * ff :].T,
    )


def solution(mesh):
    rows, both = P(("wide", "narrow"), None), P(("wide", "narrow"))
    cols, across = P(None, "narrow"), P("narrow", None)
    grid, turned = P("wide", "narrow"), P("narrow", "wide")
    pages = P("wide", None, None)
    return jax.shard_map(
        functools.partial(shards, mesh.shape["wide"], mesh.shape["narrow"]),
        mesh=mesh,
        in_specs=(
            rows, rows, P(), P(), cols, cols, cols, across, cols, cols, cols, cols, cols, across,
            P("wide"), P("wide", None), pages, pages, pages,
        ),
        out_specs=(
            rows, rows, both, both, grid, grid, grid, turned, grid, grid, grid, grid, grid, turned,
        ),
        check_vma=False,
    )
```

```python
import functools
import math

import jax
import jax.numpy as jnp
from jax import lax
from jax.experimental import pallas as pl
from jax.experimental.pallas import tpu as pltpu
from jax.sharding import PartitionSpec as P

F32 = jnp.float32
BF = jnp.bfloat16
I32 = jnp.int32
HEAD_DIM = 64
LANES = 128
EPS = 1e-06
NT = (((1,), (1,)), ((), ()))
TN = (((0,), (0,)), ((), ()))

FIXED = 2048.0
OFFSET = 8192
MASKED = -3.0e12
VMEM_LIMIT = 56 << 20
MESH = pl.DeviceIdType.MESH


def lookup(table_row, ids):
    return jnp.take_along_axis(table_row, ids, axis=1, mode="promise_in_bounds")


def neighbours():
    w, n = lax.axis_index("wide"), lax.axis_index("narrow")
    return w, n, (w, n ^ 1), (w, n ^ 2), (w, n ^ 3), (w ^ 1, n)


def greet(devices):
    barrier = pltpu.get_barrier_semaphore()
    for device in devices:
        pl.semaphore_signal(barrier, inc=1, device_id=device, device_id_type=MESH)
    pl.semaphore_wait(barrier, len(devices))


def remote(src, dst, sems, device):
    return pltpu.make_async_remote_copy(
        src_ref=src, dst_ref=dst, send_sem=sems.at[0], recv_sem=sems.at[1], device_id=device, device_id_type=MESH
    )


def forward_kernel(
    heads, chunk,
    x_ref, gain1_ref, gain2_ref, valid_ref, tab_ref, wq_ref, wk_ref, wv_ref, wo_ref, ir_ref, ih_ref, iv_ref,
    go_ref, wg_ref, wu_ref, wd_ref,
    qkv_ref, e_ref, ctx_ref, linv_ref, wall_ref, woall_ref, middle_ref, ffn_ref, gofar_ref, wgc_ref, wuc_ref, wdc_ref,
    normed_ref, mask_ref, ids_ref, tabs_ref, words_ref, ebuf_ref,
    own_sem, id_sem, e_sem, core_sem, far_sem, wide_sem, fwd_sem, tab_sem, big_sem,
):
    pw = 2 * HEAD_DIM
    slots, d = x_ref.shape
    w, n, core, far, diag, side = neighbours()
    half = w & 1
    other = 1 - half

    def source(m, pair):
        cols = pl.ds(pl.multiple_of(pair * pw, pw), pw)
        return wo_ref.at[cols, :] if m == 3 else (wq_ref, wk_ref, wv_ref)[m].at[:, cols]

    def place(m, slot):
        cols = pl.ds(pl.multiple_of(slot * pw, pw), pw)
        return woall_ref.at[cols, :] if m == 3 else wall_ref.at[m, :, cols]

    ids_in = [pltpu.make_async_copy(r.at[n], ids_ref.at[t], id_sem.at[t]) for t, r in enumerate((ir_ref, ih_ref, iv_ref))]
    own_in = [[pltpu.make_async_copy(source(m, p), place(m, p), own_sem.at[p, m]) for m in range(4)] for p in range(2)]
    for copy in own_in[0][:3] + ids_in + own_in[0][3:] + own_in[1]:
        copy.start()

    greet((core, far, diag, side))
    far_out = [remote(source(m, half), place(m, 4 + half), far_sem.at[m], far) for m in range(4)]
    core_out = [[remote(source(m, p), place(m, 2 + p), core_sem.at[p, m], core) for m in range(4)] for p in range(2)]
    tabs_out = [remote(tab_ref, tabs_ref.at[r], tab_sem.at[r - 1], dev) for r, dev in ((1, core), (2, far), (3, diag))]
    for copy in tabs_out + far_out[:1] + core_out[0] + core_out[1] + far_out[1:]:
        copy.start()
    wide_out = [remote(place(m, 4 + half), place(m, 4 + half), wide_sem.at[m], side) for m in range(4)]
    fwd_out = [
        [remote(place(m, 4 + p), place(m, 6 + p), fwd_sem.at[i, m], core) for m in range(4)]
        for i, p in enumerate((half, other))
    ]
    go_out = remote(go_ref, gofar_ref, big_sem.at[0], far)
    ffn_out = [
        remote(wg_ref, wgc_ref, big_sem.at[1], core),
        remote(wu_ref, wuc_ref, big_sem.at[2], core),
        remote(wd_ref, wdc_ref, big_sem.at[3], core),
    ]

    x = x_ref[...].astype(F32)
    inv = lax.rsqrt(jnp.mean(x * x, axis=-1, keepdims=True) + EPS)
    normed_ref[...] = (x * inv * gain1_ref[...]).astype(BF)
    lane_all = lax.broadcasted_iota(I32, (slots, pw), 1)
    shown = jnp.broadcast_to(valid_ref[...], (slots, pw)) > 0.5
    mask_ref[...] = jnp.where(lane_all == 0, jnp.where(shown, 0.0, MASKED), 0.0).astype(BF)
    ones = jnp.ones((slots, pw), BF)
    lane = lax.broadcasted_iota(I32, (chunk, pw), 1)
    low = lane < HEAD_DIM
    first = jnp.where(lane == 0, 1.0, 0.0).astype(BF)
    to_log2 = math.log2(math.e) / FIXED

    tabs_ref[0] = tab_ref[...]
    for copy in ids_in:
        copy.wait()
    for copy in tabs_out:
        copy.wait()
    for r in range(4):
        fixed = tabs_ref[r].astype(I32)
        for p in range(2):
            for t in range(3):
                row = t * heads + 2 * p
                words_ref[2 * r + p, t : t + 1, :] = fixed[row + 1 : row + 2] * 65536 + fixed[row : row + 1] + OFFSET

    def e_out(parity, slot):
        return pltpu.make_async_copy(ebuf_ref.at[parity], e_ref.at[slot], e_sem.at[parity])

    def slot_of(t):
        late = 4 + 2 * (t & 1) + jnp.where(t >= 6, other, half)
        return jnp.where(t < 4, t, late)

    def step(t, carry):
        slot = slot_of(t)
        for p in range(2):

            @pl.when(t == p)
            def _():
                for m in range(3):
                    own_in[p][m].wait()

            @pl.when(t == 2 + p)
            def _():
                for m in range(3):
                    core_out[p][m].wait_recv()

        for m in range(4):

            @pl.when(t == 2 + m)
            def _():
                far_out[m].wait_recv()
                wide_out[m].start()
                fwd_out[0][m].start()

        @pl.when(t == 3)
        def _():
            for copy in ffn_out:
                copy.start()

        @pl.when(t == 4)
        def _():
            go_out.start()

        @pl.when(t == 5)
        def _():
            for m in range(3):
                fwd_out[0][m].wait_recv()

        @pl.when(t == 6)
        def _():
            for m in range(3):
                wide_out[m].wait_recv()
                fwd_out[1][m].start()

        @pl.when(t == 7)
        def _():
            for m in range(3):
                fwd_out[1][m].wait_recv()
            wide_out[3].wait_recv()
            fwd_out[1][3].start()

        parity = t & 1

        @pl.when(t >= 2)
        def _():
            e_out(parity, slot).wait()

        cols = pl.ds(pl.multiple_of(slot * pw, pw), pw)
        weights = jnp.concatenate([wall_ref[m, :, cols] for m in range(3)], axis=1)
        joined = jnp.dot(normed_ref[...], weights, preferred_element_type=F32).astype(BF)
        for m in range(3):
            qkv_ref[m, :, cols] = joined[:, m * pw : (m + 1) * pw]
        kx = jnp.concatenate([joined[:, pw : 2 * pw], mask_ref[...]], axis=1)
        vx = jnp.concatenate([joined[:, 2 * pw :], ones], axis=1)
        words = words_ref[slot]
        for c in range(slots // chunk):
            rows = slice(c * chunk, (c + 1) * chunk)
            q2 = joined[rows, :pw] * jnp.bfloat16(FIXED)
            zero = jnp.zeros_like(q2)
            scores = []
            for sub in range(2):
                q = jnp.where(low, q2, zero) if sub == 0 else jnp.where(low, zero, q2)
                q = jnp.concatenate([q, first], axis=1)
                scores.append(lax.dot_general(q, kx, NT, preferred_element_type=F32))
            tabs = [jnp.broadcast_to(words[k : k + 1, :], (chunk, LANES)) for k in range(3)]
            parts = ([], [])
            for j in range(slots // LANES):
                sl = slice(j * LANES, (j + 1) * LANES)
                bias = (
                    lookup(tabs[0], ids_ref[0, rows, sl])
                    + lookup(tabs[1], ids_ref[1, rows, sl])
                    + lookup(tabs[2], ids_ref[2, rows, sl])
                )
                parts[0].append(scores[0][:, sl] + (bias & 0xFFFF).astype(F32))
                parts[1].append(scores[1][:, sl] + (bias >> 16).astype(F32))
            outs = []
            for sub in range(2):
                s = jnp.concatenate(parts[sub], axis=1)
                peak = jnp.max(s, axis=1, keepdims=True)
                e = jnp.exp2((s - peak) * to_log2).astype(BF)
                ebuf_ref[parity, sub, rows, :] = e
                outs.append(jnp.dot(e, vx, preferred_element_type=F32))
            linv = 1.0 / jnp.where(low, outs[0][:, pw:], outs[1][:, pw:])
            linv_ref[rows, cols] = linv
            ctx_ref[rows, cols] = (jnp.where(low, outs[0][:, :pw], outs[1][:, :pw]) * linv).astype(BF)
        e_out(parity, slot).start()
        return carry

    lax.fori_loop(0, 8, step, 0)
    for p in range(2):
        own_in[p][3].wait()
        core_out[p][3].wait_recv()
    for i in range(2):
        fwd_out[i][3].wait_recv()
    middle = x_ref[...].astype(F32) + jnp.dot(ctx_ref[...], woall_ref[...], preferred_element_type=F32)
    middle_ref[...] = middle
    inv = lax.rsqrt(jnp.mean(middle * middle, axis=-1, keepdims=True) + EPS)
    ffn_ref[...] = (middle * inv * gain2_ref[...]).astype(BF)
    for p in range(2):
        e_out(p, p).wait()
        for m in range(4):
            core_out[p][m].wait_send()
            fwd_out[p][m].wait_send()
    for m in range(4):
        far_out[m].wait_send()
        wide_out[m].wait_send()
    for copy in ffn_out:
        copy.wait()
    go_out.wait()


def forward(x, gain1, gain2, valid, tab, wq, wk, wv, wo, ids, grad_out, wg, wu, wd, chunk=256):
    slots, d = x.shape
    heads = wq.shape[1] // HEAD_DIM
    ff = wg.shape[1]
    assert heads == 4
    vmem, anywhere = pl.BlockSpec(memory_space=pltpu.VMEM), pl.BlockSpec(memory_space=pl.ANY)
    shape = jax.ShapeDtypeStruct
    dma = pltpu.SemaphoreType.DMA
    return pl.pallas_call(
        functools.partial(forward_kernel, heads, chunk),
        in_specs=[vmem] * 5 + [anywhere] * 11,
        out_specs=[vmem, anywhere] + [vmem] * 6 + [anywhere] * 4,
        out_shape=[
            shape((3, slots, d), BF),
            shape((8, 2, slots, slots), BF),
            shape((slots, d), BF),
            shape((slots, d), F32),
            shape((3, d, d), BF),
            shape((d, d), BF),
            shape((slots, d), F32),
            shape((slots, d), BF),
            shape((slots, d), BF),
            shape((d, ff), BF),
            shape((d, ff), BF),
            shape((ff, d), BF),
        ],
        scratch_shapes=[
            pltpu.VMEM((slots, d), BF),
            pltpu.VMEM((slots, 2 * HEAD_DIM), BF),
            pltpu.VMEM((3, slots, slots), I32),
            pltpu.VMEM((4, 16, LANES), F32),
            pltpu.VMEM((8, 8, LANES), I32),
            pltpu.VMEM((2, 2, slots, slots), BF),
            dma((2, 4)), dma((3,)), dma((2,)), dma((2, 4, 2)), dma((4, 2)), dma((4, 2)), dma((2, 4, 2)),
            dma((3, 2)), dma((4, 2)),
        ],
        compiler_params=pltpu.CompilerParams(
            vmem_limit_bytes=VMEM_LIMIT, collective_id=1, has_side_effects=True
        ),
        cost_estimate=pl.CostEstimate(flops=20 * slots * d * d, bytes_accessed=40 << 20, transcendentals=16 * slots * slots),
        name="forward",
    )(x, gain1, gain2, valid, tab, wq, wk, wv, wo, *ids, grad_out, wg, wu, wd)


def attn_bwd_body(
    heads, ga_ref, wo_ref, ctx_ref, linv_ref, q_ref, k_ref, v_ref, p_ref,
    dq_ref, dk_ref, dv_ref, ds_ref, do_ref,
):
    hd, pw = HEAD_DIM, 2 * HEAD_DIM
    slots = ga_ref.shape[0]
    pair = pl.program_id(0)

    @pl.when(pair == 0)
    def _():
        d = lax.dot_general(ga_ref[...], wo_ref[...], NT, preferred_element_type=F32)
        for p in range(heads // 2):
            do_ref[p] = (d[:, p * pw : (p + 1) * pw] * linv_ref[:, p * pw : (p + 1) * pw]).astype(BF)

    lane = lax.broadcasted_iota(I32, (slots, pw), 1)
    low = lane < hd
    do2 = do_ref[pair]
    prod = do2.astype(F32) * ctx_ref[...].astype(F32)
    q2, k2, v2 = q_ref[...], k_ref[...], v_ref[...]
    vx = jnp.concatenate([v2, jnp.where(lane < 2, 1.0, 0.0).astype(BF)], axis=1)
    do_t, q_t = do2.T, q2.T
    zero = jnp.zeros_like(do2)
    dq, dk, dv = [], [], []
    for sub in range(2):
        mine = low if sub == 0 else jnp.logical_not(low)
        row = -jnp.sum(jnp.where(mine, prod, 0.0), axis=1, keepdims=True)
        head_part = row.astype(BF).astype(F32)
        extra = jnp.where(lane == 0, head_part, jnp.where(lane == 1, row - head_part, 0.0)).astype(BF)
        dox = jnp.concatenate([jnp.where(mine, do2, zero), extra], axis=1)
        t = lax.dot_general(dox, vx, NT, preferred_element_type=F32)
        e = p_ref[sub]
        ds = (e.astype(F32) * t).astype(BF)
        ds_ref[sub] = ds
        dv.append(jnp.dot(do_t[sub * hd : (sub + 1) * hd], e, preferred_element_type=F32))
        dk.append(jnp.dot(q_t[sub * hd : (sub + 1) * hd], ds, preferred_element_type=F32))
        dq.append(jnp.dot(ds, k2, preferred_element_type=F32))
    dq_ref[...] = jnp.where(low, dq[0], dq[1]).astype(BF)
    dk_ref[...] = jnp.concatenate(dk, axis=0).T.astype(BF)
    dv_ref[...] = jnp.concatenate(dv, axis=0).T.astype(BF)


def attn_bwd(ga, wo, ctx, linv, qkv, p, heads):
    slots, d = ga.shape
    hw, pw, pairs = heads * HEAD_DIM, 2 * HEAD_DIM, heads // 2
    full = lambda *sh: pl.BlockSpec(sh, lambda i: (0,) * len(sh))
    col = lambda off: pl.BlockSpec((slots, pw), lambda i: (0, off + i))
    block = pl.BlockSpec((2, slots, slots), lambda i: (i, 0, 0))
    return pl.pallas_call(
        functools.partial(attn_bwd_body, heads),
        grid=(pairs,),
        in_specs=[full(slots, d), full(hw, d), col(0), full(slots, hw), col(0), col(pairs), col(2 * pairs), block],
        out_specs=[col(0), col(0), col(0), block],
        scratch_shapes=[pltpu.VMEM((pairs, slots, pw), BF)],
        out_shape=[jax.ShapeDtypeStruct((slots, hw), BF)] * 3 + [jax.ShapeDtypeStruct((heads, slots, slots), BF)],
        compiler_params=pltpu.CompilerParams(vmem_limit_bytes=VMEM_LIMIT),
        cost_estimate=pl.CostEstimate(flops=6 * slots * d * hw, bytes_accessed=8 << 20, transcendentals=0),
        name="attn_bwd",
    )(ga, wo, ctx, linv, qkv, qkv, qkv, p)


def table_body(heads, buckets, blk, page_ref, ir_ref, ih_ref, iv_ref, *rest):
    ds_refs, (out_ref, acc_ref) = rest[:-2], rest[-2:]

    @pl.when(pl.program_id(0) == 0)
    def _():
        acc_ref[...] = jnp.zeros_like(acc_ref)

    rows, slots = ir_ref.shape[1], ir_ref.shape[2]
    one, zero = jnp.ones((blk, slots), BF), jnp.zeros((blk, slots), BF)

    def step(c, carry):
        r0 = pl.multiple_of(c * blk, blk)
        g = jnp.concatenate([r[h, pl.ds(r0, blk), :] for r in ds_refs for h in range(r.shape[0])], axis=0)
        for t, ref in enumerate((ir_ref, ih_ref, iv_ref)):
            ids = ref[0, pl.ds(r0, blk), :].astype(F32).astype(BF)
            hot = jnp.concatenate([jnp.where(ids == jnp.bfloat16(b), one, zero) for b in range(buckets)], axis=0)
            span = slice(t * buckets * blk, (t + 1) * buckets * blk)
            acc_ref[span, :] += lax.dot_general(hot, g, NT, preferred_element_type=F32)
        return carry

    lax.fori_loop(0, rows // blk, step, 0)

    @pl.when(pl.program_id(0) == pl.num_programs(0) - 1)
    def _():
        n = heads * blk
        same = lax.broadcasted_iota(I32, (blk, n), 0) == (lax.broadcasted_iota(I32, (blk, n), 1) & (blk - 1))
        for b in range(3 * buckets):
            rows_b = jnp.where(same, acc_ref[b * blk : (b + 1) * blk, :], 0.0)
            out_ref[b : b + 1, :] = jnp.sum(rows_b, axis=0, keepdims=True)


def table_grads(page, ids, dss, buckets, rows=64, blk=16):
    heads = sum(d.shape[0] for d in dss)
    slots = ids[0].shape[1]
    id_spec = pl.BlockSpec((1, rows, slots), lambda i, n: (n[0], i, 0))
    grid_spec = pltpu.PrefetchScalarGridSpec(
        num_scalar_prefetch=1,
        grid=(slots // rows,),
        in_specs=[id_spec] * 3 + [pl.BlockSpec((d.shape[0], rows, slots), lambda i, n: (0, i, 0)) for d in dss],
        out_specs=pl.BlockSpec((3 * buckets, heads * blk), lambda i, n: (0, 0)),
        scratch_shapes=[pltpu.VMEM((3 * buckets * blk, heads * blk), F32)],
    )
    out = pl.pallas_call(
        functools.partial(table_body, heads, buckets, blk),
        grid_spec=grid_spec,
        out_shape=jax.ShapeDtypeStruct((3 * buckets, heads * blk), F32),
        compiler_params=pltpu.CompilerParams(vmem_limit_bytes=VMEM_LIMIT),
        cost_estimate=pl.CostEstimate(
            flops=6 * buckets * blk * heads * slots * slots, bytes_accessed=12 << 20, transcendentals=0
        ),
        name="table_grads",
    )(page, *ids, *dss)
    return out.reshape(3 * buckets, heads, blk).sum(-1)


def fixed_tables(tables):
    rows = jnp.concatenate([t.T for t in tables], axis=0).astype(F32)
    rows = jnp.round(rows * FIXED)
    return jnp.pad(rows, ((0, 16 - rows.shape[0]), (0, LANES - rows.shape[1])))


def swap(x, axis, bit, size):
    return lax.ppermute(x, axis, [(i, i ^ bit) for i in range(size)])


def after(x, *others):
    return lax.optimization_barrier((x,) + others)[0]


def scatter_wide(x, size, kind):
    left = size
    while left > 1:
        bit = size // left
        side = (lax.axis_index("wide") // bit) % 2
        view = x.reshape((left // 2, 2) + x.shape[1:])
        keep = lax.dynamic_index_in_dim(view, side, 1, False)
        send = lax.dynamic_index_in_dim(view, 1 - side, 1, False).astype(kind)
        x = keep.astype(F32) + swap(send, "wide", bit, size).astype(F32)
        left //= 2
        if left > 1:
            x = x.astype(kind)
    return x[0]


def rms_forward(row_data, gain_vec):
    inv_rms = lax.rsqrt(jnp.mean(row_data * row_data, axis=-1, keepdims=True) + EPS)
    return (row_data * inv_rms * gain_vec, inv_rms)


def rms_backward(upstream, row_data, inv_rms, gain_vec):
    lifted = upstream * gain_vec
    inner = jnp.mean(lifted * row_data, axis=-1, keepdims=True)
    grad_rows = inv_rms * lifted - row_data * inv_rms * inv_rms * inv_rms * inner
    grad_gain = jnp.sum(upstream * row_data * inv_rms, axis=0)
    return (grad_rows, grad_gain)


def gated(gate, upper):
    return jax.nn.gelu(gate, approximate=True) * upper


def dot(a, b):
    return jnp.dot(a, b, preferred_element_type=F32)


def dot_nt(a, b):
    return lax.dot_general(a, b, NT, preferred_element_type=F32)


def dot_tn(a, b):
    return lax.dot_general(a, b, TN, preferred_element_type=F32)


def shards(
    wide, narrow, hidden_in, grad_out, gain_attn, gain_ffn, w_query, w_key, w_value, w_output,
    table_rel, table_horiz, table_vert, wi_gate, wi_up, wo_ffn, counts, patch_mask,
    bucket_rel, bucket_horiz, bucket_vert,
):
    slots = bucket_rel.shape[1]
    rows, d = hidden_in.shape
    buckets, heads = table_rel.shape
    width = w_query.shape[1]
    ff = wi_gate.shape[1]
    assert rows == slots and narrow == 4 and heads * HEAD_DIM == width
    me = lax.axis_index("narrow").astype(I32)
    page = me[None]
    core = lambda x: swap(x, "narrow", 1, narrow)
    far = lambda x: swap(x, "narrow", 2, narrow)

    positions = jnp.arange(slots, dtype=I32)
    text = slots - patch_mask.shape[1]
    count = lax.dynamic_index_in_dim(counts, me, 0, False)
    patches = lax.dynamic_index_in_dim(patch_mask, me, 0, False)
    valid = jnp.concatenate([positions[:text] < count, patches == 1]).astype(F32)[:, None]
    ids = (bucket_rel, bucket_horiz, bucket_vert)

    gain_first = gain_attn.astype(F32)
    gain_second = gain_ffn.astype(F32)
    qkv, exps, context, linv, w_all, wo_all, middle, ffn_own, grad_far, wg_core, wu_core, wd_core = forward(
        hidden_in, gain_first[None], gain_second[None], valid, fixed_tables((table_rel, table_horiz, table_vert)),
        w_query, w_key, w_value, w_output, ids, grad_out, wi_gate, wi_up, wo_ffn,
    )
    wg = jnp.concatenate([wi_gate, wg_core], axis=1)
    wu = jnp.concatenate([wi_up, wu_core], axis=1)
    wd = jnp.concatenate([wo_ffn, wd_core], axis=0)
    resid = hidden_in.astype(F32)
    normed, inv_first = rms_forward(resid, gain_first)
    normed = normed.astype(BF)
    _, inv_second = rms_forward(middle, gain_second)
    ffn_far = far(ffn_own)

    def ffn(rows_in, g):
        gate, upper = dot(rows_in, wg), dot(rows_in, wu)
        hidden = gated(gate, upper).astype(BF)
        out = dot(hidden, wd)
        grad_hidden = dot_nt(g, wd)
        _, pull = jax.vjp(gated, gate, upper)
        dg, du = pull(grad_hidden)
        dg, du = dg.astype(BF), du.astype(BF)
        back = dot_nt(dg, wg) + dot_nt(du, wu)
        return hidden, out, dg, du, back

    hid_f, out_f, dg_f, du_f, back_f = ffn(ffn_far, grad_far)
    hid_o, out_o, dg_o, du_o, back_o = ffn(ffn_own, grad_out)
    back_in = far(back_f.astype(BF))
    out_in = far(after(out_f.astype(BF), back_in))
    block_out = (middle + (out_o + out_in.astype(F32))).astype(BF)
    grad_normed_ffn = back_o + back_in.astype(F32)

    grad_norm, grad_gain_second = rms_backward(grad_normed_ffn, middle, inv_second, gain_second)
    grad_middle = grad_out.astype(F32) + grad_norm
    grad_attn = grad_middle.astype(BF)

    both = lambda a, b: jnp.concatenate([a, b], axis=0)
    x2, g2 = both(ffn_own, ffn_far), both(grad_out, grad_far)
    dw = [dot_tn(x2, both(dg_o, dg_f)), dot_tn(x2, both(du_o, du_f)), dot_tn(g2, both(hid_o, hid_f))]
    dw = [x.astype(BF) for x in dw]
    keep = jnp.concatenate([x[:, :ff] for x in dw], axis=1)
    send = jnp.concatenate([x[:, ff:] for x in dw], axis=1)
    ffn_sum = (keep.astype(F32) + core(send).astype(F32)).astype(BF)
    ffn_sum = scatter_wide(ffn_sum.reshape(wide, d // wide, 3 * ff), wide, BF)

    grads, dss, dqkv = [None] * 4, [None] * 4, [None] * 4
    for r in (3, 2, 1, 0):
        cols = slice(r * width, (r + 1) * width)
        ctx = context[:, cols]
        joined = jnp.concatenate([qkv[m, :, cols] for m in range(3)], axis=1)
        p = exps[2 * r : 2 * r + 2].reshape(heads, slots, slots)
        dq, dk, dv, dss[r] = attn_bwd(grad_attn, wo_all[cols], ctx, linv[:, cols], joined, p, heads)
        dqkv[r] = jnp.concatenate([dq, dk, dv], axis=1)
        grads[r] = jnp.concatenate([dot_tn(normed, dqkv[r]), dot_tn(grad_attn, ctx)], axis=1).astype(BF)
    far_sum = (grads[2].astype(F32) + core(grads[3]).astype(F32)).astype(BF)
    own_sum = grads[0].astype(F32) + core(grads[1]).astype(F32)
    attn_sum = (own_sum + far(far_sum).astype(F32)).astype(BF)
    attn_sum = scatter_wide(attn_sum.reshape(wide, d // wide, 4 * width), wide, BF)

    table_sum = table_grads(page, ids, dss, buckets)

    full_dqkv = [jnp.concatenate([dqkv[r][:, m * width : (m + 1) * width] for r in range(4)], axis=1) for m in range(3)]
    grad_normed = sum(dot_nt(full_dqkv[m], w_all[m]) for m in range(3))
    grad_norm, grad_gain_first = rms_backward(grad_normed, resid, inv_first, gain_first)
    grad_input = grad_middle + grad_norm

    per = d // (wide * narrow)
    gains = jnp.stack([grad_gain_first, grad_gain_second]).reshape(2, wide, narrow, per)
    gains = jnp.stack([lax.dynamic_index_in_dim(gains, me ^ r, 2, False) for r in range(4)], axis=2)
    gains = gains.transpose(2, 1, 0, 3).reshape(4, wide, 2 * per)
    tabs = table_sum.reshape(3, wide, buckets // wide, 4, heads).transpose(3, 1, 0, 2, 4)
    small = jnp.concatenate([gains, tabs.reshape(4, wide, -1)], axis=2)
    small = small[0::2] + core(small[1::2])
    small = small[0] + far(small[1])
    small = scatter_wide(small, wide, F32)
    small_gains = small[: 2 * per].reshape(2, per)
    small_tabs = small[2 * per :].reshape(3, buckets // wide, heads)

    return (
        block_out,
        grad_input,
        small_gains[0],
        small_gains[1],
        attn_sum[:, :width],
        attn_sum[:, width : 2 * width],
        attn_sum[:, 2 * width : 3 * width],
        attn_sum[:, 3 * width :].T,
        small_tabs[0],
        small_tabs[1],
        small_tabs[2],
        ffn_sum[:, :ff],
        ffn_sum[:, ff : 2 * ff],
        ffn_sum[:, 2 * ff :].T,
    )


def solution(mesh):
    rows, both = P(("wide", "narrow"), None), P(("wide", "narrow"))
    cols, across = P(None, "narrow"), P("narrow", None)
    grid, turned = P("wide", "narrow"), P("narrow", "wide")
    pages = P("wide", None, None)
    return jax.shard_map(
        functools.partial(shards, mesh.shape["wide"], mesh.shape["narrow"]),
        mesh=mesh,
        in_specs=(
            rows, rows, P(), P(), cols, cols, cols, across, cols, cols, cols, cols, cols, across,
            P("wide"), P("wide", None), pages, pages, pages,
        ),
        out_specs=(
            rows, rows, both, both, grid, grid, grid, turned, grid, grid, grid, grid, grid, turned,
        ),
        check_vma=False,
    )
```

```python
import functools
import math

import jax
import jax.numpy as jnp
from jax import lax
from jax.experimental import pallas as pl
from jax.experimental.pallas import tpu as pltpu
from jax.sharding import PartitionSpec as P

F32 = jnp.float32
BF = jnp.bfloat16
I32 = jnp.int32
HEAD_DIM = 64
LANES = 128
EPS = 1e-06
NT = (((1,), (1,)), ((), ()))
TN = (((0,), (0,)), ((), ()))

FIXED = 2048.0
OFFSET = 8192
MASKED = -3.0e12
VMEM_LIMIT = 60 << 20
MESH = pl.DeviceIdType.MESH


def lookup(table_row, ids):
    return jnp.take_along_axis(table_row, ids, axis=1, mode="promise_in_bounds")


def neighbours():
    w, n = lax.axis_index("wide"), lax.axis_index("narrow")
    return w, n, (w, n ^ 1), (w, n ^ 2), (w, n ^ 3), (w ^ 1, n)


def greet(devices):
    barrier = pltpu.get_barrier_semaphore()
    for device in devices:
        pl.semaphore_signal(barrier, inc=1, device_id=device, device_id_type=MESH)
    pl.semaphore_wait(barrier, len(devices))


def remote(src, dst, sems, device):
    return pltpu.make_async_remote_copy(
        src_ref=src, dst_ref=dst, send_sem=sems.at[0], recv_sem=sems.at[1], device_id=device, device_id_type=MESH
    )


def forward_kernel(
    heads, chunk,
    x_ref, gain1_ref, gain2_ref, valid_ref, tab_ref, wq_ref, wk_ref, wv_ref, wo_ref, ir_ref, ih_ref, iv_ref,
    go_ref, wg_ref, wu_ref, wd_ref,
    qkv_ref, e_ref, ctx_ref, linv_ref, wall_ref, woall_ref, middle_ref, ffn_ref, gofar_ref, wgc_ref, wuc_ref, wdc_ref,
    normed_ref, mask_ref, ids_ref, tabs_ref, words_ref, ebuf_ref,
    own_sem, id_sem, e_sem, core_sem, far_sem, wide_sem, fwd_sem, tab_sem, big_sem,
):
    pw = 2 * HEAD_DIM
    slots, d = x_ref.shape
    w, n, core, far, diag, side = neighbours()
    half = w & 1
    other = 1 - half

    def source(m, pair):
        cols = pl.ds(pl.multiple_of(pair * pw, pw), pw)
        return wo_ref.at[cols, :] if m == 3 else (wq_ref, wk_ref, wv_ref)[m].at[:, cols]

    def place(m, slot):
        cols = pl.ds(pl.multiple_of(slot * pw, pw), pw)
        return woall_ref.at[cols, :] if m == 3 else wall_ref.at[m, :, cols]

    ids_in = [pltpu.make_async_copy(r.at[n], ids_ref.at[t], id_sem.at[t]) for t, r in enumerate((ir_ref, ih_ref, iv_ref))]
    own_in = [[pltpu.make_async_copy(source(m, p), place(m, p), own_sem.at[p, m]) for m in range(4)] for p in range(2)]
    for copy in own_in[0][:3] + ids_in + own_in[0][3:] + own_in[1]:
        copy.start()

    greet((core, far, diag, side))
    far_out = [remote(source(m, half), place(m, 4 + half), far_sem.at[m], far) for m in range(4)]
    core_out = [[remote(source(m, p), place(m, 2 + p), core_sem.at[p, m], core) for m in range(4)] for p in range(2)]
    tabs_out = [remote(tab_ref, tabs_ref.at[r], tab_sem.at[r - 1], dev) for r, dev in ((1, core), (2, far), (3, diag))]
    for copy in tabs_out + far_out[:1] + core_out[0] + core_out[1] + far_out[1:]:
        copy.start()
    wide_out = [remote(place(m, 4 + half), place(m, 4 + half), wide_sem.at[m], side) for m in range(4)]
    fwd_out = [
        [remote(place(m, 4 + p), place(m, 6 + p), fwd_sem.at[i, m], core) for m in range(4)]
        for i, p in enumerate((half, other))
    ]
    go_out = remote(go_ref, gofar_ref, big_sem.at[0], far)
    ffn_out = [
        remote(wg_ref, wgc_ref, big_sem.at[1], core),
        remote(wu_ref, wuc_ref, big_sem.at[2], core),
        remote(wd_ref, wdc_ref, big_sem.at[3], core),
    ]

    x = x_ref[...].astype(F32)
    inv = lax.rsqrt(jnp.mean(x * x, axis=-1, keepdims=True) + EPS)
    normed_ref[...] = (x * inv * gain1_ref[...]).astype(BF)
    lane_all = lax.broadcasted_iota(I32, (slots, pw), 1)
    shown = jnp.broadcast_to(valid_ref[...], (slots, pw)) > 0.5
    mask_ref[...] = jnp.where(lane_all == 0, jnp.where(shown, 0.0, MASKED), 0.0).astype(BF)
    ones = jnp.ones((slots, pw), BF)
    lane = lax.broadcasted_iota(I32, (chunk, pw), 1)
    low = lane < HEAD_DIM
    first = jnp.where(lane == 0, 1.0, 0.0).astype(BF)
    to_log2 = math.log2(math.e) / FIXED

    tabs_ref[0] = tab_ref[...]
    for copy in ids_in:
        copy.wait()
    for copy in tabs_out:
        copy.wait()
    for r in range(4):
        fixed = tabs_ref[r].astype(I32)
        for p in range(2):
            for t in range(3):
                row = t * heads + 2 * p
                words_ref[2 * r + p, t : t + 1, :] = fixed[row + 1 : row + 2] * 65536 + fixed[row : row + 1] + OFFSET

    def e_out(parity, slot):
        return pltpu.make_async_copy(ebuf_ref.at[parity], e_ref.at[slot], e_sem.at[parity])

    def slot_of(t):
        late = 4 + 2 * (t & 1) + jnp.where(t >= 6, other, half)
        return jnp.where(t < 4, t, late)

    def step(t, carry):
        slot = slot_of(t)
        for p in range(2):

            @pl.when(t == p)
            def _():
                for m in range(3):
                    own_in[p][m].wait()

            @pl.when(t == 2 + p)
            def _():
                for m in range(3):
                    core_out[p][m].wait_recv()

        for m in range(4):

            @pl.when(t == 2 + m)
            def _():
                far_out[m].wait_recv()
                wide_out[m].start()
                fwd_out[0][m].start()

        @pl.when(t == 3)
        def _():
            for copy in ffn_out:
                copy.start()

        @pl.when(t == 4)
        def _():
            go_out.start()

        @pl.when(t == 5)
        def _():
            for m in range(3):
                fwd_out[0][m].wait_recv()

        @pl.when(t == 6)
        def _():
            for m in range(3):
                wide_out[m].wait_recv()
                fwd_out[1][m].start()

        @pl.when(t == 7)
        def _():
            for m in range(3):
                fwd_out[1][m].wait_recv()
            wide_out[3].wait_recv()
            fwd_out[1][3].start()

        parity = t & 1

        @pl.when(t >= 2)
        def _():
            e_out(parity, slot).wait()

        cols = pl.ds(pl.multiple_of(slot * pw, pw), pw)
        weights = jnp.concatenate([wall_ref[m, :, cols] for m in range(3)], axis=1)
        joined = jnp.dot(normed_ref[...], weights, preferred_element_type=F32).astype(BF)
        for m in range(3):
            qkv_ref[m, :, cols] = joined[:, m * pw : (m + 1) * pw]
        kx = jnp.concatenate([joined[:, pw : 2 * pw], mask_ref[...]], axis=1)
        vx = jnp.concatenate([joined[:, 2 * pw :], ones], axis=1)
        words = words_ref[slot]
        for c in range(slots // chunk):
            rows = slice(c * chunk, (c + 1) * chunk)
            q2 = joined[rows, :pw] * jnp.bfloat16(FIXED)
            zero = jnp.zeros_like(q2)
            scores = []
            for sub in range(2):
                q = jnp.where(low, q2, zero) if sub == 0 else jnp.where(low, zero, q2)
                q = jnp.concatenate([q, first], axis=1)
                scores.append(lax.dot_general(q, kx, NT, preferred_element_type=F32))
            tabs = [jnp.broadcast_to(words[k : k + 1, :], (chunk, LANES)) for k in range(3)]
            parts = ([], [])
            for j in range(slots // LANES):
                sl = slice(j * LANES, (j + 1) * LANES)
                bias = (
                    lookup(tabs[0], ids_ref[0, rows, sl])
                    + lookup(tabs[1], ids_ref[1, rows, sl])
                    + lookup(tabs[2], ids_ref[2, rows, sl])
                )
                parts[0].append(scores[0][:, sl] + (bias & 0xFFFF).astype(F32))
                parts[1].append(scores[1][:, sl] + (bias >> 16).astype(F32))
            outs = []
            for sub in range(2):
                s = jnp.concatenate(parts[sub], axis=1)
                peak = jnp.max(s, axis=1, keepdims=True)
                e = jnp.exp2((s - peak) * to_log2).astype(BF)
                ebuf_ref[parity, sub, rows, :] = e
                outs.append(jnp.dot(e, vx, preferred_element_type=F32))
            linv = 1.0 / jnp.where(low, outs[0][:, pw:], outs[1][:, pw:])
            linv_ref[rows, cols] = linv
            ctx_ref[rows, cols] = (jnp.where(low, outs[0][:, :pw], outs[1][:, :pw]) * linv).astype(BF)
        e_out(parity, slot).start()
        return carry

    lax.fori_loop(0, 8, step, 0)
    for p in range(2):
        own_in[p][3].wait()
        core_out[p][3].wait_recv()
    for i in range(2):
        fwd_out[i][3].wait_recv()
    middle = x_ref[...].astype(F32) + jnp.dot(ctx_ref[...], woall_ref[...], preferred_element_type=F32)
    middle_ref[...] = middle
    inv = lax.rsqrt(jnp.mean(middle * middle, axis=-1, keepdims=True) + EPS)
    ffn_ref[...] = (middle * inv * gain2_ref[...]).astype(BF)
    for p in range(2):
        e_out(p, p).wait()
        for m in range(4):
            core_out[p][m].wait_send()
            fwd_out[p][m].wait_send()
    for m in range(4):
        far_out[m].wait_send()
        wide_out[m].wait_send()
    for copy in ffn_out:
        copy.wait()
    go_out.wait()


def forward(x, gain1, gain2, valid, tab, wq, wk, wv, wo, ids, grad_out, wg, wu, wd, chunk=256):
    slots, d = x.shape
    heads = wq.shape[1] // HEAD_DIM
    ff = wd.shape[0]
    assert heads == 4
    vmem, anywhere = pl.BlockSpec(memory_space=pltpu.VMEM), pl.BlockSpec(memory_space=pl.ANY)
    shape = jax.ShapeDtypeStruct
    dma = pltpu.SemaphoreType.DMA
    return pl.pallas_call(
        functools.partial(forward_kernel, heads, chunk),
        in_specs=[vmem] * 5 + [anywhere] * 11,
        out_specs=[vmem, anywhere] + [vmem] * 6 + [anywhere] * 4,
        out_shape=[
            shape((3, slots, d), BF),
            shape((8, 2, slots, slots), BF),
            shape((slots, d), BF),
            shape((slots, d), F32),
            shape((3, d, d), BF),
            shape((d, d), BF),
            shape((slots, d), F32),
            shape((slots, d), BF),
            shape((slots, d), BF),
            shape((ff, d), BF),
            shape((ff, d), BF),
            shape((ff, d), BF),
        ],
        scratch_shapes=[
            pltpu.VMEM((slots, d), BF),
            pltpu.VMEM((slots, 2 * HEAD_DIM), BF),
            pltpu.VMEM((3, slots, slots), I32),
            pltpu.VMEM((4, 16, LANES), F32),
            pltpu.VMEM((8, 8, LANES), I32),
            pltpu.VMEM((2, 2, slots, slots), BF),
            dma((2, 4)), dma((3,)), dma((2,)), dma((2, 4, 2)), dma((4, 2)), dma((4, 2)), dma((2, 4, 2)),
            dma((3, 2)), dma((4, 2)),
        ],
        compiler_params=pltpu.CompilerParams(
            vmem_limit_bytes=VMEM_LIMIT, collective_id=1, has_side_effects=True
        ),
        cost_estimate=pl.CostEstimate(flops=20 * slots * d * d, bytes_accessed=40 << 20, transcendentals=16 * slots * slots),
        name="forward",
    )(x, gain1, gain2, valid, tab, wq, wk, wv, wo, *ids, grad_out, wg, wu, wd)


def gelu_parts(v):
    c, k = math.sqrt(2.0 / math.pi), 0.044715
    square = v * v
    t = jnp.tanh(c * v * (1.0 + k * square))
    up = 0.5 * (1.0 + t)
    slope = up + 0.5 * v * (1.0 - t * t) * (c * (1.0 + 3.0 * k * square))
    return v * up, slope


def ffn_kernel(
    block,
    x_ref, go_ref, gofar_ref, middle_ref, gain_ref, w0_ref, w1_ref, w2_ref, c0_ref, c1_ref, c2_ref,
    out_ref, sum_ref, gm_ref, ga_ref, gain_out_ref,
    xall_ref, gall_ref, w_ref, xt_ref, gt_ref, act_ref, send_ref, recv_ref, own_ref, backfar_ref, backin_ref,
    in_sem, w_sem, x_sem, back_sem, dw_sem,
):
    slots, d = middle_ref.shape
    ff = w_ref.shape[2]
    halves = slots // block
    _, _, core, far, _, _ = neighbours()

    ins = [
        pltpu.make_async_copy(x_ref, xall_ref.at[pl.ds(0, slots), :], in_sem.at[0]),
        pltpu.make_async_copy(go_ref, gall_ref.at[pl.ds(0, slots), :], in_sem.at[1]),
        pltpu.make_async_copy(gofar_ref, gall_ref.at[pl.ds(slots, slots), :], in_sem.at[2]),
    ]
    weights = [
        [pltpu.make_async_copy(r, w_ref.at[q, m], w_sem.at[q, m]) for m, r in enumerate(group)]
        for q, group in enumerate(((w0_ref, w1_ref, w2_ref), (c0_ref, c1_ref, c2_ref)))
    ]
    for copy in ins[:2] + weights[0] + weights[1] + ins[2:]:
        copy.start()
    greet((core, far))
    x_out = [
        remote(x_ref.at[pl.ds(i * block, block), :], xall_ref.at[pl.ds(slots + i * block, block), :], x_sem.at[i], far)
        for i in range(halves)
    ]
    for copy in x_out:
        copy.start()
    back_out = [
        remote(backfar_ref.at[pl.ds(i * block, block), :], backin_ref.at[pl.ds(i * block, block), :], back_sem.at[i], far)
        for i in range(halves)
    ]
    for copy in ins + weights[0] + weights[1]:
        copy.wait()

    def step(b, carry):
        for i in range(halves):

            @pl.when(b == halves + i)
            def _():
                x_out[i].wait_recv()

        rows = pl.ds(pl.multiple_of(b * block, block), block)
        x, g = xall_ref[rows, :], gall_ref[rows, :]
        xt_ref[:, rows] = x.T
        gt_ref[:, rows] = g.T
        out = back = None
        for q in range(2):
            gate = lax.dot_general(x, w_ref[q, 0], NT, preferred_element_type=F32)
            upper = lax.dot_general(x, w_ref[q, 1], NT, preferred_element_type=F32)
            grad_hidden = lax.dot_general(g, w_ref[q, 2], NT, preferred_element_type=F32)
            gelu, slope = gelu_parts(gate)
            dg = (grad_hidden * upper * slope).astype(BF)
            du = (grad_hidden * gelu).astype(BF)
            hidden = (gelu * upper).astype(BF)
            act_ref[q, 0, rows, :] = dg
            act_ref[q, 1, rows, :] = du
            act_ref[q, 2, rows, :] = hidden
            o = jnp.dot(hidden, w_ref[q, 2], preferred_element_type=F32)
            k = jnp.dot(dg, w_ref[q, 0], preferred_element_type=F32)
            k = k + jnp.dot(du, w_ref[q, 1], preferred_element_type=F32)
            out, back = (o, k) if q == 0 else (out + o, back + k)
        out_ref[rows, :] = out.astype(BF)

        @pl.when(b < halves)
        def _():
            own_ref[rows, :] = back

        for i in range(halves):

            @pl.when(b == halves + i)
            def _():
                backfar_ref[i * block : (i + 1) * block, :] = back.astype(BF)
                back_out[i].start()

        return carry

    lax.fori_loop(0, 2 * halves, step, 0)

    tile = 256
    dw_out = [remote(send_ref.at[m], recv_ref.at[m], dw_sem.at[m], core) for m in range(3)]
    for q in (1, 0):
        for m in range(3):
            left = gt_ref if m == 2 else xt_ref
            target = send_ref if q == 1 else sum_ref

            def part(c, carry):
                rows = pl.ds(pl.multiple_of(c * tile, tile), tile)
                target[m, rows, :] = jnp.dot(left[rows, :], act_ref[q, m], preferred_element_type=F32).astype(BF)
                return carry

            lax.fori_loop(0, d // tile, part, 0)
            if q == 1:
                dw_out[m].start()
    for m in range(3):
        dw_out[m].wait_recv()
        sum_ref[m] = (sum_ref[m].astype(F32) + recv_ref[m].astype(F32)).astype(BF)

    for copy in back_out:
        copy.wait_recv()
    middle = middle_ref[...]
    inv = lax.rsqrt(jnp.mean(middle * middle, axis=-1, keepdims=True) + EPS)
    upstream = own_ref[...] + backin_ref[...].astype(F32)
    lifted = upstream * gain_ref[...]
    inner = jnp.mean(lifted * middle, axis=-1, keepdims=True)
    gain_out_ref[...] = jnp.sum(upstream * middle * inv, axis=0, keepdims=True)
    gm = gall_ref[0:slots, :].astype(F32) + inv * lifted - middle * (inv * inv * inv * inner)
    gm_ref[...] = gm
    ga_ref[...] = gm.astype(BF)
    for copy in x_out + back_out + dw_out:
        copy.wait_send()


def feed_forward(x, go, gofar, middle, gain, own, other, block=256):
    slots, d = x.shape
    ff = own[0].shape[0]
    vmem, anywhere = pl.BlockSpec(memory_space=pltpu.VMEM), pl.BlockSpec(memory_space=pl.ANY)
    shape = jax.ShapeDtypeStruct
    dma = pltpu.SemaphoreType.DMA
    halves = slots // block
    return pl.pallas_call(
        functools.partial(ffn_kernel, block),
        in_specs=[anywhere] * 3 + [vmem] * 2 + [anywhere] * 6,
        out_specs=[vmem] * 5,
        out_shape=[
            shape((2 * slots, d), BF),
            shape((3, d, ff), BF),
            shape((slots, d), F32),
            shape((slots, d), BF),
            shape((1, d), F32),
        ],
        scratch_shapes=[
            pltpu.VMEM((2 * slots, d), BF),
            pltpu.VMEM((2 * slots, d), BF),
            pltpu.VMEM((2, 3, ff, d), BF),
            pltpu.VMEM((d, 2 * slots), BF),
            pltpu.VMEM((d, 2 * slots), BF),
            pltpu.VMEM((2, 3, 2 * slots, ff), BF),
            pltpu.VMEM((3, d, ff), BF),
            pltpu.VMEM((3, d, ff), BF),
            pltpu.VMEM((slots, d), F32),
            pltpu.VMEM((slots, d), BF),
            pltpu.VMEM((slots, d), BF),
            dma((3,)), dma((2, 3)), dma((halves, 2)), dma((halves, 2)), dma((3, 2)),
        ],
        compiler_params=pltpu.CompilerParams(
            vmem_limit_bytes=VMEM_LIMIT, collective_id=2, has_side_effects=True
        ),
        cost_estimate=pl.CostEstimate(flops=36 * slots * d * ff, bytes_accessed=40 << 20, transcendentals=4 * slots * ff),
        name="feed_forward",
    )(x, go, gofar, middle, gain, *own, *other)


def attn_bwd_body(
    heads, ga_ref, wo_ref, ctx_ref, linv_ref, q_ref, k_ref, v_ref, p_ref,
    dq_ref, dk_ref, dv_ref, ds_ref, do_ref,
):
    hd, pw = HEAD_DIM, 2 * HEAD_DIM
    slots = ga_ref.shape[0]
    pair = pl.program_id(0)

    @pl.when(pair == 0)
    def _():
        d = lax.dot_general(ga_ref[...], wo_ref[...], NT, preferred_element_type=F32)
        for p in range(heads // 2):
            do_ref[p] = (d[:, p * pw : (p + 1) * pw] * linv_ref[:, p * pw : (p + 1) * pw]).astype(BF)

    lane = lax.broadcasted_iota(I32, (slots, pw), 1)
    low = lane < hd
    do2 = do_ref[pair]
    prod = do2.astype(F32) * ctx_ref[...].astype(F32)
    q2, k2, v2 = q_ref[...], k_ref[...], v_ref[...]
    vx = jnp.concatenate([v2, jnp.where(lane < 2, 1.0, 0.0).astype(BF)], axis=1)
    do_t, q_t = do2.T, q2.T
    zero = jnp.zeros_like(do2)
    dq, dk, dv = [], [], []
    for sub in range(2):
        mine = low if sub == 0 else jnp.logical_not(low)
        row = -jnp.sum(jnp.where(mine, prod, 0.0), axis=1, keepdims=True)
        head_part = row.astype(BF).astype(F32)
        extra = jnp.where(lane == 0, head_part, jnp.where(lane == 1, row - head_part, 0.0)).astype(BF)
        dox = jnp.concatenate([jnp.where(mine, do2, zero), extra], axis=1)
        t = lax.dot_general(dox, vx, NT, preferred_element_type=F32)
        e = p_ref[sub]
        ds = (e.astype(F32) * t).astype(BF)
        ds_ref[sub] = ds
        dv.append(jnp.dot(do_t[sub * hd : (sub + 1) * hd], e, preferred_element_type=F32))
        dk.append(jnp.dot(q_t[sub * hd : (sub + 1) * hd], ds, preferred_element_type=F32))
        dq.append(jnp.dot(ds, k2, preferred_element_type=F32))
    dq_ref[...] = jnp.where(low, dq[0], dq[1]).astype(BF)
    dk_ref[...] = jnp.concatenate(dk, axis=0).T.astype(BF)
    dv_ref[...] = jnp.concatenate(dv, axis=0).T.astype(BF)


def attn_bwd(ga, wo, ctx, linv, qkv, p, heads):
    slots, d = ga.shape
    hw, pw, pairs = heads * HEAD_DIM, 2 * HEAD_DIM, heads // 2
    full = lambda *sh: pl.BlockSpec(sh, lambda i: (0,) * len(sh))
    col = lambda off: pl.BlockSpec((slots, pw), lambda i: (0, off + i))
    block = pl.BlockSpec((2, slots, slots), lambda i: (i, 0, 0))
    return pl.pallas_call(
        functools.partial(attn_bwd_body, heads),
        grid=(pairs,),
        in_specs=[full(slots, d), full(hw, d), col(0), full(slots, hw), col(0), col(pairs), col(2 * pairs), block],
        out_specs=[col(0), col(0), col(0), block],
        scratch_shapes=[pltpu.VMEM((pairs, slots, pw), BF)],
        out_shape=[jax.ShapeDtypeStruct((slots, hw), BF)] * 3 + [jax.ShapeDtypeStruct((heads, slots, slots), BF)],
        compiler_params=pltpu.CompilerParams(vmem_limit_bytes=VMEM_LIMIT),
        cost_estimate=pl.CostEstimate(flops=6 * slots * d * hw, bytes_accessed=8 << 20, transcendentals=0),
        name="attn_bwd",
    )(ga, wo, ctx, linv, qkv, qkv, qkv, p)


def table_body(heads, buckets, blk, page_ref, ir_ref, ih_ref, iv_ref, *rest):
    ds_refs, (out_ref, acc_ref) = rest[:-2], rest[-2:]

    @pl.when(pl.program_id(0) == 0)
    def _():
        acc_ref[...] = jnp.zeros_like(acc_ref)

    rows, slots = ir_ref.shape[1], ir_ref.shape[2]
    one, zero = jnp.ones((blk, slots), BF), jnp.zeros((blk, slots), BF)

    def step(c, carry):
        r0 = pl.multiple_of(c * blk, blk)
        g = jnp.concatenate([r[h, pl.ds(r0, blk), :] for r in ds_refs for h in range(r.shape[0])], axis=0)
        for t, ref in enumerate((ir_ref, ih_ref, iv_ref)):
            ids = ref[0, pl.ds(r0, blk), :].astype(F32).astype(BF)
            hot = jnp.concatenate([jnp.where(ids == jnp.bfloat16(b), one, zero) for b in range(buckets)], axis=0)
            span = slice(t * buckets * blk, (t + 1) * buckets * blk)
            acc_ref[span, :] += lax.dot_general(hot, g, NT, preferred_element_type=F32)
        return carry

    lax.fori_loop(0, rows // blk, step, 0)

    @pl.when(pl.program_id(0) == pl.num_programs(0) - 1)
    def _():
        n = heads * blk
        same = lax.broadcasted_iota(I32, (blk, n), 0) == (lax.broadcasted_iota(I32, (blk, n), 1) & (blk - 1))
        for b in range(3 * buckets):
            rows_b = jnp.where(same, acc_ref[b * blk : (b + 1) * blk, :], 0.0)
            out_ref[b : b + 1, :] = jnp.sum(rows_b, axis=0, keepdims=True)


def table_grads(page, ids, dss, buckets, rows=64, blk=16):
    heads = sum(d.shape[0] for d in dss)
    slots = ids[0].shape[1]
    id_spec = pl.BlockSpec((1, rows, slots), lambda i, n: (n[0], i, 0))
    grid_spec = pltpu.PrefetchScalarGridSpec(
        num_scalar_prefetch=1,
        grid=(slots // rows,),
        in_specs=[id_spec] * 3 + [pl.BlockSpec((d.shape[0], rows, slots), lambda i, n: (0, i, 0)) for d in dss],
        out_specs=pl.BlockSpec((3 * buckets, heads * blk), lambda i, n: (0, 0)),
        scratch_shapes=[pltpu.VMEM((3 * buckets * blk, heads * blk), F32)],
    )
    out = pl.pallas_call(
        functools.partial(table_body, heads, buckets, blk),
        grid_spec=grid_spec,
        out_shape=jax.ShapeDtypeStruct((3 * buckets, heads * blk), F32),
        compiler_params=pltpu.CompilerParams(vmem_limit_bytes=VMEM_LIMIT),
        cost_estimate=pl.CostEstimate(
            flops=6 * buckets * blk * heads * slots * slots, bytes_accessed=12 << 20, transcendentals=0
        ),
        name="table_grads",
    )(page, *ids, *dss)
    return out.reshape(3 * buckets, heads, blk).sum(-1)


def fixed_tables(tables):
    rows = jnp.concatenate([t.T for t in tables], axis=0).astype(F32)
    rows = jnp.round(rows * FIXED)
    return jnp.pad(rows, ((0, 16 - rows.shape[0]), (0, LANES - rows.shape[1])))


def swap(x, axis, bit, size):
    return lax.ppermute(x, axis, [(i, i ^ bit) for i in range(size)])


def after(x, *others):
    return lax.optimization_barrier((x,) + others)[0]


def scatter_wide(x, size, kind):
    left = size
    while left > 1:
        bit = size // left
        side = (lax.axis_index("wide") // bit) % 2
        view = x.reshape((left // 2, 2) + x.shape[1:])
        keep = lax.dynamic_index_in_dim(view, side, 1, False)
        send = lax.dynamic_index_in_dim(view, 1 - side, 1, False).astype(kind)
        x = keep.astype(F32) + swap(send, "wide", bit, size).astype(F32)
        left //= 2
        if left > 1:
            x = x.astype(kind)
    return x[0]


def rms_forward(row_data, gain_vec):
    inv_rms = lax.rsqrt(jnp.mean(row_data * row_data, axis=-1, keepdims=True) + EPS)
    return (row_data * inv_rms * gain_vec, inv_rms)


def rms_backward(upstream, row_data, inv_rms, gain_vec):
    lifted = upstream * gain_vec
    inner = jnp.mean(lifted * row_data, axis=-1, keepdims=True)
    grad_rows = inv_rms * lifted - row_data * inv_rms * inv_rms * inv_rms * inner
    grad_gain = jnp.sum(upstream * row_data * inv_rms, axis=0)
    return (grad_rows, grad_gain)


def dot(a, b):
    return jnp.dot(a, b, preferred_element_type=F32)


def dot_nt(a, b):
    return lax.dot_general(a, b, NT, preferred_element_type=F32)


def dot_tn(a, b):
    return lax.dot_general(a, b, TN, preferred_element_type=F32)


def shards(
    wide, narrow, hidden_in, grad_out, gain_attn, gain_ffn, w_query, w_key, w_value, w_output,
    table_rel, table_horiz, table_vert, wi_gate, wi_up, wo_ffn, counts, patch_mask,
    bucket_rel, bucket_horiz, bucket_vert,
):
    slots = bucket_rel.shape[1]
    rows, d = hidden_in.shape
    buckets, heads = table_rel.shape
    width = w_query.shape[1]
    ff = wi_gate.shape[1]
    assert rows == slots and narrow == 4 and heads * HEAD_DIM == width
    me = lax.axis_index("narrow").astype(I32)
    page = me[None]
    core = lambda x: swap(x, "narrow", 1, narrow)
    far = lambda x: swap(x, "narrow", 2, narrow)

    positions = jnp.arange(slots, dtype=I32)
    text = slots - patch_mask.shape[1]
    count = lax.dynamic_index_in_dim(counts, me, 0, False)
    patches = lax.dynamic_index_in_dim(patch_mask, me, 0, False)
    valid = jnp.concatenate([positions[:text] < count, patches == 1]).astype(F32)[:, None]
    ids = (bucket_rel, bucket_horiz, bucket_vert)

    gain_first = gain_attn.astype(F32)
    gain_second = gain_ffn.astype(F32)
    qkv, exps, context, linv, w_all, wo_all, middle, ffn_own, grad_far, wg_core, wu_core, wd_core = forward(
        hidden_in, gain_first[None], gain_second[None], valid, fixed_tables((table_rel, table_horiz, table_vert)),
        w_query, w_key, w_value, w_output, ids, grad_out, wi_gate.T, wi_up.T, wo_ffn,
    )
    resid = hidden_in.astype(F32)
    normed, inv_first = rms_forward(resid, gain_first)
    normed = normed.astype(BF)
    out, ffn_sum, grad_middle, grad_attn, grad_gain_second = feed_forward(
        ffn_own, grad_out, grad_far, middle, gain_second[None],
        (wi_gate.T, wi_up.T, wo_ffn), (wg_core, wu_core, wd_core),
    )
    out_in = far(out[slots:])
    block_out = (middle + (out[:slots].astype(F32) + out_in.astype(F32))).astype(BF)
    ffn_sum = ffn_sum.reshape(3, wide, d // wide, ff).transpose(1, 0, 2, 3)
    ffn_sum = scatter_wide(ffn_sum, wide, BF)

    grads, dss, dqkv = [None] * 4, [None] * 4, [None] * 4
    for r in (3, 2, 1, 0):
        cols = slice(r * width, (r + 1) * width)
        ctx = context[:, cols]
        joined = jnp.concatenate([qkv[m, :, cols] for m in range(3)], axis=1)
        p = exps[2 * r : 2 * r + 2].reshape(heads, slots, slots)
        dq, dk, dv, dss[r] = attn_bwd(grad_attn, wo_all[cols], ctx, linv[:, cols], joined, p, heads)
        dqkv[r] = jnp.concatenate([dq, dk, dv], axis=1)
        grads[r] = jnp.concatenate([dot_tn(normed, dqkv[r]), dot_tn(grad_attn, ctx)], axis=1).astype(BF)
    far_sum = (grads[2].astype(F32) + core(grads[3]).astype(F32)).astype(BF)
    own_sum = grads[0].astype(F32) + core(grads[1]).astype(F32)
    attn_sum = (own_sum + far(far_sum).astype(F32)).astype(BF)
    attn_sum = scatter_wide(attn_sum.reshape(wide, d // wide, 4 * width), wide, BF)

    table_sum = table_grads(page, ids, dss, buckets)

    full_dqkv = [jnp.concatenate([dqkv[r][:, m * width : (m + 1) * width] for r in range(4)], axis=1) for m in range(3)]
    grad_normed = sum(dot_nt(full_dqkv[m], w_all[m]) for m in range(3))
    grad_norm, grad_gain_first = rms_backward(grad_normed, resid, inv_first, gain_first)
    grad_input = grad_middle + grad_norm

    per = d // (wide * narrow)
    gains = jnp.stack([grad_gain_first, grad_gain_second[0]]).reshape(2, wide, narrow, per)
    gains = jnp.stack([lax.dynamic_index_in_dim(gains, me ^ r, 2, False) for r in range(4)], axis=2)
    gains = gains.transpose(2, 1, 0, 3).reshape(4, wide, 2 * per)
    tabs = table_sum.reshape(3, wide, buckets // wide, 4, heads).transpose(3, 1, 0, 2, 4)
    small = jnp.concatenate([gains, tabs.reshape(4, wide, -1)], axis=2)
    small = small[0::2] + core(small[1::2])
    small = small[0] + far(small[1])
    small = scatter_wide(small, wide, F32)
    small_gains = small[: 2 * per].reshape(2, per)
    small_tabs = small[2 * per :].reshape(3, buckets // wide, heads)

    return (
        block_out,
        grad_input,
        small_gains[0],
        small_gains[1],
        attn_sum[:, :width],
        attn_sum[:, width : 2 * width],
        attn_sum[:, 2 * width : 3 * width],
        attn_sum[:, 3 * width :].T,
        small_tabs[0],
        small_tabs[1],
        small_tabs[2],
        ffn_sum[0],
        ffn_sum[1],
        ffn_sum[2].T,
    )


def solution(mesh):
    rows, both = P(("wide", "narrow"), None), P(("wide", "narrow"))
    cols, across = P(None, "narrow"), P("narrow", None)
    grid, turned = P("wide", "narrow"), P("narrow", "wide")
    pages = P("wide", None, None)
    return jax.shard_map(
        functools.partial(shards, mesh.shape["wide"], mesh.shape["narrow"]),
        mesh=mesh,
        in_specs=(
            rows, rows, P(), P(), cols, cols, cols, across, cols, cols, cols, cols, cols, across,
            P("wide"), P("wide", None), pages, pages, pages,
        ),
        out_specs=(
            rows, rows, both, both, grid, grid, grid, turned, grid, grid, grid, grid, grid, turned,
        ),
        check_vma=False,
    )
```

```python
import functools
import math

import jax
import jax.numpy as jnp
from jax import lax
from jax.experimental import pallas as pl
from jax.experimental.pallas import tpu as pltpu
from jax.sharding import PartitionSpec as P

F32 = jnp.float32
BF = jnp.bfloat16
I32 = jnp.int32
HEAD_DIM = 64
LANES = 128
EPS = 1e-06
NT = (((1,), (1,)), ((), ()))

FIXED = 2048.0
OFFSET = 8192
MASKED = -3.0e12
VMEM_LIMIT = 60 << 20
MESH = pl.DeviceIdType.MESH


def lookup(table_row, ids):
    return jnp.take_along_axis(table_row, ids, axis=1, mode="promise_in_bounds")


def neighbours():
    w, n = lax.axis_index("wide"), lax.axis_index("narrow")
    return w, n, (w, n ^ 1), (w, n ^ 2), (w, n ^ 3), (w ^ 1, n)


def greet(devices):
    barrier = pltpu.get_barrier_semaphore()
    for device in devices:
        pl.semaphore_signal(barrier, inc=1, device_id=device, device_id_type=MESH)
    pl.semaphore_wait(barrier, len(devices))


def remote(src, dst, sems, device):
    return pltpu.make_async_remote_copy(
        src_ref=src, dst_ref=dst, send_sem=sems.at[0], recv_sem=sems.at[1], device_id=device, device_id_type=MESH
    )


def forward_kernel(
    heads, chunk,
    x_ref, gain1_ref, gain2_ref, valid_ref, tab_ref, wq_ref, wk_ref, wv_ref, wo_ref, ir_ref, ih_ref, iv_ref,
    go_ref, wg_ref, wu_ref, wd_ref,
    qkv_ref, e_ref, ctx_ref, linv_ref, wall_ref, woall_ref, middle_ref, ffn_ref, gofar_ref, wgc_ref, wuc_ref, wdc_ref,
    normed_ref, mask_ref, ids_ref, tabs_ref, words_ref, ebuf_ref,
    own_sem, id_sem, e_sem, core_sem, far_sem, wide_sem, fwd_sem, tab_sem, big_sem,
):
    pw = 2 * HEAD_DIM
    slots, d = x_ref.shape
    w, n, core, far, diag, side = neighbours()
    half = w & 1
    other = 1 - half

    def source(m, pair):
        cols = pl.ds(pl.multiple_of(pair * pw, pw), pw)
        return wo_ref.at[cols, :] if m == 3 else (wq_ref, wk_ref, wv_ref)[m].at[:, cols]

    def place(m, slot):
        cols = pl.ds(pl.multiple_of(slot * pw, pw), pw)
        return woall_ref.at[cols, :] if m == 3 else wall_ref.at[m, :, cols]

    ids_in = [pltpu.make_async_copy(r.at[n], ids_ref.at[t], id_sem.at[t]) for t, r in enumerate((ir_ref, ih_ref, iv_ref))]
    own_in = [[pltpu.make_async_copy(source(m, p), place(m, p), own_sem.at[p, m]) for m in range(4)] for p in range(2)]
    for copy in own_in[0][:3] + ids_in + own_in[0][3:] + own_in[1]:
        copy.start()

    greet((core, far, diag, side))
    far_out = [remote(source(m, half), place(m, 4 + half), far_sem.at[m], far) for m in range(4)]
    core_out = [[remote(source(m, p), place(m, 2 + p), core_sem.at[p, m], core) for m in range(4)] for p in range(2)]
    tabs_out = [remote(tab_ref, tabs_ref.at[r], tab_sem.at[r - 1], dev) for r, dev in ((1, core), (2, far), (3, diag))]
    for copy in tabs_out + far_out[:1] + core_out[0] + core_out[1] + far_out[1:]:
        copy.start()
    wide_out = [remote(place(m, 4 + half), place(m, 4 + half), wide_sem.at[m], side) for m in range(4)]
    fwd_out = [
        [remote(place(m, 4 + p), place(m, 6 + p), fwd_sem.at[i, m], core) for m in range(4)]
        for i, p in enumerate((half, other))
    ]
    go_out = remote(go_ref, gofar_ref, big_sem.at[0], far)
    ffn_out = [
        remote(wg_ref, wgc_ref, big_sem.at[1], core),
        remote(wu_ref, wuc_ref, big_sem.at[2], core),
        remote(wd_ref, wdc_ref, big_sem.at[3], core),
    ]

    x = x_ref[...].astype(F32)
    inv = lax.rsqrt(jnp.mean(x * x, axis=-1, keepdims=True) + EPS)
    normed_ref[...] = (x * inv * gain1_ref[...]).astype(BF)
    lane_all = lax.broadcasted_iota(I32, (slots, pw), 1)
    shown = jnp.broadcast_to(valid_ref[...], (slots, pw)) > 0.5
    mask_ref[...] = jnp.where(lane_all == 0, jnp.where(shown, 0.0, MASKED), 0.0).astype(BF)
    ones = jnp.ones((slots, pw), BF)
    lane = lax.broadcasted_iota(I32, (chunk, pw), 1)
    low = lane < HEAD_DIM
    first = jnp.where(lane == 0, 1.0, 0.0).astype(BF)
    to_log2 = math.log2(math.e) / FIXED

    tabs_ref[0] = tab_ref[...]
    for copy in ids_in:
        copy.wait()
    for copy in tabs_out:
        copy.wait()
    for r in range(4):
        fixed = tabs_ref[r].astype(I32)
        for p in range(2):
            for t in range(3):
                row = t * heads + 2 * p
                words_ref[2 * r + p, t : t + 1, :] = fixed[row + 1 : row + 2] * 65536 + fixed[row : row + 1] + OFFSET

    def e_out(parity, slot):
        return pltpu.make_async_copy(ebuf_ref.at[parity], e_ref.at[slot], e_sem.at[parity])

    def slot_of(t):
        late = 4 + 2 * (t & 1) + jnp.where(t >= 6, other, half)
        return jnp.where(t < 4, t, late)

    def step(t, carry):
        slot = slot_of(t)
        for p in range(2):

            @pl.when(t == p)
            def _():
                for m in range(3):
                    own_in[p][m].wait()

            @pl.when(t == 2 + p)
            def _():
                for m in range(3):
                    core_out[p][m].wait_recv()

        for m in range(4):

            @pl.when(t == 2 + m)
            def _():
                far_out[m].wait_recv()
                wide_out[m].start()
                fwd_out[0][m].start()

        @pl.when(t == 3)
        def _():
            for copy in ffn_out:
                copy.start()

        @pl.when(t == 4)
        def _():
            go_out.start()

        @pl.when(t == 5)
        def _():
            for m in range(3):
                fwd_out[0][m].wait_recv()

        @pl.when(t == 6)
        def _():
            for m in range(3):
                wide_out[m].wait_recv()
                fwd_out[1][m].start()

        @pl.when(t == 7)
        def _():
            for m in range(3):
                fwd_out[1][m].wait_recv()
            wide_out[3].wait_recv()
            fwd_out[1][3].start()

        parity = t & 1

        @pl.when(t >= 2)
        def _():
            e_out(parity, slot).wait()

        cols = pl.ds(pl.multiple_of(slot * pw, pw), pw)
        weights = jnp.concatenate([wall_ref[m, :, cols] for m in range(3)], axis=1)
        joined = jnp.dot(normed_ref[...], weights, preferred_element_type=F32).astype(BF)
        for m in range(3):
            qkv_ref[m, :, cols] = joined[:, m * pw : (m + 1) * pw]
        kx = jnp.concatenate([joined[:, pw : 2 * pw], mask_ref[...]], axis=1)
        vx = jnp.concatenate([joined[:, 2 * pw :], ones], axis=1)
        words = words_ref[slot]
        for c in range(slots // chunk):
            rows = slice(c * chunk, (c + 1) * chunk)
            q2 = joined[rows, :pw] * jnp.bfloat16(FIXED)
            zero = jnp.zeros_like(q2)
            scores = []
            for sub in range(2):
                q = jnp.where(low, q2, zero) if sub == 0 else jnp.where(low, zero, q2)
                q = jnp.concatenate([q, first], axis=1)
                scores.append(lax.dot_general(q, kx, NT, preferred_element_type=F32))
            tabs = [jnp.broadcast_to(words[k : k + 1, :], (chunk, LANES)) for k in range(3)]
            parts = ([], [])
            for j in range(slots // LANES):
                sl = slice(j * LANES, (j + 1) * LANES)
                bias = (
                    lookup(tabs[0], ids_ref[0, rows, sl])
                    + lookup(tabs[1], ids_ref[1, rows, sl])
                    + lookup(tabs[2], ids_ref[2, rows, sl])
                )
                parts[0].append(scores[0][:, sl] + (bias & 0xFFFF).astype(F32))
                parts[1].append(scores[1][:, sl] + (bias >> 16).astype(F32))
            outs = []
            for sub in range(2):
                s = jnp.concatenate(parts[sub], axis=1)
                peak = jnp.max(s, axis=1, keepdims=True)
                e = jnp.exp2((s - peak) * to_log2).astype(BF)
                ebuf_ref[parity, sub, rows, :] = e
                outs.append(jnp.dot(e, vx, preferred_element_type=F32))
            linv = 1.0 / jnp.where(low, outs[0][:, pw:], outs[1][:, pw:])
            linv_ref[rows, cols] = linv
            ctx_ref[rows, cols] = (jnp.where(low, outs[0][:, :pw], outs[1][:, :pw]) * linv).astype(BF)
        e_out(parity, slot).start()
        return carry

    lax.fori_loop(0, 8, step, 0)
    for p in range(2):
        own_in[p][3].wait()
        core_out[p][3].wait_recv()
    for i in range(2):
        fwd_out[i][3].wait_recv()
    middle = x_ref[...].astype(F32) + jnp.dot(ctx_ref[...], woall_ref[...], preferred_element_type=F32)
    middle_ref[...] = middle
    inv = lax.rsqrt(jnp.mean(middle * middle, axis=-1, keepdims=True) + EPS)
    ffn_ref[...] = (middle * inv * gain2_ref[...]).astype(BF)
    for p in range(2):
        e_out(p, p).wait()
        for m in range(4):
            core_out[p][m].wait_send()
            fwd_out[p][m].wait_send()
    for m in range(4):
        far_out[m].wait_send()
        wide_out[m].wait_send()
    for copy in ffn_out:
        copy.wait()
    go_out.wait()


def forward(x, gain1, gain2, valid, tab, wq, wk, wv, wo, ids, grad_out, wg, wu, wd, chunk=256):
    slots, d = x.shape
    heads = wq.shape[1] // HEAD_DIM
    ff = wd.shape[0]
    assert heads == 4
    vmem, anywhere = pl.BlockSpec(memory_space=pltpu.VMEM), pl.BlockSpec(memory_space=pl.ANY)
    shape = jax.ShapeDtypeStruct
    dma = pltpu.SemaphoreType.DMA
    return pl.pallas_call(
        functools.partial(forward_kernel, heads, chunk),
        in_specs=[vmem] * 5 + [anywhere] * 11,
        out_specs=[vmem, anywhere] + [vmem] * 6 + [anywhere] * 4,
        out_shape=[
            shape((3, slots, d), BF),
            shape((8, 2, slots, slots), BF),
            shape((slots, d), BF),
            shape((slots, d), F32),
            shape((3, d, d), BF),
            shape((d, d), BF),
            shape((slots, d), F32),
            shape((slots, d), BF),
            shape((slots, d), BF),
            shape((ff, d), BF),
            shape((ff, d), BF),
            shape((ff, d), BF),
        ],
        scratch_shapes=[
            pltpu.VMEM((slots, d), BF),
            pltpu.VMEM((slots, 2 * HEAD_DIM), BF),
            pltpu.VMEM((3, slots, slots), I32),
            pltpu.VMEM((4, 16, LANES), F32),
            pltpu.VMEM((8, 8, LANES), I32),
            pltpu.VMEM((2, 2, slots, slots), BF),
            dma((2, 4)), dma((3,)), dma((2,)), dma((2, 4, 2)), dma((4, 2)), dma((4, 2)), dma((2, 4, 2)),
            dma((3, 2)), dma((4, 2)),
        ],
        compiler_params=pltpu.CompilerParams(
            vmem_limit_bytes=VMEM_LIMIT, collective_id=1, has_side_effects=True
        ),
        cost_estimate=pl.CostEstimate(flops=20 * slots * d * d, bytes_accessed=40 << 20, transcendentals=16 * slots * slots),
        name="forward",
    )(x, gain1, gain2, valid, tab, wq, wk, wv, wo, *ids, grad_out, wg, wu, wd)


def gelu_parts(v):
    c, k = math.sqrt(2.0 / math.pi), 0.044715
    square = v * v
    t = jnp.tanh(c * v * (1.0 + k * square))
    up = 0.5 * (1.0 + t)
    slope = up + 0.5 * v * (1.0 - t * t) * (c * (1.0 + 3.0 * k * square))
    return v * up, slope


def ffn_kernel(
    block,
    x_ref, go_ref, gofar_ref, middle_ref, gain_ref, w0_ref, w1_ref, w2_ref, c0_ref, c1_ref, c2_ref,
    out_ref, sum_ref, gm_ref, ga_ref, gain_out_ref,
    xall_ref, gall_ref, w_ref, xt_ref, gt_ref, act_ref, send_ref, recv_ref, own_ref, backfar_ref, backin_ref,
    in_sem, w_sem, x_sem, back_sem, dw_sem,
):
    slots, d = middle_ref.shape
    ff = w_ref.shape[2]
    halves = slots // block
    _, _, core, far, _, _ = neighbours()

    ins = [
        pltpu.make_async_copy(x_ref, xall_ref.at[pl.ds(0, slots), :], in_sem.at[0]),
        pltpu.make_async_copy(go_ref, gall_ref.at[pl.ds(0, slots), :], in_sem.at[1]),
        pltpu.make_async_copy(gofar_ref, gall_ref.at[pl.ds(slots, slots), :], in_sem.at[2]),
    ]
    weights = [
        [pltpu.make_async_copy(r, w_ref.at[q, m], w_sem.at[q, m]) for m, r in enumerate(group)]
        for q, group in enumerate(((w0_ref, w1_ref, w2_ref), (c0_ref, c1_ref, c2_ref)))
    ]
    for copy in ins[:2] + weights[0] + weights[1] + ins[2:]:
        copy.start()
    greet((core, far))
    x_out = [
        remote(x_ref.at[pl.ds(i * block, block), :], xall_ref.at[pl.ds(slots + i * block, block), :], x_sem.at[i], far)
        for i in range(halves)
    ]
    for copy in x_out:
        copy.start()
    back_out = [
        remote(backfar_ref.at[pl.ds(i * block, block), :], backin_ref.at[pl.ds(i * block, block), :], back_sem.at[i], far)
        for i in range(halves)
    ]
    for copy in ins + weights[0] + weights[1]:
        copy.wait()

    def step(b, carry):
        for i in range(halves):

            @pl.when(b == halves + i)
            def _():
                x_out[i].wait_recv()

        rows = pl.ds(pl.multiple_of(b * block, block), block)
        x, g = xall_ref[rows, :], gall_ref[rows, :]
        xt_ref[:, rows] = x.T
        gt_ref[:, rows] = g.T
        out = back = None
        for q in range(2):
            gate = lax.dot_general(x, w_ref[q, 0], NT, preferred_element_type=F32)
            upper = lax.dot_general(x, w_ref[q, 1], NT, preferred_element_type=F32)
            grad_hidden = lax.dot_general(g, w_ref[q, 2], NT, preferred_element_type=F32)
            gelu, slope = gelu_parts(gate)
            dg = (grad_hidden * upper * slope).astype(BF)
            du = (grad_hidden * gelu).astype(BF)
            hidden = (gelu * upper).astype(BF)
            act_ref[q, 0, rows, :] = dg
            act_ref[q, 1, rows, :] = du
            act_ref[q, 2, rows, :] = hidden
            o = jnp.dot(hidden, w_ref[q, 2], preferred_element_type=F32)
            k = jnp.dot(dg, w_ref[q, 0], preferred_element_type=F32)
            k = k + jnp.dot(du, w_ref[q, 1], preferred_element_type=F32)
            out, back = (o, k) if q == 0 else (out + o, back + k)
        out_ref[rows, :] = out.astype(BF)

        @pl.when(b < halves)
        def _():
            own_ref[rows, :] = back

        for i in range(halves):

            @pl.when(b == halves + i)
            def _():
                backfar_ref[i * block : (i + 1) * block, :] = back.astype(BF)
                back_out[i].start()

        return carry

    lax.fori_loop(0, 2 * halves, step, 0)

    tile = 256
    dw_out = [remote(send_ref.at[m], recv_ref.at[m], dw_sem.at[m], core) for m in range(3)]
    for q in (1, 0):
        for m in range(3):
            left = gt_ref if m == 2 else xt_ref
            target = send_ref if q == 1 else sum_ref

            def part(c, carry):
                rows = pl.ds(pl.multiple_of(c * tile, tile), tile)
                target[m, rows, :] = jnp.dot(left[rows, :], act_ref[q, m], preferred_element_type=F32).astype(BF)
                return carry

            lax.fori_loop(0, d // tile, part, 0)
            if q == 1:
                dw_out[m].start()
    for m in range(3):
        dw_out[m].wait_recv()
        sum_ref[m] = (sum_ref[m].astype(F32) + recv_ref[m].astype(F32)).astype(BF)

    for copy in back_out:
        copy.wait_recv()
    middle = middle_ref[...]
    inv = lax.rsqrt(jnp.mean(middle * middle, axis=-1, keepdims=True) + EPS)
    upstream = own_ref[...] + backin_ref[...].astype(F32)
    lifted = upstream * gain_ref[...]
    inner = jnp.mean(lifted * middle, axis=-1, keepdims=True)
    gain_out_ref[...] = jnp.sum(upstream * middle * inv, axis=0, keepdims=True)
    gm = gall_ref[0:slots, :].astype(F32) + inv * lifted - middle * (inv * inv * inv * inner)
    gm_ref[...] = gm
    ga_ref[...] = gm.astype(BF)
    for copy in x_out + back_out + dw_out:
        copy.wait_send()


def feed_forward(x, go, gofar, middle, gain, own, other, block=256):
    slots, d = x.shape
    ff = own[0].shape[0]
    vmem, anywhere = pl.BlockSpec(memory_space=pltpu.VMEM), pl.BlockSpec(memory_space=pl.ANY)
    shape = jax.ShapeDtypeStruct
    dma = pltpu.SemaphoreType.DMA
    halves = slots // block
    return pl.pallas_call(
        functools.partial(ffn_kernel, block),
        in_specs=[anywhere] * 3 + [vmem] * 2 + [anywhere] * 6,
        out_specs=[vmem] * 5,
        out_shape=[
            shape((2 * slots, d), BF),
            shape((3, d, ff), BF),
            shape((slots, d), F32),
            shape((slots, d), BF),
            shape((1, d), F32),
        ],
        scratch_shapes=[
            pltpu.VMEM((2 * slots, d), BF),
            pltpu.VMEM((2 * slots, d), BF),
            pltpu.VMEM((2, 3, ff, d), BF),
            pltpu.VMEM((d, 2 * slots), BF),
            pltpu.VMEM((d, 2 * slots), BF),
            pltpu.VMEM((2, 3, 2 * slots, ff), BF),
            pltpu.VMEM((3, d, ff), BF),
            pltpu.VMEM((3, d, ff), BF),
            pltpu.VMEM((slots, d), F32),
            pltpu.VMEM((slots, d), BF),
            pltpu.VMEM((slots, d), BF),
            dma((3,)), dma((2, 3)), dma((halves, 2)), dma((halves, 2)), dma((3, 2)),
        ],
        compiler_params=pltpu.CompilerParams(
            vmem_limit_bytes=VMEM_LIMIT, collective_id=2, has_side_effects=True
        ),
        cost_estimate=pl.CostEstimate(flops=36 * slots * d * ff, bytes_accessed=40 << 20, transcendentals=4 * slots * ff),
        name="feed_forward",
    )(x, go, gofar, middle, gain, *own, *other)


def backward_kernel(
    wide, heads, buckets, trows,
    ga_ref, x_ref, gain_ref, gain2_ref, fsum_ref, gm_ref, e_ref, ir_ref, ih_ref, iv_ref, out_ref,
    wo_ref, ctx_ref, linv_ref, qkv_ref, wall_ref,
    gi_ref, outin_ref, small_ref, gq_ref, gk_ref, gv_ref, go_ref, fg_ref, fu_ref, fd_ref,
    ds_ref, ids_ref, nt_ref, gat_ref, dx_ref, acc_ref, part_ref, crecv_ref, frecv_ref, xarecv_ref, zarecv_ref,
    xfrecv_ref, zfrecv_ref, nsend_ref, nrecv_ref, sxrecv_ref, szrecv_ref,
    in_sem, e_sem, core_sem, far_sem, out_sem, xf_sem, zf_sem, xa_sem, za_sem, sn_sem, sx_sem, sz_sem,
):
    pw = 2 * HEAD_DIM
    slots, d = ga_ref.shape
    half_rows = slots // 2
    ranks = wide // 2
    chunk = d // wide
    steps = 8 + slots // trows
    u = pl.program_id(0)
    w, n, core, far, diag, side = neighbours()
    par, rank = w & 1, w >> 1
    opp = 1 - par
    peer = lambda r: (2 * (rank ^ r) + par, n)
    slot_of = lambda k: 6 - 2 * (k >> 1) + (k & 1)
    slot = slot_of(jnp.minimum(u, 7))

    ins = [pltpu.make_async_copy(r.at[n], ids_ref.at[t], in_sem.at[t]) for t, r in enumerate((ir_ref, ih_ref, iv_ref))]
    gm_in = pltpu.make_async_copy(gm_ref, gi_ref, in_sem.at[3])
    core_out = [remote(part_ref.at[s], crecv_ref.at[i], core_sem.at[i], core) for i, s in enumerate((6, 7, 2, 3))]
    far_out = [
        [remote(part_ref.at[4 + i, :, p], frecv_ref.at[i, :, p], far_sem.at[i, k], far) for k, p in enumerate((opp, par))]
        for i in range(2)
    ]
    out_out = [
        remote(
            out_ref.at[pl.ds(slots + i * half_rows, half_rows), :],
            outin_ref.at[pl.ds(i * half_rows, half_rows), :], out_sem.at[i], far,
        )
        for i in range(2)
    ]
    xf_out = [remote(fsum_ref.at[:, rank ^ r, opp], xfrecv_ref.at[r], xf_sem.at[r], side) for r in range(ranks)]
    zf_out = [None] + [remote(xfrecv_ref.at[r], zfrecv_ref.at[r - 1], zf_sem.at[r - 1], peer(r)) for r in range(1, ranks)]
    xa_out = [remote(part_ref.at[i, :, opp], xarecv_ref.at[i], xa_sem.at[i], side) for i in range(2)]
    za_out = [
        [None]
        + [remote(part_ref.at[i, rank ^ r, par], zarecv_ref.at[i, r - 1], za_sem.at[i, r - 1], peer(r)) for r in range(1, ranks)]
        for i in range(2)
    ]
    sn_out = [
        remote(nsend_ref.at[r], nrecv_ref.at[r - 1], sn_sem.at[r - 1], dev) for r, dev in ((1, core), (2, far), (3, diag))
    ]
    sx_out = remote(nsend_ref.at[1], sxrecv_ref, sx_sem, side)
    sz_out = [None] + [remote(nsend_ref.at[2], szrecv_ref.at[r - 1], sz_sem.at[r - 1], peer(r)) for r in range(1, ranks)]

    def e_in(k):
        s = slot_of(k)
        return pltpu.make_async_copy(e_ref.at[s], ds_ref.at[s], e_sem.at[k & 1])

    def wide_f32(ref_value):
        return ref_value.astype(F32)

    @pl.when(u == 0)
    def _():
        e_in(0).start()
        for copy in ins + [gm_in]:
            copy.start()
        greet([core, far, diag, side] + [peer(r) for r in range(1, ranks)])
        for r in range(1, max(2, ranks - 1)):
            xf_out[r].start()
        out_out[0].start()
        x = x_ref[...].astype(F32)
        inv = lax.rsqrt(jnp.mean(x * x, axis=-1, keepdims=True) + EPS)
        nt_ref[...] = (x * inv * gain_ref[...]).astype(BF).T
        gat_ref[...] = ga_ref[...].T
        dx_ref[...] = jnp.zeros_like(dx_ref)
        acc_ref[...] = jnp.zeros_like(acc_ref)

    @pl.when(u < 8)
    def _():
        e_in(u).wait()

        @pl.when(u < 7)
        def _():
            e_in(u + 1).start()

        lane = lax.broadcasted_iota(I32, (slots, pw), 1)
        low = lane < HEAD_DIM
        do2 = (lax.dot_general(ga_ref[...], wo_ref[...], NT, preferred_element_type=F32) * linv_ref[...]).astype(BF)
        prod = do2.astype(F32) * ctx_ref[...].astype(F32)
        q2, k2, v2 = qkv_ref[0], qkv_ref[1], qkv_ref[2]
        vx = jnp.concatenate([v2, jnp.where(lane < 2, 1.0, 0.0).astype(BF)], axis=1)
        do_t, q_t = do2.T, q2.T
        zero = jnp.zeros_like(do2)
        dq, dk, dv = [], [], []
        for sub in range(2):
            mine = low if sub == 0 else jnp.logical_not(low)
            row = -jnp.sum(jnp.where(mine, prod, 0.0), axis=1, keepdims=True)
            head_part = row.astype(BF).astype(F32)
            extra = jnp.where(lane == 0, head_part, jnp.where(lane == 1, row - head_part, 0.0)).astype(BF)
            dox = jnp.concatenate([jnp.where(mine, do2, zero), extra], axis=1)
            t = lax.dot_general(dox, vx, NT, preferred_element_type=F32)
            e = ds_ref[slot, sub]
            ds = (e.astype(F32) * t).astype(BF)
            dv.append(jnp.dot(do_t[sub * HEAD_DIM : (sub + 1) * HEAD_DIM], e, preferred_element_type=F32))
            ds_ref[slot, sub] = ds
            dk.append(jnp.dot(q_t[sub * HEAD_DIM : (sub + 1) * HEAD_DIM], ds, preferred_element_type=F32))
            dq.append(jnp.dot(ds, k2, preferred_element_type=F32))
        joined = jnp.concatenate(
            [
                jnp.where(low, dq[0], dq[1]).astype(BF),
                jnp.concatenate(dk, axis=0).T.astype(BF),
                jnp.concatenate(dv, axis=0).T.astype(BF),
            ],
            axis=1,
        )
        weights = jnp.concatenate([wall_ref[m] for m in range(3)], axis=1)
        dx_ref[...] += lax.dot_general(joined, weights, NT, preferred_element_type=F32)
        part = jnp.dot(nt_ref[...], joined, preferred_element_type=F32).astype(BF)
        part_ref[slot, :, :, :, : 3 * pw] = part.reshape(ranks, 2, chunk, 3 * pw)
        part = jnp.dot(gat_ref[...], ctx_ref[...], preferred_element_type=F32).astype(BF)
        part_ref[slot, :, :, :, 3 * pw :] = part.reshape(ranks, 2, chunk, pw)

    @pl.when(u >= 8)
    def _():
        blk = 16
        one, zero = jnp.ones((blk, slots), BF), jnp.zeros((blk, slots), BF)

        @pl.when(u == 8)
        def _():
            for copy in ins:
                copy.wait()

        def sub_block(c, carry):
            rows = pl.ds(pl.multiple_of((u - 8) * trows + c * blk, blk), blk)
            g = jnp.concatenate([ds_ref[s, sub, rows, :] for s in range(8) for sub in range(2)], axis=0)
            for t in range(3):
                ids = ids_ref[t, rows, :].astype(F32).astype(BF)
                hot = jnp.concatenate([jnp.where(ids == jnp.bfloat16(b), one, zero) for b in range(buckets)], axis=0)
                span = slice(t * buckets * blk, (t + 1) * buckets * blk)
                acc_ref[span, :] += lax.dot_general(hot, g, NT, preferred_element_type=F32)
            return carry

        lax.fori_loop(0, trows // blk, sub_block, 0)

    def event(step):
        return lambda body: pl.when(u == step)(body)

    for i in range(2):

        @event(i)
        def _():
            core_out[i].start()

        @event(4 + i)
        def _():
            core_out[2 + i].start()

        @event(2 + i)
        def _():
            core_out[i].wait_recv()
            for k, p in enumerate((opp, par)):
                total = wide_f32(part_ref[4 + i, :, p]) + wide_f32(crecv_ref[i, :, p])
                part_ref[4 + i, :, p] = total.astype(BF)
                far_out[i][k].start()

    def far_stage(i):
        core_out[2 + i].wait_recv()
        far_out[i][0].wait_recv()
        total = wide_f32(part_ref[i, :, opp]) + wide_f32(crecv_ref[2 + i, :, opp]) + wide_f32(frecv_ref[i, :, opp])
        part_ref[i, :, opp] = total.astype(BF)
        xa_out[i].start()

    def side_stage(i):
        far_out[i][1].wait_recv()
        xa_out[i].wait_recv()
        total = wide_f32(part_ref[i, :, par]) + wide_f32(crecv_ref[2 + i, :, par])
        total = total + wide_f32(frecv_ref[i, :, par]) + wide_f32(xarecv_ref[i])
        part_ref[i, :, par] = total.astype(BF)
        for r in range(1, ranks):
            za_out[i][r].start()

    def ffn_stage(r):
        xf_out[r].wait_recv()
        xfrecv_ref[r] = (wide_f32(fsum_ref[:, rank ^ r, par]) + wide_f32(xfrecv_ref[r])).astype(BF)
        if r > 0:
            zf_out[r].start()

    for r in range(1, ranks):

        @event(3 + (r - 1) * 6 // max(1, ranks - 2))
        def _():
            ffn_stage(r)

    @event(4)
    def _():
        if ranks > 2:
            xf_out[ranks - 1].start()

    event(6)(lambda: far_stage(0))

    @event(7)
    def _():
        gm_in.wait()
        x = x_ref[...].astype(F32)
        inv = lax.rsqrt(jnp.mean(x * x, axis=-1, keepdims=True) + EPS)
        upstream = dx_ref[...]
        lifted = upstream * gain_ref[...]
        inner = jnp.mean(lifted * x, axis=-1, keepdims=True)
        gi_ref[...] = gi_ref[...] + inv * lifted - x * (inv * inv * inv * inner)
        gains = jnp.sum(upstream * x * inv, axis=0, keepdims=True)
        lanes = d // LANES
        for r in range(4):
            for j in range(lanes):
                span = slice(j * LANES, (j + 1) * LANES)
                nsend_ref[r, 3 * buckets + j : 3 * buckets + j + 1, :] = gains[:, span]
                nsend_ref[r, 3 * buckets + lanes + j : 3 * buckets + lanes + j + 1, :] = gain2_ref[:, span]

    event(12)(lambda: side_stage(0))

    @event(13)
    def _():
        far_stage(1)
        xf_out[0].start()
        out_out[1].start()

    @pl.when(u == steps - 1)
    def _():
        blk, cols = 16, 16 * 16
        same = lax.broadcasted_iota(I32, (blk, cols), 0) == (lax.broadcasted_iota(I32, (blk, cols), 1) & (blk - 1))
        picked = [
            jnp.sum(jnp.where(same, acc_ref[b * blk : (b + 1) * blk, :], 0.0), axis=0, keepdims=True)
            for b in range(3 * buckets)
        ]
        picked = jnp.concatenate(picked, axis=0)
        source = lax.broadcasted_iota(I32, (cols, LANES), 0) >> 4
        target = lax.broadcasted_iota(I32, (cols, LANES), 1)
        for r in range(4):
            choose = jnp.where((source == target + heads * r) & (target < heads), 1.0, 0.0).astype(F32)
            nsend_ref[r, : 3 * buckets, :] = jnp.dot(
                picked, choose, preferred_element_type=F32, precision=lax.Precision.HIGHEST
            )
        for copy in sn_out:
            copy.start()
        for copy in sn_out:
            copy.wait()
        nsend_ref[1] = nsend_ref[0] + nrecv_ref[0] + nrecv_ref[1] + nrecv_ref[2]
        sx_out.start()
        side_stage(1)
        sx_out.wait()
        nsend_ref[2] = nsend_ref[1] + sxrecv_ref[...]
        for r in range(1, ranks):
            sz_out[r].start()

        def finish(i):
            total = wide_f32(part_ref[i, rank, par])
            for r in range(1, ranks):
                za_out[i][r].wait_recv()
                total = total + wide_f32(zarecv_ref[i, r - 1])
            cols = slice(i * pw, (i + 1) * pw)
            gq_ref[:, cols] = total[:, :pw]
            gk_ref[:, cols] = total[:, pw : 2 * pw]
            gv_ref[:, cols] = total[:, 2 * pw : 3 * pw]
            go_ref[cols, :] = total[:, 3 * pw :].T

        finish(0)
        total = nsend_ref[2]
        for r in range(1, ranks):
            sz_out[r].wait_recv()
            total = total + szrecv_ref[r - 1]
        small_ref[...] = total
        ffn_stage(0)
        for r in range(1, ranks):
            zf_out[r].wait_recv()
        for m, ref in enumerate((fg_ref, fu_ref, fd_ref)):
            total = wide_f32(xfrecv_ref[0, m])
            for r in range(1, ranks):
                total = total + wide_f32(zfrecv_ref[r - 1, m])
            ref[...] = total.T
        finish(1)
        for copy in out_out:
            copy.wait()
        for copy in core_out + far_out[0] + far_out[1] + xf_out + zf_out[1:] + xa_out + za_out[0][1:] + za_out[1][1:] + sz_out[1:]:
            copy.wait_send()


def backward(wide, buckets, ga, x, gain, gain2, fsum, gm, e, ids, out, wo_all, ctx, linv, qkv, w_all, trows=64):
    slots, d = x.shape
    heads = 4
    pw = 2 * HEAD_DIM
    ranks, chunk = wide // 2, d // wide
    ff = fsum.shape[-1]
    width = heads * HEAD_DIM
    small = 3 * buckets + 2 * d // LANES
    vmem, anywhere = pl.BlockSpec(memory_space=pltpu.VMEM), pl.BlockSpec(memory_space=pl.ANY)
    shape = jax.ShapeDtypeStruct
    dma = pltpu.SemaphoreType.DMA

    def slot(u):
        k = jnp.minimum(u, 7)
        return 6 - 2 * (k >> 1) + (k & 1)

    return pl.pallas_call(
        functools.partial(backward_kernel, wide, heads, buckets, trows),
        grid=(8 + slots // trows,),
        in_specs=[vmem] * 5 + [anywhere] * 6 + [
            pl.BlockSpec((pw, d), lambda u: (slot(u), 0)),
            pl.BlockSpec((slots, pw), lambda u: (0, slot(u))),
            pl.BlockSpec((slots, pw), lambda u: (0, slot(u))),
            pl.BlockSpec((3, slots, pw), lambda u: (0, 0, slot(u))),
            pl.BlockSpec((3, d, pw), lambda u: (0, 0, slot(u))),
        ],
        out_specs=[vmem, anywhere] + [vmem] * 8,
        out_shape=[
            shape((slots, d), F32),
            shape((slots, d), BF),
            shape((small, LANES), F32),
            shape((chunk, width), F32),
            shape((chunk, width), F32),
            shape((chunk, width), F32),
            shape((width, chunk), F32),
            shape((ff, chunk), F32),
            shape((ff, chunk), F32),
            shape((ff, chunk), F32),
        ],
        scratch_shapes=[
            pltpu.VMEM((8, 2, slots, slots), BF),
            pltpu.VMEM((3, slots, slots), I32),
            pltpu.VMEM((d, slots), BF),
            pltpu.VMEM((d, slots), BF),
            pltpu.VMEM((slots, d), F32),
            pltpu.VMEM((3 * buckets * 16, 16 * 16), F32),
            pltpu.VMEM((8, ranks, 2, chunk, 4 * pw), BF),
            pltpu.VMEM((4, ranks, 2, chunk, 4 * pw), BF),
            pltpu.VMEM((2, ranks, 2, chunk, 4 * pw), BF),
            pltpu.VMEM((2, ranks, chunk, 4 * pw), BF),
            pltpu.VMEM((2, ranks - 1, chunk, 4 * pw), BF),
            pltpu.VMEM((ranks, 3, chunk, ff), BF),
            pltpu.VMEM((ranks - 1, 3, chunk, ff), BF),
            pltpu.VMEM((4, small, LANES), F32),
            pltpu.VMEM((3, small, LANES), F32),
            pltpu.VMEM((small, LANES), F32),
            pltpu.VMEM((ranks - 1, small, LANES), F32),
            dma((4,)), dma((2,)), dma((4, 2)), dma((2, 2, 2)), dma((2, 2)), dma((ranks, 2)), dma((ranks - 1, 2)),
            dma((2, 2)), dma((2, ranks - 1, 2)), dma((3, 2)), dma((2,)), dma((ranks - 1, 2)),
        ],
        compiler_params=pltpu.CompilerParams(
            vmem_limit_bytes=VMEM_LIMIT, collective_id=3, has_side_effects=True
        ),
        cost_estimate=pl.CostEstimate(flops=30 * slots * d * d, bytes_accessed=60 << 20, transcendentals=0),
        name="backward",
    )(ga, x, gain, gain2, fsum, gm, e, *ids, out, wo_all, ctx, linv, qkv, w_all)


def fixed_tables(tables):
    rows = jnp.concatenate([t.T for t in tables], axis=0).astype(F32)
    rows = jnp.round(rows * FIXED)
    return jnp.pad(rows, ((0, 16 - rows.shape[0]), (0, LANES - rows.shape[1])))


def shards(
    wide, narrow, hidden_in, grad_out, gain_attn, gain_ffn, w_query, w_key, w_value, w_output,
    table_rel, table_horiz, table_vert, wi_gate, wi_up, wo_ffn, counts, patch_mask,
    bucket_rel, bucket_horiz, bucket_vert,
):
    slots = bucket_rel.shape[1]
    rows, d = hidden_in.shape
    buckets, heads = table_rel.shape
    width = w_query.shape[1]
    ff = wi_gate.shape[1]
    assert rows == slots and narrow == 4 and heads * HEAD_DIM == width
    me = lax.axis_index("narrow").astype(I32)

    positions = jnp.arange(slots, dtype=I32)
    text = slots - patch_mask.shape[1]
    count = lax.dynamic_index_in_dim(counts, me, 0, False)
    patches = lax.dynamic_index_in_dim(patch_mask, me, 0, False)
    valid = jnp.concatenate([positions[:text] < count, patches == 1]).astype(F32)[:, None]
    ids = (bucket_rel, bucket_horiz, bucket_vert)

    gain_first = gain_attn.astype(F32)
    gain_second = gain_ffn.astype(F32)
    qkv, exps, context, linv, w_all, wo_all, middle, ffn_own, grad_far, wg_core, wu_core, wd_core = forward(
        hidden_in, gain_first[None], gain_second[None], valid, fixed_tables((table_rel, table_horiz, table_vert)),
        w_query, w_key, w_value, w_output, ids, grad_out, wi_gate.T, wi_up.T, wo_ffn,
    )
    out, ffn_sum, grad_middle, grad_attn, grad_gain_second = feed_forward(
        ffn_own, grad_out, grad_far, middle, gain_second[None],
        (wi_gate.T, wi_up.T, wo_ffn), (wg_core, wu_core, wd_core),
    )
    grad_input, out_in, small, gq, gk, gv, go, fg, fu, fd = backward(
        wide, buckets, grad_attn, hidden_in, gain_first[None], grad_gain_second,
        ffn_sum.reshape(3, wide // 2, 2, d // wide, ff), grad_middle, exps, ids, out,
        wo_all, context, linv, qkv, w_all,
    )
    block_out = (middle + (out[:slots].astype(F32) + out_in.astype(F32))).astype(BF)

    place = lax.axis_index("wide")
    per = d // (wide * narrow)
    gains = small[3 * buckets :].reshape(2, d)
    gains = lax.dynamic_slice_in_dim(gains, (place * narrow + me) * per, per, 1)
    tables = small[: 3 * buckets, :heads].reshape(3, buckets, heads)
    tables = lax.dynamic_slice_in_dim(tables, place * (buckets // wide), buckets // wide, 1)
    return (
        block_out, grad_input, gains[0], gains[1], gq, gk, gv, go,
        tables[0], tables[1], tables[2], fg.T, fu.T, fd,
    )


def solution(mesh):
    rows, both = P(("wide", "narrow"), None), P(("wide", "narrow"))
    cols, across = P(None, "narrow"), P("narrow", None)
    grid, turned = P("wide", "narrow"), P("narrow", "wide")
    pages = P("wide", None, None)
    return jax.shard_map(
        functools.partial(shards, mesh.shape["wide"], mesh.shape["narrow"]),
        mesh=mesh,
        in_specs=(
            rows, rows, P(), P(), cols, cols, cols, across, cols, cols, cols, cols, cols, across,
            P("wide"), P("wide", None), pages, pages, pages,
        ),
        out_specs=(
            rows, rows, both, both, grid, grid, grid, turned, grid, grid, grid, grid, grid, turned,
        ),
        check_vma=False,
    )
```

```python
import functools
import math

import jax
import jax.numpy as jnp
from jax import lax
from jax.experimental import pallas as pl
from jax.experimental.pallas import tpu as pltpu
from jax.sharding import PartitionSpec as P

F32 = jnp.float32
BF = jnp.bfloat16
I32 = jnp.int32
HEAD_DIM = 64
LANES = 128
EPS = 1e-06
NT = (((1,), (1,)), ((), ()))

FIXED = 2048.0
OFFSET = 8192
MASKED = -3.0e12
VMEM_LIMIT = 60 << 20
MESH = pl.DeviceIdType.MESH


def lookup(table_row, ids):
    return jnp.take_along_axis(table_row, ids, axis=1, mode="promise_in_bounds")


def neighbours():
    w, n = lax.axis_index("wide"), lax.axis_index("narrow")
    return w, n, (w, n ^ 1), (w, n ^ 2), (w, n ^ 3), (w ^ 1, n)


def greet(devices):
    barrier = pltpu.get_barrier_semaphore()
    for device in devices:
        pl.semaphore_signal(barrier, inc=1, device_id=device, device_id_type=MESH)
    pl.semaphore_wait(barrier, len(devices))


def remote(src, dst, sems, device):
    return pltpu.make_async_remote_copy(
        src_ref=src, dst_ref=dst, send_sem=sems.at[0], recv_sem=sems.at[1], device_id=device, device_id_type=MESH
    )


def forward_kernel(
    heads, buckets, chunk,
    counts_ref, patch_ref, x_ref, gain1_ref, gain2_ref, tr_ref, th_ref, tv_ref,
    wq_ref, wk_ref, wv_ref, wo_ref, ir_ref, ih_ref, iv_ref, go_ref, wg_ref, wu_ref, wd_ref,
    qkv_ref, e_ref, ctx_ref, linv_ref, wall_ref, woall_ref, middle_ref, ffn_ref, gofar_ref, wgc_ref, wuc_ref, wdc_ref,
    normed_ref, mask_ref, ids_ref, tab_ref, tabs_ref, words_ref, ebuf_ref,
    own_sem, id_sem, e_sem, core_sem, far_sem, deep_sem, wide_sem, fwd_sem, tab_sem, big_sem,
):
    pw = 2 * HEAD_DIM
    slots, d = x_ref.shape
    piece = d // 2
    w, n, core, far, diag, side = neighbours()
    deep = (w ^ 2, n)
    half, share = w & 1, (w >> 1) & 1
    other = 1 - half

    def source(m, pair, part=None):
        cols = pl.ds(pl.multiple_of(pair * pw, pw), pw)
        span = slice(None) if part is None else pl.ds(pl.multiple_of(part * piece, piece), piece)
        return wo_ref.at[cols, span] if m == 3 else (wq_ref, wk_ref, wv_ref)[m].at[span, cols]

    def place(m, slot, part=None):
        cols = pl.ds(pl.multiple_of(slot * pw, pw), pw)
        span = slice(None) if part is None else pl.ds(pl.multiple_of(part * piece, piece), piece)
        return woall_ref.at[cols, span] if m == 3 else wall_ref.at[m, span, cols]

    ids_in = [pltpu.make_async_copy(r.at[n], ids_ref.at[t], id_sem.at[t]) for t, r in enumerate((ir_ref, ih_ref, iv_ref))]
    own_in = [[pltpu.make_async_copy(source(m, p), place(m, p), own_sem.at[p, m]) for m in range(4)] for p in range(2)]
    for copy in own_in[0][:3] + ids_in + own_in[0][3:] + own_in[1]:
        copy.start()

    tab_ref[...] = jnp.zeros_like(tab_ref)
    for t, r in enumerate((tr_ref, th_ref, tv_ref)):
        tab_ref[t * heads : (t + 1) * heads, :buckets] = jnp.floor(r[...].astype(F32) * FIXED + 0.5)

    greet((core, far, diag, side, deep))
    far_out = [remote(source(m, half, share), place(m, 4 + half, share), far_sem.at[m], far) for m in range(4)]
    deep_out = [remote(place(m, 4 + half, share), place(m, 4 + half, share), deep_sem.at[m], deep) for m in range(4)]
    core_out = [[remote(source(m, p), place(m, 2 + p), core_sem.at[p, m], core) for m in range(4)] for p in range(2)]
    tabs_out = [remote(tab_ref, tabs_ref.at[r - 1], tab_sem.at[r - 1], dev) for r, dev in ((1, core), (2, far), (3, diag))]
    wide_out = [
        [remote(place(m, 4 + half, k), place(m, 4 + half, k), wide_sem.at[m, i], side) for i, k in enumerate((share, 1 - share))]
        for m in range(4)
    ]
    fwd_out = [
        [remote(place(m, 4 + half, k), place(m, 6 + half, k), fwd_sem.at[m, i], core) for i, k in enumerate((share, 1 - share))]
        for m in range(4)
    ]
    last_out = [remote(place(m, 4 + other), place(m, 6 + other), fwd_sem.at[m, 2], core) for m in range(4)]
    go_out = remote(go_ref, gofar_ref, big_sem.at[0], far)
    ffn_out = [
        remote(wg_ref, wgc_ref, big_sem.at[1], core),
        remote(wu_ref, wuc_ref, big_sem.at[2], core),
        remote(wd_ref, wdc_ref, big_sem.at[3], core),
    ]
    for copy in tabs_out + far_out + [go_out] + core_out[0] + core_out[1]:
        copy.start()

    x = x_ref[...].astype(F32)
    inv = lax.rsqrt(jnp.mean(x * x, axis=-1, keepdims=True) + EPS)
    normed_ref[...] = (x * inv * gain1_ref[...].astype(F32)[None]).astype(BF)
    text = slots - patch_ref.shape[1]
    shown = jnp.concatenate(
        [
            jnp.where(lax.broadcasted_iota(I32, (1, text), 1) < counts_ref[n], 1, 0),
            patch_ref[pl.ds(n, 1), :],
        ],
        axis=1,
    )
    column = jnp.broadcast_to(jnp.where(shown == 1, 0.0, MASKED), (pw, slots)).T
    lane_all = lax.broadcasted_iota(I32, (slots, pw), 1)
    mask_ref[...] = jnp.where(lane_all == 0, column, 0.0).astype(BF)
    ones = jnp.ones((slots, pw), BF)
    lane = lax.broadcasted_iota(I32, (chunk, pw), 1)
    low = lane < HEAD_DIM
    first = jnp.where(lane == 0, 1.0, 0.0).astype(BF)
    to_log2 = math.log2(math.e) / FIXED

    def pack_words(r, table):
        fixed = table.astype(I32)
        for p in range(2):
            for t in range(3):
                row = t * heads + 2 * p
                words_ref[2 * r + p, t : t + 1, :] = fixed[row + 1 : row + 2] * 65536 + fixed[row : row + 1] + OFFSET

    pack_words(0, tab_ref[...])
    for copy in ids_in:
        copy.wait()

    def e_out(parity, slot):
        return pltpu.make_async_copy(ebuf_ref.at[parity], e_ref.at[slot], e_sem.at[parity])

    def slot_of(t):
        late = 4 + 2 * (t & 1) + jnp.where(t >= 6, other, half)
        return jnp.where(t < 4, t, late)

    plan = [[] for _ in range(16)]

    def far_arrived(m):
        far_out[m].wait_recv()
        deep_out[m].start()
        wide_out[m][0].start()
        fwd_out[m][0].start()

    def deep_arrived(m):
        deep_out[m].wait_recv()
        wide_out[m][1].start()
        fwd_out[m][1].start()

    def wide_arrived(m):
        for copy in wide_out[m]:
            copy.wait_recv()
        last_out[m].start()

    def tables_arrived():
        for r, copy in enumerate(tabs_out):
            copy.wait()
            pack_words(r + 1, tabs_ref[r])

    for p in range(2):
        plan[2 * p].extend(own_in[p][m].wait for m in range(3))
        plan[4 + 2 * p].extend(core_out[p][m].wait_recv for m in range(3))
    plan[3].append(tables_arrived)
    for m in range(4):
        plan[2 + m].append(functools.partial(far_arrived, m))
        plan[4 + m].append(functools.partial(deep_arrived, m))
    plan[7].extend(copy.start for copy in ffn_out)
    plan[10].extend(copy.wait_recv for m in range(3) for copy in fwd_out[m])
    plan[12].extend(functools.partial(wide_arrived, m) for m in range(3))
    plan[14].extend(last_out[m].wait_recv for m in range(3))
    plan[14].append(functools.partial(wide_arrived, 3))

    def events(t, c):
        for k in range(8):
            if plan[2 * k + c]:

                @pl.when(t == k)
                def _():
                    for action in plan[2 * k + c]:
                        action()

    def step(t, carry):
        slot = slot_of(t)
        events(t, 0)
        parity = t & 1

        @pl.when(t >= 2)
        def _():
            e_out(parity, slot).wait()

        cols = pl.ds(pl.multiple_of(slot * pw, pw), pw)
        weights = jnp.concatenate([wall_ref[m, :, cols] for m in range(3)], axis=1)
        joined = jnp.dot(normed_ref[...], weights, preferred_element_type=F32).astype(BF)
        for m in range(3):
            qkv_ref[m, :, cols] = joined[:, m * pw : (m + 1) * pw]
        kx = jnp.concatenate([joined[:, pw : 2 * pw], mask_ref[...]], axis=1)
        vx = jnp.concatenate([joined[:, 2 * pw :], ones], axis=1)
        words = words_ref[slot]
        for c in range(slots // chunk):
            if c == slots // chunk // 2:
                events(t, 1)
            rows = slice(c * chunk, (c + 1) * chunk)
            q2 = joined[rows, :pw] * jnp.bfloat16(FIXED)
            zero = jnp.zeros_like(q2)
            scores = []
            for sub in range(2):
                q = jnp.where(low, q2, zero) if sub == 0 else jnp.where(low, zero, q2)
                q = jnp.concatenate([q, first], axis=1)
                scores.append(lax.dot_general(q, kx, NT, preferred_element_type=F32))
            tabs = [jnp.broadcast_to(words[k : k + 1, :], (chunk, LANES)) for k in range(3)]
            parts = ([], [])
            for j in range(slots // LANES):
                sl = slice(j * LANES, (j + 1) * LANES)
                bias = (
                    lookup(tabs[0], ids_ref[0, rows, sl])
                    + lookup(tabs[1], ids_ref[1, rows, sl])
                    + lookup(tabs[2], ids_ref[2, rows, sl])
                )
                parts[0].append(scores[0][:, sl] + (bias & 0xFFFF).astype(F32))
                parts[1].append(scores[1][:, sl] + (bias >> 16).astype(F32))
            outs = []
            for sub in range(2):
                s = jnp.concatenate(parts[sub], axis=1)
                peak = jnp.max(s, axis=1, keepdims=True)
                e = jnp.exp2((s - peak) * to_log2).astype(BF)
                ebuf_ref[parity, sub, rows, :] = e
                outs.append(jnp.dot(e, vx, preferred_element_type=F32))
            linv = 1.0 / jnp.where(low, outs[0][:, pw:], outs[1][:, pw:])
            linv_ref[rows, cols] = linv
            ctx_ref[rows, cols] = (jnp.where(low, outs[0][:, :pw], outs[1][:, :pw]) * linv).astype(BF)
        e_out(parity, slot).start()
        return carry

    lax.fori_loop(0, 8, step, 0)
    for p in range(2):
        own_in[p][3].wait()
        core_out[p][3].wait_recv()
    for copy in fwd_out[3] + last_out[3:]:
        copy.wait_recv()
    middle = x_ref[...].astype(F32) + jnp.dot(ctx_ref[...], woall_ref[...], preferred_element_type=F32)
    middle_ref[...] = middle
    inv = lax.rsqrt(jnp.mean(middle * middle, axis=-1, keepdims=True) + EPS)
    ffn_ref[...] = (middle * inv * gain2_ref[...].astype(F32)[None]).astype(BF)
    for p in range(2):
        e_out(p, p).wait()
        for m in range(4):
            core_out[p][m].wait_send()
    for m in range(4):
        for copy in [far_out[m], deep_out[m], last_out[m]] + wide_out[m] + fwd_out[m]:
            copy.wait_send()
    for copy in ffn_out:
        copy.wait()
    go_out.wait()


def forward(counts, patches, x, gain1, gain2, tables, wq, wk, wv, wo, ids, grad_out, wg, wu, wd, chunk=256):
    slots, d = x.shape
    heads = wq.shape[1] // HEAD_DIM
    buckets = tables[0].shape[1]
    ff = wd.shape[0]
    assert heads == 4
    vmem, anywhere = pl.BlockSpec(memory_space=pltpu.VMEM), pl.BlockSpec(memory_space=pl.ANY)
    shape = jax.ShapeDtypeStruct
    dma = pltpu.SemaphoreType.DMA
    return pl.pallas_call(
        functools.partial(forward_kernel, heads, buckets, chunk),
        in_specs=[pl.BlockSpec(memory_space=pltpu.SMEM)] + [vmem] * 7 + [anywhere] * 11,
        out_specs=[vmem, anywhere] + [vmem] * 6 + [anywhere] * 4,
        out_shape=[
            shape((3, slots, d), BF),
            shape((8, 2, slots, slots), BF),
            shape((slots, d), BF),
            shape((slots, d), F32),
            shape((3, d, d), BF),
            shape((d, d), BF),
            shape((slots, d), F32),
            shape((slots, d), BF),
            shape((slots, d), BF),
            shape((ff, d), BF),
            shape((ff, d), BF),
            shape((ff, d), BF),
        ],
        scratch_shapes=[
            pltpu.VMEM((slots, d), BF),
            pltpu.VMEM((slots, 2 * HEAD_DIM), BF),
            pltpu.VMEM((3, slots, slots), I32),
            pltpu.VMEM((16, LANES), F32),
            pltpu.VMEM((3, 16, LANES), F32),
            pltpu.VMEM((8, 8, LANES), I32),
            pltpu.VMEM((2, 2, slots, slots), BF),
            dma((2, 4)), dma((3,)), dma((2,)), dma((2, 4, 2)), dma((4, 2)), dma((4, 2)), dma((4, 2, 2)), dma((4, 3, 2)),
            dma((3, 2)), dma((4, 2)),
        ],
        compiler_params=pltpu.CompilerParams(
            vmem_limit_bytes=VMEM_LIMIT, collective_id=1, has_side_effects=True
        ),
        cost_estimate=pl.CostEstimate(flops=20 * slots * d * d, bytes_accessed=40 << 20, transcendentals=16 * slots * slots),
        name="forward",
    )(counts, patches, x, gain1, gain2, *tables, wq, wk, wv, wo, *ids, grad_out, wg, wu, wd)


def gelu_parts(v):
    c, k = math.sqrt(2.0 / math.pi), 0.044715
    square = v * v
    t = jnp.tanh(c * v * (1.0 + k * square))
    up = 0.5 * (1.0 + t)
    slope = up + 0.5 * v * (1.0 - t * t) * (c * (1.0 + 3.0 * k * square))
    return v * up, slope


def split_quarter(ff):
    return ff // LANES * LANES, ff % LANES


def packed_width(ff):
    full, rest = split_quarter(ff)
    return 3 * full + -(-3 * rest // LANES) * LANES


def ffn_kernel(
    block, ff,
    x_ref, go_ref, gofar_ref, middle_ref, gain_ref, w0_ref, w1_ref, w2_ref, c0_ref, c1_ref, c2_ref,
    out_ref, sum_ref, gm_ref, ga_ref, gain_out_ref,
    xall_ref, gall_ref, wgu_ref, wd_ref, xt_ref, gt_ref, act_ref, send_ref, recv_ref, own_ref, backfar_ref, backin_ref,
    in_sem, w_sem, x_sem, back_sem, dw_sem,
):
    slots, d = middle_ref.shape
    halves = slots // block
    full, rest = split_quarter(ff)
    both = 2 * ff
    _, _, core, far, _, _ = neighbours()

    ins = [
        pltpu.make_async_copy(x_ref, xall_ref.at[pl.ds(0, slots), :], in_sem.at[0]),
        pltpu.make_async_copy(go_ref, gall_ref.at[pl.ds(0, slots), :], in_sem.at[1]),
        pltpu.make_async_copy(gofar_ref, gall_ref.at[pl.ds(slots, slots), :], in_sem.at[2]),
    ]
    weights = []
    for m, pair in enumerate(((w0_ref, c0_ref), (w1_ref, c1_ref), (w2_ref, c2_ref))):
        target, base = (wd_ref, 0) if m == 2 else (wgu_ref, m * both)
        for q, r in enumerate(pair):
            for k, (start, size, at) in enumerate(((0, full, q * full), (full, rest, 2 * full + q * rest))):
                if size:
                    weights.append(
                        pltpu.make_async_copy(
                            r.at[pl.ds(start, size), :], target.at[pl.ds(base + at, size), :], w_sem.at[m, q, k]
                        )
                    )
    for copy in ins[:2] + weights + ins[2:]:
        copy.start()
    greet((core, far))
    x_out = [
        remote(x_ref.at[pl.ds(i * block, block), :], xall_ref.at[pl.ds(slots + i * block, block), :], x_sem.at[i], far)
        for i in range(halves)
    ]
    for copy in x_out:
        copy.start()
    back_out = [
        remote(backfar_ref.at[pl.ds(i * block, block), :], backin_ref.at[pl.ds(i * block, block), :], back_sem.at[i], far)
        for i in range(halves)
    ]
    for copy in ins + weights:
        copy.wait()

    def step(b, carry):
        for i in range(halves):

            @pl.when(b == halves + i)
            def _():
                x_out[i].wait_recv()

        rows = pl.ds(pl.multiple_of(b * block, block), block)
        x, g = xall_ref[rows, :], gall_ref[rows, :]
        xt_ref[:, rows] = x.T
        gt_ref[:, rows] = g.T
        grown = lax.dot_general(x, wgu_ref[...], NT, preferred_element_type=F32)
        grad_hidden = lax.dot_general(g, wd_ref[...], NT, preferred_element_type=F32)
        gate, upper = grown[:, :both], grown[:, both:]
        gelu, slope = gelu_parts(gate)
        dg = (grad_hidden * upper * slope).astype(BF)
        du = (grad_hidden * gelu).astype(BF)
        hidden = (gelu * upper).astype(BF)
        act_ref[0, rows, :] = dg
        act_ref[1, rows, :] = du
        act_ref[2, rows, :] = hidden
        back = jnp.dot(jnp.concatenate([dg, du], axis=1), wgu_ref[...], preferred_element_type=F32)

        @pl.when(b < halves)
        def _():
            own_ref[rows, :] = back

        for i in range(halves):

            @pl.when(b == halves + i)
            def _():
                backfar_ref[i * block : (i + 1) * block, :] = back.astype(BF)
                back_out[i].start()

        out_ref[rows, :] = jnp.dot(hidden, wd_ref[...], preferred_element_type=F32).astype(BF)
        return carry

    lax.fori_loop(0, 2 * halves, step, 0)

    tile = d // 2
    used = 3 * (full + rest)
    dw_out = [
        remote(send_ref.at[pl.ds(c * tile, tile), :], recv_ref.at[pl.ds(c * tile, tile), :], dw_sem.at[c], core)
        for c in range(2)
    ]
    for c in range(2):
        rows = slice(c * tile, (c + 1) * tile)
        for m in range(3):
            left = gt_ref if m == 2 else xt_ref
            dw = jnp.dot(left[rows, :], act_ref[m], preferred_element_type=F32).astype(BF)
            for q, target in enumerate((sum_ref, send_ref)):
                target[rows, m * full : (m + 1) * full] = dw[:, q * full : (q + 1) * full]
                if rest:
                    at = 2 * full + q * rest
                    target[rows, 3 * full + m * rest : 3 * full + (m + 1) * rest] = dw[:, at : at + rest]
        for target in (sum_ref, send_ref):
            if used < target.shape[1]:
                target[rows, used:] = jnp.zeros((tile, target.shape[1] - used), BF)
        dw_out[c].start()
    for c in range(2):
        rows = slice(c * tile, (c + 1) * tile)
        dw_out[c].wait_recv()
        sum_ref[rows, :] = (sum_ref[rows, :].astype(F32) + recv_ref[rows, :].astype(F32)).astype(BF)

    for copy in back_out:
        copy.wait_recv()
    middle = middle_ref[...]
    inv = lax.rsqrt(jnp.mean(middle * middle, axis=-1, keepdims=True) + EPS)
    upstream = own_ref[...] + backin_ref[...].astype(F32)
    lifted = upstream * gain_ref[...].astype(F32)[None]
    inner = jnp.mean(lifted * middle, axis=-1, keepdims=True)
    gain_out_ref[...] = jnp.sum(upstream * middle * inv, axis=0, keepdims=True)
    gm = gall_ref[0:slots, :].astype(F32) + inv * lifted - middle * (inv * inv * inv * inner)
    gm_ref[...] = gm
    ga_ref[...] = gm.astype(BF)
    for copy in x_out + back_out + dw_out:
        copy.wait_send()


def feed_forward(x, go, gofar, middle, gain, own, other, block=256):
    slots, d = x.shape
    ff = own[0].shape[0]
    vmem, anywhere = pl.BlockSpec(memory_space=pltpu.VMEM), pl.BlockSpec(memory_space=pl.ANY)
    shape = jax.ShapeDtypeStruct
    dma = pltpu.SemaphoreType.DMA
    halves = slots // block
    packed = packed_width(ff)
    return pl.pallas_call(
        functools.partial(ffn_kernel, block, ff),
        in_specs=[anywhere] * 3 + [vmem] * 2 + [anywhere] * 6,
        out_specs=[vmem] * 5,
        out_shape=[
            shape((2 * slots, d), BF),
            shape((d, packed), BF),
            shape((slots, d), F32),
            shape((slots, d), BF),
            shape((1, d), F32),
        ],
        scratch_shapes=[
            pltpu.VMEM((2 * slots, d), BF),
            pltpu.VMEM((2 * slots, d), BF),
            pltpu.VMEM((4 * ff, d), BF),
            pltpu.VMEM((2 * ff, d), BF),
            pltpu.VMEM((d, 2 * slots), BF),
            pltpu.VMEM((d, 2 * slots), BF),
            pltpu.VMEM((3, 2 * slots, 2 * ff), BF),
            pltpu.VMEM((d, packed), BF),
            pltpu.VMEM((d, packed), BF),
            pltpu.VMEM((slots, d), F32),
            pltpu.VMEM((slots, d), BF),
            pltpu.VMEM((slots, d), BF),
            dma((3,)), dma((3, 2, 2)), dma((halves, 2)), dma((halves, 2)), dma((2, 2)),
        ],
        compiler_params=pltpu.CompilerParams(
            vmem_limit_bytes=VMEM_LIMIT, collective_id=2, has_side_effects=True
        ),
        cost_estimate=pl.CostEstimate(flops=36 * slots * d * ff, bytes_accessed=40 << 20, transcendentals=4 * slots * ff),
        name="feed_forward",
    )(x, go, gofar, middle, gain, *own, *other)


def backward_slot(k):
    return jnp.where(k < 4, 6 - 2 * (k & 1) + (k >> 1), 6 - 2 * (k >> 1) + (k & 1))


def backward_kernel(
    wide, heads, buckets, trows, ff,
    ga_ref, x_ref, gain_ref, gain2_ref, fsum_ref, gm_ref, e_ref, ir_ref, ih_ref, iv_ref, out_ref,
    wo_ref, ctx_ref, linv_ref, qkv_ref, wall_ref,
    gi_ref, outin_ref, small_ref, gq_ref, gk_ref, gv_ref, go_ref, fg_ref, fu_ref, fd_ref,
    ds_ref, ids_ref, nt_ref, gat_ref, dx_ref, acc_ref, part_ref, crecv_ref, frecv_ref, xarecv_ref, zarecv_ref,
    xfrecv_ref, zfrecv_ref, nsend_ref, nrecv_ref, sxrecv_ref, szrecv_ref,
    in_sem, e_sem, core_sem, far_sem, out_sem, xf_sem, zf_sem, xa_sem, za_sem, sn_sem, sx_sem, sz_sem,
):
    pw = 2 * HEAD_DIM
    slots, d = ga_ref.shape
    half_rows = slots // 2
    ranks = wide // 2
    chunk = d // wide
    steps = 8 + slots // trows
    u = pl.program_id(0)
    w, n, core, far, diag, side = neighbours()
    par, rank = w & 1, w >> 1
    opp = 1 - par
    peer = lambda r: (2 * (rank ^ r) + par, n)
    slot_of = backward_slot
    slot = slot_of(jnp.minimum(u, 7))

    ins = [pltpu.make_async_copy(r.at[n], ids_ref.at[t], in_sem.at[t]) for t, r in enumerate((ir_ref, ih_ref, iv_ref))]
    gm_in = pltpu.make_async_copy(gm_ref, gi_ref, in_sem.at[3])
    core_out = [remote(part_ref.at[s], crecv_ref.at[i], core_sem.at[i], core) for i, s in enumerate((6, 7, 2, 3))]
    order = list(range(ranks - 1, 0, -2)) + list(range(ranks - 2, -1, -2))
    far_out = [
        [
            [
                remote(part_ref.at[4 + i, rank ^ r, p], frecv_ref.at[i, rank ^ r, p], far_sem.at[i, k, r], far)
                for r in range(ranks)
            ]
            for k, p in enumerate((opp, par))
        ]
        for i in range(2)
    ]
    out_out = [
        remote(
            out_ref.at[pl.ds(slots + i * half_rows, half_rows), :],
            outin_ref.at[pl.ds(i * half_rows, half_rows), :], out_sem.at[i], far,
        )
        for i in range(2)
    ]
    xf_out = [None] + [remote(fsum_ref.at[rank ^ r, opp], xfrecv_ref.at[r], xf_sem.at[r], side) for r in range(1, ranks)]
    some = chunk // 2
    xf_last = [
        remote(
            fsum_ref.at[rank, opp, pl.ds(k * some, some), :], xfrecv_ref.at[0, pl.ds(k * some, some), :],
            xf_sem.at[k * ranks], side,
        )
        for k in range(2)
    ]
    low_bit = lambda r: r & -r
    zf_out = [None] + [
        remote(xfrecv_ref.at[r], zfrecv_ref.at[r - 1], zf_sem.at[r - 1], peer(low_bit(r))) for r in range(1, ranks)
    ]
    feeds = lambda r: [r | (1 << b) for b in range(ranks.bit_length() - 1) if (1 << b) < (low_bit(r) if r else ranks)]
    xa_out = [
        [remote(part_ref.at[i, rank ^ r, opp], xarecv_ref.at[i, r], xa_sem.at[i, r], side) for r in range(ranks)]
        for i in range(2)
    ]
    za_out = [
        [None]
        + [
            remote(part_ref.at[i, rank ^ r, par], zarecv_ref.at[i, r - 1], za_sem.at[i, r - 1], peer(low_bit(r)))
            for r in range(1, ranks)
        ]
        for i in range(2)
    ]
    sn_out = [
        remote(nsend_ref.at[r], nrecv_ref.at[r - 1], sn_sem.at[r - 1], dev) for r, dev in ((1, core), (2, far), (3, diag))
    ]
    sx_out = remote(nsend_ref.at[1], sxrecv_ref, sx_sem, side)
    sz_out = [None] + [remote(nsend_ref.at[2], szrecv_ref.at[r - 1], sz_sem.at[r - 1], peer(r)) for r in range(1, ranks)]

    def e_in(k):
        s = slot_of(k)
        return pltpu.make_async_copy(e_ref.at[s], ds_ref.at[s], e_sem.at[k & 1])

    def wide_f32(ref_value):
        return ref_value.astype(F32)

    @pl.when(u == 0)
    def _():
        e_in(0).start()
        for copy in ins + [gm_in]:
            copy.start()
        greet([core, far, diag, side] + [peer(r) for r in range(1, ranks)])
        for r in range(ranks - 1, 0, -1):
            xf_out[r].start()
        out_out[0].start()
        x = x_ref[...].astype(F32)
        inv = lax.rsqrt(jnp.mean(x * x, axis=-1, keepdims=True) + EPS)
        nt_ref[...] = (x * inv * gain_ref[...].astype(F32)[None]).astype(BF).T
        gat_ref[...] = ga_ref[...].T
        dx_ref[...] = jnp.zeros_like(dx_ref)
        acc_ref[...] = jnp.zeros_like(acc_ref)

    @pl.when(u < 8)
    def _():
        e_in(u).wait()

        @pl.when(u < 7)
        def _():
            e_in(u + 1).start()

        lane = lax.broadcasted_iota(I32, (slots, pw), 1)
        low = lane < HEAD_DIM
        do2 = (lax.dot_general(ga_ref[...], wo_ref[...], NT, preferred_element_type=F32) * linv_ref[...]).astype(BF)
        prod = do2.astype(F32) * ctx_ref[...].astype(F32)
        q2, k2, v2 = qkv_ref[0], qkv_ref[1], qkv_ref[2]
        vx = jnp.concatenate([v2, jnp.where(lane < 2, 1.0, 0.0).astype(BF)], axis=1)
        do_t, q_t = do2.T, q2.T
        zero = jnp.zeros_like(do2)
        dq, dk, dv = [], [], []
        for sub in range(2):
            mine = low if sub == 0 else jnp.logical_not(low)
            row = -jnp.sum(jnp.where(mine, prod, 0.0), axis=1, keepdims=True)
            head_part = row.astype(BF).astype(F32)
            extra = jnp.where(lane == 0, head_part, jnp.where(lane == 1, row - head_part, 0.0)).astype(BF)
            dox = jnp.concatenate([jnp.where(mine, do2, zero), extra], axis=1)
            t = lax.dot_general(dox, vx, NT, preferred_element_type=F32)
            e = ds_ref[slot, sub]
            ds = (e.astype(F32) * t).astype(BF)
            dv.append(jnp.dot(do_t[sub * HEAD_DIM : (sub + 1) * HEAD_DIM], e, preferred_element_type=F32))
            ds_ref[slot, sub] = ds
            dk.append(jnp.dot(q_t[sub * HEAD_DIM : (sub + 1) * HEAD_DIM], ds, preferred_element_type=F32))
            dq.append(jnp.dot(ds, k2, preferred_element_type=F32))
        joined = jnp.concatenate(
            [
                jnp.where(low, dq[0], dq[1]).astype(BF),
                jnp.concatenate(dk, axis=0).T.astype(BF),
                jnp.concatenate(dv, axis=0).T.astype(BF),
            ],
            axis=1,
        )
        weights = jnp.concatenate([wall_ref[m] for m in range(3)], axis=1)
        dx_ref[...] += lax.dot_general(joined, weights, NT, preferred_element_type=F32)
        part = jnp.dot(nt_ref[...], joined, preferred_element_type=F32).astype(BF)
        part_ref[slot, :, :, :, : 3 * pw] = part.reshape(ranks, 2, chunk, 3 * pw)
        part = jnp.dot(gat_ref[...], ctx_ref[...], preferred_element_type=F32).astype(BF)
        part_ref[slot, :, :, :, 3 * pw :] = part.reshape(ranks, 2, chunk, pw)

    @pl.when(u >= 8)
    def _():
        blk = 16
        one, zero = jnp.ones((blk, slots), BF), jnp.zeros((blk, slots), BF)

        @pl.when(u == 8)
        def _():
            for copy in ins:
                copy.wait()

        def sub_block(c, carry):
            rows = pl.ds(pl.multiple_of((u - 8) * trows + c * blk, blk), blk)
            g = jnp.concatenate([ds_ref[s, sub, rows, :] for s in range(8) for sub in range(2)], axis=0)
            for t in range(3):
                ids = ids_ref[t, rows, :].astype(F32).astype(BF)
                hot = jnp.concatenate([jnp.where(ids == jnp.bfloat16(b), one, zero) for b in range(buckets)], axis=0)
                span = slice(t * buckets * blk, (t + 1) * buckets * blk)
                acc_ref[span, :] += lax.dot_general(hot, g, NT, preferred_element_type=F32)
            return carry

        lax.fori_loop(0, trows // blk, sub_block, 0)

    def event(step):
        return lambda body: pl.when(u == step)(body)

    def core_stage(i):
        core_out[i].wait_recv()
        for p in (opp, par):
            total = wide_f32(part_ref[4 + i, :, p]) + wide_f32(crecv_ref[i, :, p])
            part_ref[4 + i, :, p] = total.astype(BF)
        for r in order:
            far_out[i][0][r].start()

    def own_sides():
        for i in range(2):
            for r in order:
                far_out[i][1][r].start()

    def far_stage(i):
        core_out[2 + i].wait_recv()
        for r in order:
            far_out[i][0][r].wait_recv()
            k = rank ^ r
            total = wide_f32(part_ref[i, k, opp]) + wide_f32(crecv_ref[2 + i, k, opp]) + wide_f32(frecv_ref[i, k, opp])
            part_ref[i, k, opp] = total.astype(BF)
            xa_out[i][r].start()

    def side_stage(i, r):
        far_out[i][1][r].wait_recv()
        xa_out[i][r].wait_recv()
        k = rank ^ r
        total = wide_f32(part_ref[i, k, par]) + wide_f32(crecv_ref[2 + i, k, par])
        total = total + wide_f32(frecv_ref[i, k, par]) + wide_f32(xarecv_ref[i, r])
        part_ref[i, k, par] = total.astype(BF)
        if r & 1:
            za_out[i][r].start()

    def rank_stage(i, r):
        total = wide_f32(part_ref[i, rank ^ r, par])
        for k in feeds(r):
            za_out[i][k].wait_recv()
            total = total + wide_f32(zarecv_ref[i, k - 1])
        if r == 0:
            return total
        part_ref[i, rank ^ r, par] = total.astype(BF)
        za_out[i][r].start()

    def ffn_stage(r):
        for copy in xf_last if r == 0 else [xf_out[r]]:
            copy.wait_recv()
        total = wide_f32(fsum_ref[rank ^ r, par]) + wide_f32(xfrecv_ref[r])
        for k in feeds(r):
            zf_out[k].wait_recv()
            total = total + wide_f32(zfrecv_ref[k - 1])
        if r == 0:
            return total
        xfrecv_ref[r] = total.astype(BF)
        zf_out[r].start()

    def input_gradient():
        gm_in.wait()
        x = x_ref[...].astype(F32)
        inv = lax.rsqrt(jnp.mean(x * x, axis=-1, keepdims=True) + EPS)
        upstream = dx_ref[...]
        lifted = upstream * gain_ref[...].astype(F32)[None]
        inner = jnp.mean(lifted * x, axis=-1, keepdims=True)
        gi_ref[...] = gi_ref[...] + inv * lifted - x * (inv * inv * inv * inner)
        gains = jnp.sum(upstream * x * inv, axis=0, keepdims=True)
        lanes = d // LANES
        for r in range(4):
            for j in range(lanes):
                span = slice(j * LANES, (j + 1) * LANES)
                nsend_ref[r, 3 * buckets + j : 3 * buckets + j + 1, :] = gains[:, span]
                nsend_ref[r, 3 * buckets + lanes + j : 3 * buckets + lanes + j + 1, :] = gain2_ref[:, span]

    plan = [[] for _ in range(steps)]
    for i in range(2):
        plan[2 * i].append(core_out[i].start)
        plan[2 * i + 1].append(functools.partial(core_stage, i))
        plan[4 + i].append(core_out[2 + i].start)
    plan[3].append(own_sides)
    for k, r in enumerate(range(ranks - 1, 0, -1)):
        plan[(3, 6, 8)[k] if ranks == 4 else 3 + k * 6 // ranks].append(functools.partial(ffn_stage, r))
    plan[6].append(functools.partial(far_stage, 0))
    plan[7].append(input_gradient)
    plan[8].append(functools.partial(far_stage, 1))
    plan[8].append(xf_last[0].start)
    plan[12].extend(functools.partial(side_stage, 0, r) for r in order)
    plan[15].extend(functools.partial(rank_stage, 0, r) for r in range(ranks - 2, 0, -2))
    for k in range(steps):

        @pl.when(u == k)
        def _():
            for action in plan[k]:
                action()

    @pl.when(u == steps - 1)
    def _():
        blk, cols = 16, 16 * 16
        same = lax.broadcasted_iota(I32, (blk, cols), 0) == (lax.broadcasted_iota(I32, (blk, cols), 1) & (blk - 1))
        picked = [
            jnp.sum(jnp.where(same, acc_ref[b * blk : (b + 1) * blk, :], 0.0), axis=0, keepdims=True)
            for b in range(3 * buckets)
        ]
        picked = jnp.concatenate(picked, axis=0)
        source = lax.broadcasted_iota(I32, (cols, LANES), 0) >> 4
        target = lax.broadcasted_iota(I32, (cols, LANES), 1)
        for r in range(4):
            choose = jnp.where((source == target + heads * r) & (target < heads), 1.0, 0.0).astype(F32)
            nsend_ref[r, : 3 * buckets, :] = jnp.dot(
                picked, choose, preferred_element_type=F32, precision=lax.Precision.HIGHEST
            )
        for copy in sn_out + out_out[1:]:
            copy.start()

        def finish(i):
            total = rank_stage(i, 0)
            cols = slice(i * pw, (i + 1) * pw)
            gq_ref[:, cols] = total[:, :pw]
            gk_ref[:, cols] = total[:, pw : 2 * pw]
            gv_ref[:, cols] = total[:, 2 * pw : 3 * pw]
            go_ref[cols, :] = total[:, 3 * pw :].T

        for r in order[:-1]:
            side_stage(1, r)
        for copy in sn_out:
            copy.wait()
        nsend_ref[1] = nsend_ref[0] + nrecv_ref[0] + nrecv_ref[1] + nrecv_ref[2]
        sx_out.start()
        xf_last[1].start()
        side_stage(1, 0)
        finish(0)
        for r in range(ranks - 2, 0, -2):
            rank_stage(1, r)
        sx_out.wait()
        nsend_ref[2] = nsend_ref[1] + sxrecv_ref[...]
        for r in range(1, ranks):
            sz_out[r].start()
        total = ffn_stage(0)
        full, rest = split_quarter(ff)
        for m, ref in enumerate((fg_ref, fu_ref, fd_ref)):
            ref[:full, :] = total[:, m * full : (m + 1) * full].T
            if rest:
                ref[full:, :] = total[:, 3 * full + m * rest : 3 * full + (m + 1) * rest].T
        total = nsend_ref[2]
        for r in range(1, ranks):
            sz_out[r].wait_recv()
            total = total + szrecv_ref[r - 1]
        small_ref[...] = total
        finish(1)
        for copy in out_out:
            copy.wait()
        for i in range(2):
            for copy in far_out[i][0] + far_out[i][1] + xa_out[i] + za_out[i][1:]:
                copy.wait_send()
        for copy in core_out + xf_out[1:] + xf_last + zf_out[1:] + sz_out[1:]:
            copy.wait_send()


def backward(wide, buckets, ff, ga, x, gain, gain2, fsum, gm, e, ids, out, wo_all, ctx, linv, qkv, w_all, trows=64):
    slots, d = x.shape
    heads = 4
    pw = 2 * HEAD_DIM
    ranks, chunk = wide // 2, d // wide
    packed = fsum.shape[-1]
    width = heads * HEAD_DIM
    small = 3 * buckets + 2 * d // LANES
    vmem, anywhere = pl.BlockSpec(memory_space=pltpu.VMEM), pl.BlockSpec(memory_space=pl.ANY)
    shape = jax.ShapeDtypeStruct
    dma = pltpu.SemaphoreType.DMA

    def slot(u):
        return backward_slot(jnp.minimum(u, 7))

    return pl.pallas_call(
        functools.partial(backward_kernel, wide, heads, buckets, trows, ff),
        grid=(8 + slots // trows,),
        in_specs=[vmem] * 5 + [anywhere] * 6 + [
            pl.BlockSpec((pw, d), lambda u: (slot(u), 0)),
            pl.BlockSpec((slots, pw), lambda u: (0, slot(u))),
            pl.BlockSpec((slots, pw), lambda u: (0, slot(u))),
            pl.BlockSpec((3, slots, pw), lambda u: (0, 0, slot(u))),
            pl.BlockSpec((3, d, pw), lambda u: (0, 0, slot(u))),
        ],
        out_specs=[vmem, anywhere] + [vmem] * 8,
        out_shape=[
            shape((slots, d), F32),
            shape((slots, d), BF),
            shape((small, LANES), F32),
            shape((chunk, width), F32),
            shape((chunk, width), F32),
            shape((chunk, width), F32),
            shape((width, chunk), F32),
            shape((ff, chunk), F32),
            shape((ff, chunk), F32),
            shape((ff, chunk), F32),
        ],
        scratch_shapes=[
            pltpu.VMEM((8, 2, slots, slots), BF),
            pltpu.VMEM((3, slots, slots), I32),
            pltpu.VMEM((d, slots), BF),
            pltpu.VMEM((d, slots), BF),
            pltpu.VMEM((slots, d), F32),
            pltpu.VMEM((3 * buckets * 16, 16 * 16), F32),
            pltpu.VMEM((8, ranks, 2, chunk, 4 * pw), BF),
            pltpu.VMEM((4, ranks, 2, chunk, 4 * pw), BF),
            pltpu.VMEM((2, ranks, 2, chunk, 4 * pw), BF),
            pltpu.VMEM((2, ranks, chunk, 4 * pw), BF),
            pltpu.VMEM((2, ranks - 1, chunk, 4 * pw), BF),
            pltpu.VMEM((ranks, chunk, packed), BF),
            pltpu.VMEM((ranks - 1, chunk, packed), BF),
            pltpu.VMEM((4, small, LANES), F32),
            pltpu.VMEM((3, small, LANES), F32),
            pltpu.VMEM((small, LANES), F32),
            pltpu.VMEM((ranks - 1, small, LANES), F32),
            dma((4,)), dma((2,)), dma((4, 2)), dma((2, 2, ranks, 2)), dma((2, 2)), dma((ranks + 1, 2)), dma((ranks - 1, 2)),
            dma((2, ranks, 2)), dma((2, ranks - 1, 2)), dma((3, 2)), dma((2,)), dma((ranks - 1, 2)),
        ],
        compiler_params=pltpu.CompilerParams(
            vmem_limit_bytes=VMEM_LIMIT, collective_id=3, has_side_effects=True
        ),
        cost_estimate=pl.CostEstimate(flops=30 * slots * d * d, bytes_accessed=60 << 20, transcendentals=0),
        name="backward",
    )(ga, x, gain, gain2, fsum, gm, e, *ids, out, wo_all, ctx, linv, qkv, w_all)


def results_kernel(
    wide, narrow, buckets, heads, middle_ref, out_ref, outin_ref, gi_ref, small_ref, *rest,
):
    sources, (block_ref, go_ref, ga_ref, gf_ref, tr_ref, th_ref, tv_ref), targets = rest[:7], rest[7:14], rest[14:]
    block_ref[...] = (middle_ref[...] + (out_ref[...].astype(F32) + outin_ref[...].astype(F32))).astype(BF)
    go_ref[...] = gi_ref[...]

    @pl.when(pl.program_id(0) == 0)
    def _():
        for a, b in zip(sources, targets):
            b[...] = a[...]
        w, n = lax.axis_index("wide"), lax.axis_index("narrow")
        d = middle_ref.shape[1]
        per, own = d // (wide * narrow), buckets // wide
        start = (w * narrow + n) * per
        for k, ref in enumerate((ga_ref, gf_ref)):
            row = small_ref[pl.ds(3 * buckets + k * (d // LANES) + start // LANES, 1), :]
            lane = lax.broadcasted_iota(I32, (per, LANES), 1)
            mine = lane == lax.broadcasted_iota(I32, (per, LANES), 0) + start % LANES
            ref[...] = jnp.sum(jnp.where(mine, jnp.broadcast_to(row, (per, LANES)), 0.0), axis=1)
        for k, ref in enumerate((tr_ref, th_ref, tv_ref)):
            ref[...] = small_ref[pl.ds(k * buckets + w * own, own), :heads]


def results(wide, narrow, buckets, heads, middle, out, outin, small, grad_input, big):
    slots, d = middle.shape
    shape = jax.ShapeDtypeStruct
    per, own = d // (wide * narrow), buckets // wide
    rows = pl.BlockSpec((slots // 4, d), lambda i: (i, 0))
    whole = lambda *sh: pl.BlockSpec(sh, lambda i: (0,) * len(sh))
    return pl.pallas_call(
        functools.partial(results_kernel, wide, narrow, buckets, heads),
        grid=(4,),
        in_specs=[rows] * 4 + [whole(*small.shape)] + [whole(*x.shape) for x in big],
        out_specs=[rows] * 2 + [whole(per)] * 2 + [whole(own, heads)] * 3 + [whole(*x.shape) for x in big],
        out_shape=[shape((slots, d), BF), shape((slots, d), F32)] + [shape((per,), F32)] * 2
        + [shape((own, heads), F32)] * 3 + [shape(x.shape, x.dtype) for x in big],
        compiler_params=pltpu.CompilerParams(vmem_limit_bytes=VMEM_LIMIT),
        name="results",
    )(middle, out, outin, grad_input, small, *big)


def shards(
    wide, narrow, hidden_in, grad_out, gain_attn, gain_ffn, w_query, w_key, w_value, w_output,
    table_rel, table_horiz, table_vert, wi_gate, wi_up, wo_ffn, counts, patch_mask,
    bucket_rel, bucket_horiz, bucket_vert,
):
    slots = bucket_rel.shape[1]
    rows, d = hidden_in.shape
    buckets, heads = table_rel.shape
    width = w_query.shape[1]
    ff = wi_gate.shape[1]
    assert rows == slots and narrow == 4 and wide >= 4 and heads * HEAD_DIM == width
    ids = (bucket_rel, bucket_horiz, bucket_vert)

    qkv, exps, context, linv, w_all, wo_all, middle, ffn_own, grad_far, wg_core, wu_core, wd_core = forward(
        counts, patch_mask, hidden_in, gain_attn, gain_ffn, (table_rel.T, table_horiz.T, table_vert.T),
        w_query, w_key, w_value, w_output, ids, grad_out, wi_gate.T, wi_up.T, wo_ffn,
    )
    out, ffn_sum, grad_middle, grad_attn, grad_gain_second = feed_forward(
        ffn_own, grad_out, grad_far, middle, gain_ffn,
        (wi_gate.T, wi_up.T, wo_ffn), (wg_core, wu_core, wd_core),
    )
    grad_input, out_in, small, gq, gk, gv, go, fg, fu, fd = backward(
        wide, buckets, ff, grad_attn, hidden_in, gain_attn, grad_gain_second,
        ffn_sum.reshape(wide // 2, 2, d // wide, -1), grad_middle, exps, ids, out,
        wo_all, context, linv, qkv, w_all,
    )
    block_out, grad_input, gain1, gain2, rel, horiz, vert, gq, gk, gv, go, fg, fu, fd = results(
        wide, narrow, buckets, heads, middle, out, out_in, small, grad_input, (gq, gk, gv, go, fg, fu, fd)
    )
    return (
        block_out, grad_input, gain1, gain2, gq, gk, gv, go, rel, horiz, vert, fg.T, fu.T, fd,
    )


def solution(mesh):
    rows, both = P(("wide", "narrow"), None), P(("wide", "narrow"))
    cols, across = P(None, "narrow"), P("narrow", None)
    grid, turned = P("wide", "narrow"), P("narrow", "wide")
    pages = P("wide", None, None)
    return jax.shard_map(
        functools.partial(shards, mesh.shape["wide"], mesh.shape["narrow"]),
        mesh=mesh,
        in_specs=(
            rows, rows, P(), P(), cols, cols, cols, across, cols, cols, cols, cols, cols, across,
            P("wide"), P("wide", None), pages, pages, pages,
        ),
        out_specs=(
            rows, rows, both, both, grid, grid, grid, turned, grid, grid, grid, grid, grid, turned,
        ),
        check_vma=False,
    )
```

```python
import functools
import math

import jax
import jax.numpy as jnp
from jax import lax
from jax.experimental import pallas as pl
from jax.experimental.pallas import tpu as pltpu
from jax.sharding import PartitionSpec as P

F32 = jnp.float32
BF = jnp.bfloat16
I32 = jnp.int32
HEAD_DIM = 64
LANES = 128
EPS = 1e-06
NT = (((1,), (1,)), ((), ()))

FIXED = 2048.0
OFFSET = 8192
MASKED = -3.0e12
VMEM_LIMIT = 60 << 20
MESH = pl.DeviceIdType.MESH


def lookup(table_row, ids):
    return jnp.take_along_axis(table_row, ids, axis=1, mode="promise_in_bounds")


def neighbours():
    w, n = lax.axis_index("wide"), lax.axis_index("narrow")
    return w, n, (w, n ^ 1), (w, n ^ 2), (w, n ^ 3), (w ^ 1, n)


def greet(devices):
    barrier = pltpu.get_barrier_semaphore()
    for device in devices:
        pl.semaphore_signal(barrier, inc=1, device_id=device, device_id_type=MESH)
    pl.semaphore_wait(barrier, len(devices))


def remote(src, dst, sems, device):
    return pltpu.make_async_remote_copy(
        src_ref=src, dst_ref=dst, send_sem=sems.at[0], recv_sem=sems.at[1], device_id=device, device_id_type=MESH
    )


def forward_kernel(
    heads, buckets, chunk,
    counts_ref, patch_ref, x_ref, gain1_ref, gain2_ref, tr_ref, th_ref, tv_ref,
    wq_ref, wk_ref, wv_ref, wo_ref, ir_ref, ih_ref, iv_ref, go_ref, wg_ref, wu_ref, wd_ref,
    qkv_to, e_ref, ctx_to, linv_to, wall_to, woall_to, middle_ref, ffn_ref, gofar_ref, wgc_ref, wuc_ref, wdc_ref,
    qkv_ref, ctx_ref, linv_ref, wall_ref, woall_ref, normed_ref, mask_ref, ids_ref, tab_ref, tabs_ref, words_ref, ebuf_ref,
    own_sem, id_sem, e_sem, core_sem, far_sem, deep_sem, wide_sem, fwd_sem, tab_sem, big_sem, leave_sem,
):
    pw = 2 * HEAD_DIM
    slots, d = x_ref.shape
    piece = d // 2
    w, n, core, far, diag, side = neighbours()
    deep = (w ^ 2, n)
    half, share = w & 1, (w >> 1) & 1
    other = 1 - half

    def source(m, pair, part=None):
        cols = pl.ds(pl.multiple_of(pair * pw, pw), pw)
        span = slice(None) if part is None else pl.ds(pl.multiple_of(part * piece, piece), piece)
        return wo_ref.at[cols, span] if m == 3 else (wq_ref, wk_ref, wv_ref)[m].at[span, cols]

    def place(m, slot, part=None):
        cols = pl.ds(pl.multiple_of(slot * pw, pw), pw)
        span = slice(None) if part is None else pl.ds(pl.multiple_of(part * piece, piece), piece)
        return woall_ref.at[cols, span] if m == 3 else wall_ref.at[m, span, cols]

    ids_in = [pltpu.make_async_copy(r.at[n], ids_ref.at[t], id_sem.at[t]) for t, r in enumerate((ir_ref, ih_ref, iv_ref))]
    own_in = [[pltpu.make_async_copy(source(m, p), place(m, p), own_sem.at[p, m]) for m in range(4)] for p in range(2)]
    for copy in own_in[0][:3] + ids_in + own_in[0][3:] + own_in[1]:
        copy.start()

    tab_ref[...] = jnp.zeros_like(tab_ref)
    for t, r in enumerate((tr_ref, th_ref, tv_ref)):
        tab_ref[t * heads : (t + 1) * heads, :buckets] = jnp.floor(r[...].astype(F32) * FIXED + 0.5)

    greet((core, far, diag, side, deep))
    far_out = [remote(source(m, half, share), place(m, 4 + half, share), far_sem.at[m], far) for m in range(4)]
    deep_out = [remote(place(m, 4 + half, share), place(m, 4 + half, share), deep_sem.at[m], deep) for m in range(4)]
    core_out = [[remote(source(m, p), place(m, 2 + p), core_sem.at[p, m], core) for m in range(4)] for p in range(2)]
    tabs_out = [remote(tab_ref, tabs_ref.at[r - 1], tab_sem.at[r - 1], dev) for r, dev in ((1, core), (2, far), (3, diag))]
    wide_out = [
        [remote(place(m, 4 + half, k), place(m, 4 + half, k), wide_sem.at[m, i], side) for i, k in enumerate((share, 1 - share))]
        for m in range(4)
    ]
    fwd_out = [
        [remote(place(m, 4 + half, k), place(m, 6 + half, k), fwd_sem.at[m, i], core) for i, k in enumerate((share, 1 - share))]
        for m in range(4)
    ]
    last_out = [remote(place(m, 4 + other), place(m, 6 + other), fwd_sem.at[m, 2], core) for m in range(4)]
    go_out = remote(go_ref, gofar_ref, big_sem.at[0], far)
    ffn_out = [
        remote(wg_ref, wgc_ref, big_sem.at[1], core),
        remote(wu_ref, wuc_ref, big_sem.at[2], core),
        remote(wd_ref, wdc_ref, big_sem.at[3], core),
    ]
    for copy in tabs_out + far_out + [go_out] + core_out[0] + core_out[1]:
        copy.start()

    x = x_ref[...].astype(F32)
    inv = lax.rsqrt(jnp.mean(x * x, axis=-1, keepdims=True) + EPS)
    normed_ref[...] = (x * inv * gain1_ref[...].astype(F32)[None]).astype(BF)
    text = slots - patch_ref.shape[1]
    shown = jnp.concatenate(
        [
            jnp.where(lax.broadcasted_iota(I32, (1, text), 1) < counts_ref[n], 1, 0),
            patch_ref[pl.ds(n, 1), :],
        ],
        axis=1,
    )
    column = jnp.broadcast_to(jnp.where(shown == 1, 0.0, MASKED), (pw, slots)).T
    lane_all = lax.broadcasted_iota(I32, (slots, pw), 1)
    mask_ref[...] = jnp.where(lane_all == 0, column, 0.0).astype(BF)
    ones = jnp.ones((slots, pw), BF)
    lane = lax.broadcasted_iota(I32, (chunk, pw), 1)
    low = lane < HEAD_DIM
    first = jnp.where(lane == 0, 1.0, 0.0).astype(BF)
    to_log2 = math.log2(math.e) / FIXED

    def pack_words(r, table):
        fixed = table.astype(I32)
        for p in range(2):
            for t in range(3):
                row = t * heads + 2 * p
                words_ref[2 * r + p, t : t + 1, :] = fixed[row + 1 : row + 2] * 65536 + fixed[row : row + 1] + OFFSET

    pack_words(0, tab_ref[...])
    for copy in ids_in:
        copy.wait()

    def e_out(parity, slot):
        return pltpu.make_async_copy(ebuf_ref.at[parity], e_ref.at[slot], e_sem.at[parity])

    def leaving(slot):
        cols = pl.ds(pl.multiple_of(slot * pw, pw), pw)
        pairs = (
            (wall_ref.at[:, :, cols], wall_to.at[:, :, cols]),
            (qkv_ref.at[:, :, cols], qkv_to.at[:, :, cols]),
            (ctx_ref.at[:, cols], ctx_to.at[:, cols]),
            (linv_ref.at[:, cols], linv_to.at[:, cols]),
        )
        return [pltpu.make_async_copy(a, b, leave_sem.at[k, slot]) for k, (a, b) in enumerate(pairs)]

    def slot_of(t):
        late = 4 + 2 * (t & 1) + jnp.where(t >= 6, other, half)
        return jnp.where(t < 4, t, late)

    plan = [[] for _ in range(16)]

    def far_arrived(m):
        far_out[m].wait_recv()
        deep_out[m].start()
        wide_out[m][0].start()
        fwd_out[m][0].start()

    def deep_arrived(m):
        deep_out[m].wait_recv()
        wide_out[m][1].start()
        fwd_out[m][1].start()

    def wide_arrived(m):
        for copy in wide_out[m]:
            copy.wait_recv()
        last_out[m].start()

    def tables_arrived():
        for r, copy in enumerate(tabs_out):
            copy.wait()
            pack_words(r + 1, tabs_ref[r])

    for p in range(2):
        plan[2 * p].extend(own_in[p][m].wait for m in range(3))
        plan[4 + 2 * p].extend(core_out[p][m].wait_recv for m in range(3))
    plan[3].append(tables_arrived)
    for m in range(4):
        plan[2 + m].append(functools.partial(far_arrived, m))
        plan[4 + m].append(functools.partial(deep_arrived, m))
    plan[7].extend(copy.start for copy in ffn_out)
    plan[10].extend(copy.wait_recv for m in range(3) for copy in fwd_out[m])
    plan[12].extend(functools.partial(wide_arrived, m) for m in range(3))
    plan[14].extend(last_out[m].wait_recv for m in range(3))
    plan[14].append(functools.partial(wide_arrived, 3))

    def events(t, c):
        for k in range(8):
            if plan[2 * k + c]:

                @pl.when(t == k)
                def _():
                    for action in plan[2 * k + c]:
                        action()

    def step(t, carry):
        slot = slot_of(t)
        events(t, 0)
        parity = t & 1

        @pl.when(t >= 2)
        def _():
            e_out(parity, slot).wait()

        cols = pl.ds(pl.multiple_of(slot * pw, pw), pw)
        weights = jnp.concatenate([wall_ref[m, :, cols] for m in range(3)], axis=1)
        joined = jnp.dot(normed_ref[...], weights, preferred_element_type=F32).astype(BF)
        for m in range(3):
            qkv_ref[m, :, cols] = joined[:, m * pw : (m + 1) * pw]
        kx = jnp.concatenate([joined[:, pw : 2 * pw], mask_ref[...]], axis=1)
        vx = jnp.concatenate([joined[:, 2 * pw :], ones], axis=1)
        words = words_ref[slot]
        for c in range(slots // chunk):
            if c == slots // chunk // 2:
                events(t, 1)
            rows = slice(c * chunk, (c + 1) * chunk)
            q2 = joined[rows, :pw] * jnp.bfloat16(FIXED)
            zero = jnp.zeros_like(q2)
            scores = []
            for sub in range(2):
                q = jnp.where(low, q2, zero) if sub == 0 else jnp.where(low, zero, q2)
                q = jnp.concatenate([q, first], axis=1)
                scores.append(lax.dot_general(q, kx, NT, preferred_element_type=F32))
            tabs = [jnp.broadcast_to(words[k : k + 1, :], (chunk, LANES)) for k in range(3)]
            parts = ([], [])
            for j in range(slots // LANES):
                sl = slice(j * LANES, (j + 1) * LANES)
                bias = (
                    lookup(tabs[0], ids_ref[0, rows, sl])
                    + lookup(tabs[1], ids_ref[1, rows, sl])
                    + lookup(tabs[2], ids_ref[2, rows, sl])
                )
                parts[0].append(scores[0][:, sl] + (bias & 0xFFFF).astype(F32))
                parts[1].append(scores[1][:, sl] + (bias >> 16).astype(F32))
            outs = []
            for sub in range(2):
                s = jnp.concatenate(parts[sub], axis=1)
                peak = jnp.max(s, axis=1, keepdims=True)
                e = jnp.exp2((s - peak) * to_log2).astype(BF)
                ebuf_ref[parity, sub, rows, :] = e
                outs.append(jnp.dot(e, vx, preferred_element_type=F32))
            linv = 1.0 / jnp.where(low, outs[0][:, pw:], outs[1][:, pw:])
            linv_ref[rows, cols] = linv
            ctx_ref[rows, cols] = (jnp.where(low, outs[0][:, :pw], outs[1][:, :pw]) * linv).astype(BF)
        e_out(parity, slot).start()
        for copy in leaving(slot):
            copy.start()
        return carry

    lax.fori_loop(0, 8, step, 0)
    for p in range(2):
        own_in[p][3].wait()
        core_out[p][3].wait_recv()
    for copy in fwd_out[3] + last_out[3:]:
        copy.wait_recv()
    wo_leaving = pltpu.make_async_copy(woall_ref, woall_to, id_sem.at[0])
    wo_leaving.start()
    middle = x_ref[...].astype(F32) + jnp.dot(ctx_ref[...], woall_ref[...], preferred_element_type=F32)
    middle_ref[...] = middle
    inv = lax.rsqrt(jnp.mean(middle * middle, axis=-1, keepdims=True) + EPS)
    ffn_ref[...] = (middle * inv * gain2_ref[...].astype(F32)[None]).astype(BF)
    for p in range(2):
        e_out(p, p).wait()
        for m in range(4):
            core_out[p][m].wait_send()
    for m in range(4):
        for copy in [far_out[m], deep_out[m], last_out[m]] + wide_out[m] + fwd_out[m]:
            copy.wait_send()
    for copy in ffn_out:
        copy.wait()
    for slot in range(8):
        for copy in leaving(slot):
            copy.wait()
    wo_leaving.wait()
    go_out.wait()


def forward(counts, patches, x, gain1, gain2, tables, wq, wk, wv, wo, ids, grad_out, wg, wu, wd, chunk=256):
    slots, d = x.shape
    heads = wq.shape[1] // HEAD_DIM
    buckets = tables[0].shape[1]
    ff = wd.shape[0]
    assert heads == 4
    vmem, anywhere = pl.BlockSpec(memory_space=pltpu.VMEM), pl.BlockSpec(memory_space=pl.ANY)
    shape = jax.ShapeDtypeStruct
    dma = pltpu.SemaphoreType.DMA
    return pl.pallas_call(
        functools.partial(forward_kernel, heads, buckets, chunk),
        in_specs=[pl.BlockSpec(memory_space=pltpu.SMEM)] + [vmem] * 7 + [anywhere] * 11,
        out_specs=[anywhere] * 6 + [vmem] * 2 + [anywhere] * 4,
        out_shape=[
            shape((3, slots, d), BF),
            shape((8, 2, slots, slots), BF),
            shape((slots, d), BF),
            shape((slots, d), F32),
            shape((3, d, d), BF),
            shape((d, d), BF),
            shape((slots, d), F32),
            shape((slots, d), BF),
            shape((slots, d), BF),
            shape((ff, d), BF),
            shape((ff, d), BF),
            shape((ff, d), BF),
        ],
        scratch_shapes=[
            pltpu.VMEM((3, slots, d), BF),
            pltpu.VMEM((slots, d), BF),
            pltpu.VMEM((slots, d), F32),
            pltpu.VMEM((3, d, d), BF),
            pltpu.VMEM((d, d), BF),
            pltpu.VMEM((slots, d), BF),
            pltpu.VMEM((slots, 2 * HEAD_DIM), BF),
            pltpu.VMEM((3, slots, slots), I32),
            pltpu.VMEM((16, LANES), F32),
            pltpu.VMEM((3, 16, LANES), F32),
            pltpu.VMEM((8, 8, LANES), I32),
            pltpu.VMEM((2, 2, slots, slots), BF),
            dma((2, 4)), dma((3,)), dma((2,)), dma((2, 4, 2)), dma((4, 2)), dma((4, 2)), dma((4, 2, 2)), dma((4, 3, 2)),
            dma((3, 2)), dma((4, 2)), dma((4, 8)),
        ],
        compiler_params=pltpu.CompilerParams(
            vmem_limit_bytes=VMEM_LIMIT, collective_id=1, has_side_effects=True
        ),
        cost_estimate=pl.CostEstimate(flops=20 * slots * d * d, bytes_accessed=40 << 20, transcendentals=16 * slots * slots),
        name="forward",
    )(counts, patches, x, gain1, gain2, *tables, wq, wk, wv, wo, *ids, grad_out, wg, wu, wd)


def gelu_parts(v):
    c, k = math.sqrt(2.0 / math.pi), 0.044715
    square = v * v
    t = jnp.tanh(c * v * (1.0 + k * square))
    up = 0.5 * (1.0 + t)
    slope = up + 0.5 * v * (1.0 - t * t) * (c * (1.0 + 3.0 * k * square))
    return v * up, slope


def split_quarter(ff):
    return ff // LANES * LANES, ff % LANES


def packed_width(ff):
    full, rest = split_quarter(ff)
    return 3 * full + -(-3 * rest // LANES) * LANES


def ffn_kernel(
    block, ff,
    x_ref, go_ref, gofar_ref, middle_ref, gain_ref, w0_ref, w1_ref, w2_ref, c0_ref, c1_ref, c2_ref,
    out_to, sum_to, gm_to, ga_to, gain_out_ref,
    out_ref, sum_ref, gm_ref, ga_ref, xall_ref, gall_ref, wgu_ref, wd_ref, xt_ref, gt_ref, act_ref, send_ref, recv_ref, own_ref, backfar_ref, backin_ref,
    in_sem, w_sem, x_sem, back_sem, dw_sem, leave_sem, end_sem,
):
    slots, d = middle_ref.shape
    halves = slots // block
    full, rest = split_quarter(ff)
    both = 2 * ff
    _, _, core, far, _, _ = neighbours()

    ins = [
        pltpu.make_async_copy(x_ref, xall_ref.at[pl.ds(0, slots), :], in_sem.at[0]),
        pltpu.make_async_copy(go_ref, gall_ref.at[pl.ds(0, slots), :], in_sem.at[1]),
        pltpu.make_async_copy(gofar_ref, gall_ref.at[pl.ds(slots, slots), :], in_sem.at[2]),
    ]
    weights = []
    for m, pair in enumerate(((w0_ref, c0_ref), (w1_ref, c1_ref), (w2_ref, c2_ref))):
        target, base = (wd_ref, 0) if m == 2 else (wgu_ref, m * both)
        for q, r in enumerate(pair):
            for k, (start, size, at) in enumerate(((0, full, q * full), (full, rest, 2 * full + q * rest))):
                if size:
                    weights.append(
                        pltpu.make_async_copy(
                            r.at[pl.ds(start, size), :], target.at[pl.ds(base + at, size), :], w_sem.at[m, q, k]
                        )
                    )
    for copy in ins[:2] + weights + ins[2:]:
        copy.start()
    greet((core, far))
    x_out = [
        remote(x_ref.at[pl.ds(i * block, block), :], xall_ref.at[pl.ds(slots + i * block, block), :], x_sem.at[i], far)
        for i in range(halves)
    ]
    for copy in x_out:
        copy.start()
    back_out = [
        remote(backfar_ref.at[pl.ds(i * block, block), :], backin_ref.at[pl.ds(i * block, block), :], back_sem.at[i], far)
        for i in range(halves)
    ]
    for copy in ins + weights:
        copy.wait()

    def step(b, carry):
        for i in range(halves):

            @pl.when(b == halves + i)
            def _():
                x_out[i].wait_recv()

        rows = pl.ds(pl.multiple_of(b * block, block), block)
        x, g = xall_ref[rows, :], gall_ref[rows, :]
        xt_ref[:, rows] = x.T
        gt_ref[:, rows] = g.T
        grown = lax.dot_general(x, wgu_ref[...], NT, preferred_element_type=F32)
        grad_hidden = lax.dot_general(g, wd_ref[...], NT, preferred_element_type=F32)
        gate, upper = grown[:, :both], grown[:, both:]
        gelu, slope = gelu_parts(gate)
        dg = (grad_hidden * upper * slope).astype(BF)
        du = (grad_hidden * gelu).astype(BF)
        hidden = (gelu * upper).astype(BF)
        act_ref[0, rows, :] = dg
        act_ref[1, rows, :] = du
        act_ref[2, rows, :] = hidden
        back = jnp.dot(jnp.concatenate([dg, du], axis=1), wgu_ref[...], preferred_element_type=F32)

        @pl.when(b < halves)
        def _():
            own_ref[rows, :] = back

        for i in range(halves):

            @pl.when(b == halves + i)
            def _():
                backfar_ref[i * block : (i + 1) * block, :] = back.astype(BF)
                back_out[i].start()

        out_ref[rows, :] = jnp.dot(hidden, wd_ref[...], preferred_element_type=F32).astype(BF)
        pltpu.make_async_copy(out_ref.at[rows, :], out_to.at[rows, :], leave_sem.at[b]).start()
        return carry

    lax.fori_loop(0, 2 * halves, step, 0)

    tile = d // 2
    used = 3 * (full + rest)
    dw_out = [
        remote(send_ref.at[pl.ds(c * tile, tile), :], recv_ref.at[pl.ds(c * tile, tile), :], dw_sem.at[c], core)
        for c in range(2)
    ]
    for c in range(2):
        rows = slice(c * tile, (c + 1) * tile)
        for m in range(3):
            left = gt_ref if m == 2 else xt_ref
            dw = jnp.dot(left[rows, :], act_ref[m], preferred_element_type=F32).astype(BF)
            for q, target in enumerate((sum_ref, send_ref)):
                target[rows, m * full : (m + 1) * full] = dw[:, q * full : (q + 1) * full]
                if rest:
                    at = 2 * full + q * rest
                    target[rows, 3 * full + m * rest : 3 * full + (m + 1) * rest] = dw[:, at : at + rest]
        for target in (sum_ref, send_ref):
            if used < target.shape[1]:
                target[rows, used:] = jnp.zeros((tile, target.shape[1] - used), BF)
        dw_out[c].start()
    leaving = []
    for c in range(2):
        rows = slice(c * tile, (c + 1) * tile)
        dw_out[c].wait_recv()
        sum_ref[rows, :] = (sum_ref[rows, :].astype(F32) + recv_ref[rows, :].astype(F32)).astype(BF)
        at = pl.ds(c * tile, tile)
        leaving.append(pltpu.make_async_copy(sum_ref.at[at, :], sum_to.at[at, :], end_sem.at[c]))
        leaving[-1].start()

    gains = 0.0
    for i in range(halves):
        rows, at = slice(i * block, (i + 1) * block), pl.ds(i * block, block)
        back_out[i].wait_recv()
        middle = middle_ref[rows, :]
        inv = lax.rsqrt(jnp.mean(middle * middle, axis=-1, keepdims=True) + EPS)
        upstream = own_ref[rows, :] + backin_ref[rows, :].astype(F32)
        lifted = upstream * gain_ref[...].astype(F32)[None]
        inner = jnp.mean(lifted * middle, axis=-1, keepdims=True)
        gains = gains + jnp.sum(upstream * middle * inv, axis=0, keepdims=True)
        gm = gall_ref[rows, :].astype(F32) + inv * lifted - middle * (inv * inv * inv * inner)
        gm_ref[rows, :] = gm
        ga_ref[rows, :] = gm.astype(BF)
        for k, (a, b) in enumerate(((gm_ref, gm_to), (ga_ref, ga_to))):
            leaving.append(pltpu.make_async_copy(a.at[at, :], b.at[at, :], end_sem.at[2 + 2 * i + k]))
            leaving[-1].start()
    gain_out_ref[...] = gains
    for copy in x_out + back_out + dw_out:
        copy.wait_send()
    for b in range(2 * halves):
        at = pl.ds(b * block, block)
        pltpu.make_async_copy(out_ref.at[at, :], out_to.at[at, :], leave_sem.at[b]).wait()
    for copy in leaving:
        copy.wait()


def feed_forward(x, go, gofar, middle, gain, own, other, block=256):
    slots, d = x.shape
    ff = own[0].shape[0]
    vmem, anywhere = pl.BlockSpec(memory_space=pltpu.VMEM), pl.BlockSpec(memory_space=pl.ANY)
    shape = jax.ShapeDtypeStruct
    dma = pltpu.SemaphoreType.DMA
    halves = slots // block
    packed = packed_width(ff)
    return pl.pallas_call(
        functools.partial(ffn_kernel, block, ff),
        in_specs=[anywhere] * 3 + [vmem] * 2 + [anywhere] * 6,
        out_specs=[anywhere] * 4 + [vmem],
        out_shape=[
            shape((2 * slots, d), BF),
            shape((d, packed), BF),
            shape((slots, d), F32),
            shape((slots, d), BF),
            shape((1, d), F32),
        ],
        scratch_shapes=[
            pltpu.VMEM((2 * slots, d), BF),
            pltpu.VMEM((d, packed), BF),
            pltpu.VMEM((slots, d), F32),
            pltpu.VMEM((slots, d), BF),
            pltpu.VMEM((2 * slots, d), BF),
            pltpu.VMEM((2 * slots, d), BF),
            pltpu.VMEM((4 * ff, d), BF),
            pltpu.VMEM((2 * ff, d), BF),
            pltpu.VMEM((d, 2 * slots), BF),
            pltpu.VMEM((d, 2 * slots), BF),
            pltpu.VMEM((3, 2 * slots, 2 * ff), BF),
            pltpu.VMEM((d, packed), BF),
            pltpu.VMEM((d, packed), BF),
            pltpu.VMEM((slots, d), F32),
            pltpu.VMEM((slots, d), BF),
            pltpu.VMEM((slots, d), BF),
            dma((3,)), dma((3, 2, 2)), dma((halves, 2)), dma((halves, 2)), dma((2, 2)),
            dma((2 * halves,)), dma((2 + 2 * halves,)),
        ],
        compiler_params=pltpu.CompilerParams(
            vmem_limit_bytes=VMEM_LIMIT, collective_id=2, has_side_effects=True
        ),
        cost_estimate=pl.CostEstimate(flops=36 * slots * d * ff, bytes_accessed=40 << 20, transcendentals=4 * slots * ff),
        name="feed_forward",
    )(x, go, gofar, middle, gain, *own, *other)


def backward_slot(k):
    return jnp.where(k < 4, 6 - 2 * (k & 1) + (k >> 1), 6 - 2 * (k >> 1) + (k & 1))


def backward_kernel(
    wide, heads, buckets, trows, ff,
    ga_ref, x_ref, gain_ref, gain2_ref, fsum_ref, gm_ref, e_ref, ir_ref, ih_ref, iv_ref, out_ref,
    wo_ref, ctx_ref, linv_ref, qkv_ref, wall_ref,
    gi_ref, outin_ref, small_ref, gq_ref, gk_ref, gv_ref, go_ref, fg_ref, fu_ref, fd_ref,
    gib_ref, fown_ref, ds_ref, ids_ref, nt_ref, gat_ref, dx_ref, acc_ref, part_ref, crecv_ref, frecv_ref, xarecv_ref, zarecv_ref,
    xfrecv_ref, zfrecv_ref, nsend_ref, nrecv_ref, sxrecv_ref, szrecv_ref,
    in_sem, e_sem, core_sem, far_sem, out_sem, xf_sem, zf_sem, xa_sem, za_sem, sn_sem, sx_sem, sz_sem,
):
    pw = 2 * HEAD_DIM
    slots, d = ga_ref.shape
    half_rows = slots // 2
    ranks = wide // 2
    chunk = d // wide
    steps = 8 + slots // trows
    u = pl.program_id(0)
    w, n, core, far, diag, side = neighbours()
    par, rank = w & 1, w >> 1
    opp = 1 - par
    peer = lambda r: (2 * (rank ^ r) + par, n)
    slot_of = backward_slot
    slot = slot_of(jnp.minimum(u, 7))

    ins = [pltpu.make_async_copy(r.at[n], ids_ref.at[t], in_sem.at[t]) for t, r in enumerate((ir_ref, ih_ref, iv_ref))]
    gm_in = pltpu.make_async_copy(gm_ref, gib_ref, in_sem.at[3])
    fown_in = pltpu.make_async_copy(fsum_ref.at[:, par], fown_ref, in_sem.at[4])
    gi_out = pltpu.make_async_copy(gib_ref, gi_ref, in_sem.at[5])
    core_out = [remote(part_ref.at[s], crecv_ref.at[i], core_sem.at[i], core) for i, s in enumerate((6, 7, 2, 3))]
    order = list(range(ranks - 1, 0, -2)) + list(range(ranks - 2, -1, -2))
    far_out = [
        [
            [
                remote(part_ref.at[4 + i, rank ^ r, p], frecv_ref.at[i, rank ^ r, p], far_sem.at[i, k, r], far)
                for r in range(ranks)
            ]
            for k, p in enumerate((opp, par))
        ]
        for i in range(2)
    ]
    out_out = [
        remote(
            out_ref.at[pl.ds(slots + i * half_rows, half_rows), :],
            outin_ref.at[pl.ds(i * half_rows, half_rows), :], out_sem.at[i], far,
        )
        for i in range(2)
    ]
    xf_out = [None] + [remote(fsum_ref.at[rank ^ r, opp], xfrecv_ref.at[r], xf_sem.at[r], side) for r in range(1, ranks)]
    some = chunk // 2
    xf_last = [
        remote(
            fsum_ref.at[rank, opp, pl.ds(k * some, some), :], xfrecv_ref.at[0, pl.ds(k * some, some), :],
            xf_sem.at[k * ranks], side,
        )
        for k in range(2)
    ]
    low_bit = lambda r: r & -r
    zf_out = [None] + [
        remote(xfrecv_ref.at[r], zfrecv_ref.at[r - 1], zf_sem.at[r - 1], peer(low_bit(r))) for r in range(1, ranks)
    ]
    feeds = lambda r: [r | (1 << b) for b in range(ranks.bit_length() - 1) if (1 << b) < (low_bit(r) if r else ranks)]
    xa_out = [
        [remote(part_ref.at[i, rank ^ r, opp], xarecv_ref.at[i, r], xa_sem.at[i, r], side) for r in range(ranks)]
        for i in range(2)
    ]
    za_out = [
        [None]
        + [
            remote(part_ref.at[i, rank ^ r, par], zarecv_ref.at[i, r - 1], za_sem.at[i, r - 1], peer(low_bit(r)))
            for r in range(1, ranks)
        ]
        for i in range(2)
    ]
    sn_out = [
        remote(nsend_ref.at[r], nrecv_ref.at[r - 1], sn_sem.at[r - 1], dev) for r, dev in ((1, core), (2, far), (3, diag))
    ]
    sx_out = remote(nsend_ref.at[1], sxrecv_ref, sx_sem, side)
    sz_out = [None] + [remote(nsend_ref.at[2], szrecv_ref.at[r - 1], sz_sem.at[r - 1], peer(r)) for r in range(1, ranks)]

    def at_edge(end, middle):
        edge = ((rank ^ (rank >> 1)) & 1) == 0
        pl.when(edge)(lambda: end())
        pl.when(jnp.logical_not(edge))(lambda: middle())

    def e_in(k):
        s = slot_of(k)
        return pltpu.make_async_copy(e_ref.at[s], ds_ref.at[s], e_sem.at[k & 1])

    def wide_f32(ref_value):
        return ref_value.astype(F32)

    @pl.when(u == 0)
    def _():
        e_in(0).start()
        for copy in [fown_in] + ins + [gm_in]:
            copy.start()
        greet([core, far, diag, side] + [peer(r) for r in range(1, ranks)])
        if ranks == 4:
            xf_out[3].start()
            at_edge(xf_out[1].start, xf_out[2].start)
            at_edge(xf_out[2].start, xf_out[1].start)
        else:
            for r in range(ranks - 1, 0, -1):
                xf_out[r].start()
        out_out[0].start()
        x = x_ref[...].astype(F32)
        inv = lax.rsqrt(jnp.mean(x * x, axis=-1, keepdims=True) + EPS)
        nt_ref[...] = (x * inv * gain_ref[...].astype(F32)[None]).astype(BF).T
        gat_ref[...] = ga_ref[...].T
        dx_ref[...] = jnp.zeros_like(dx_ref)
        acc_ref[...] = jnp.zeros_like(acc_ref)

    @pl.when(u < 8)
    def _():
        e_in(u).wait()

        @pl.when(u < 7)
        def _():
            e_in(u + 1).start()

        lane = lax.broadcasted_iota(I32, (slots, pw), 1)
        low = lane < HEAD_DIM
        do2 = (lax.dot_general(ga_ref[...], wo_ref[...], NT, preferred_element_type=F32) * linv_ref[...]).astype(BF)
        prod = do2.astype(F32) * ctx_ref[...].astype(F32)
        q2, k2, v2 = qkv_ref[0], qkv_ref[1], qkv_ref[2]
        vx = jnp.concatenate([v2, jnp.where(lane < 2, 1.0, 0.0).astype(BF)], axis=1)
        do_t, q_t = do2.T, q2.T
        zero = jnp.zeros_like(do2)
        dq, dk, dv = [], [], []
        for sub in range(2):
            mine = low if sub == 0 else jnp.logical_not(low)
            row = -jnp.sum(jnp.where(mine, prod, 0.0), axis=1, keepdims=True)
            head_part = row.astype(BF).astype(F32)
            extra = jnp.where(lane == 0, head_part, jnp.where(lane == 1, row - head_part, 0.0)).astype(BF)
            dox = jnp.concatenate([jnp.where(mine, do2, zero), extra], axis=1)
            t = lax.dot_general(dox, vx, NT, preferred_element_type=F32)
            e = ds_ref[slot, sub]
            ds = (e.astype(F32) * t).astype(BF)
            dv.append(jnp.dot(do_t[sub * HEAD_DIM : (sub + 1) * HEAD_DIM], e, preferred_element_type=F32))
            ds_ref[slot, sub] = ds
            dk.append(jnp.dot(q_t[sub * HEAD_DIM : (sub + 1) * HEAD_DIM], ds, preferred_element_type=F32))
            dq.append(jnp.dot(ds, k2, preferred_element_type=F32))
        joined = jnp.concatenate(
            [
                jnp.where(low, dq[0], dq[1]).astype(BF),
                jnp.concatenate(dk, axis=0).T.astype(BF),
                jnp.concatenate(dv, axis=0).T.astype(BF),
            ],
            axis=1,
        )
        weights = jnp.concatenate([wall_ref[m] for m in range(3)], axis=1)
        dx_ref[...] += lax.dot_general(joined, weights, NT, preferred_element_type=F32)
        part = jnp.dot(nt_ref[...], joined, preferred_element_type=F32).astype(BF)
        part_ref[slot, :, :, :, : 3 * pw] = part.reshape(ranks, 2, chunk, 3 * pw)
        part = jnp.dot(gat_ref[...], ctx_ref[...], preferred_element_type=F32).astype(BF)
        part_ref[slot, :, :, :, 3 * pw :] = part.reshape(ranks, 2, chunk, pw)

    @pl.when(u >= 8)
    def _():
        blk = 16
        one, zero = jnp.ones((blk, slots), BF), jnp.zeros((blk, slots), BF)

        @pl.when(u == 8)
        def _():
            for copy in ins:
                copy.wait()

        def sub_block(c, carry):
            rows = pl.ds(pl.multiple_of((u - 8) * trows + c * blk, blk), blk)
            g = jnp.concatenate([ds_ref[s, sub, rows, :] for s in range(8) for sub in range(2)], axis=0)
            for t in range(3):
                ids = ids_ref[t, rows, :].astype(F32).astype(BF)
                hot = jnp.concatenate([jnp.where(ids == jnp.bfloat16(b), one, zero) for b in range(buckets)], axis=0)
                span = slice(t * buckets * blk, (t + 1) * buckets * blk)
                acc_ref[span, :] += lax.dot_general(hot, g, NT, preferred_element_type=F32)
            return carry

        lax.fori_loop(0, trows // blk, sub_block, 0)

    def event(step):
        return lambda body: pl.when(u == step)(body)

    def core_stage(i):
        core_out[i].wait_recv()
        for p in (opp, par):
            total = wide_f32(part_ref[4 + i, :, p]) + wide_f32(crecv_ref[i, :, p])
            part_ref[4 + i, :, p] = total.astype(BF)
        for r in order:
            far_out[i][0][r].start()

    def own_sides():
        for i in range(2):
            for r in order:
                far_out[i][1][r].start()

    def far_stage(i):
        core_out[2 + i].wait_recv()
        for r in order:
            far_out[i][0][r].wait_recv()
            k = rank ^ r
            total = wide_f32(part_ref[i, k, opp]) + wide_f32(crecv_ref[2 + i, k, opp]) + wide_f32(frecv_ref[i, k, opp])
            part_ref[i, k, opp] = total.astype(BF)
            xa_out[i][r].start()

    def side_stage(i, r):
        far_out[i][1][r].wait_recv()
        xa_out[i][r].wait_recv()
        k = rank ^ r
        total = wide_f32(part_ref[i, k, par]) + wide_f32(crecv_ref[2 + i, k, par])
        total = total + wide_f32(frecv_ref[i, k, par]) + wide_f32(xarecv_ref[i, r])
        part_ref[i, k, par] = total.astype(BF)
        if r & 1:
            za_out[i][r].start()

    def rank_stage(i, r):
        total = wide_f32(part_ref[i, rank ^ r, par])
        for k in feeds(r):
            za_out[i][k].wait_recv()
            total = total + wide_f32(zarecv_ref[i, k - 1])
        if r == 0:
            return total
        part_ref[i, rank ^ r, par] = total.astype(BF)
        za_out[i][r].start()

    def ffn_stage(r):
        for copy in xf_last if r == 0 else [xf_out[r]]:
            copy.wait_recv()
        total = wide_f32(fown_ref[rank ^ r]) + wide_f32(xfrecv_ref[r])
        for k in feeds(r):
            zf_out[k].wait_recv()
            total = total + wide_f32(zfrecv_ref[k - 1])
        if r == 0:
            return total
        xfrecv_ref[r] = total.astype(BF)
        zf_out[r].start()

    def input_gradient():
        gm_in.wait()
        x = x_ref[...].astype(F32)
        inv = lax.rsqrt(jnp.mean(x * x, axis=-1, keepdims=True) + EPS)
        upstream = dx_ref[...]
        lifted = upstream * gain_ref[...].astype(F32)[None]
        inner = jnp.mean(lifted * x, axis=-1, keepdims=True)
        gib_ref[...] = gib_ref[...] + inv * lifted - x * (inv * inv * inv * inner)
        gi_out.start()
        gains = jnp.sum(upstream * x * inv, axis=0, keepdims=True)
        lanes = d // LANES
        for r in range(4):
            for j in range(lanes):
                span = slice(j * LANES, (j + 1) * LANES)
                nsend_ref[r, 3 * buckets + j : 3 * buckets + j + 1, :] = gains[:, span]
                nsend_ref[r, 3 * buckets + lanes + j : 3 * buckets + lanes + j + 1, :] = gain2_ref[:, span]

    plan = [[] for _ in range(steps)]
    for i in range(2):
        plan[2 * i].append(core_out[i].start)
        plan[2 * i + 1].append(functools.partial(core_stage, i))
        plan[4 + i].append(core_out[2 + i].start)
    plan[3].append(own_sides)
    plan[1].append(fown_in.wait)
    if ranks == 4:
        turn = lambda a, b: functools.partial(at_edge, functools.partial(ffn_stage, a), functools.partial(ffn_stage, b))
        plan[2].append(functools.partial(ffn_stage, 3))
        plan[5].append(turn(1, 2))
        plan[8].append(turn(2, 1))
    else:
        for k, r in enumerate(range(ranks - 1, 0, -1)):
            plan[3 + k * 6 // ranks].append(functools.partial(ffn_stage, r))
    plan[6].append(functools.partial(far_stage, 0))
    plan[7].append(input_gradient)
    plan[8].append(functools.partial(far_stage, 1))
    plan[8].append(xf_last[0].start)
    plan[12].extend(functools.partial(side_stage, 0, r) for r in order)
    plan[15].extend(functools.partial(rank_stage, 0, r) for r in range(ranks - 2, 0, -2))
    for k in range(steps):

        @pl.when(u == k)
        def _():
            for action in plan[k]:
                action()

    @pl.when(u == steps - 1)
    def _():
        blk, cols = 16, 16 * 16
        same = lax.broadcasted_iota(I32, (blk, cols), 0) == (lax.broadcasted_iota(I32, (blk, cols), 1) & (blk - 1))
        picked = [
            jnp.sum(jnp.where(same, acc_ref[b * blk : (b + 1) * blk, :], 0.0), axis=0, keepdims=True)
            for b in range(3 * buckets)
        ]
        picked = jnp.concatenate(picked, axis=0)
        source = lax.broadcasted_iota(I32, (cols, LANES), 0) >> 4
        target = lax.broadcasted_iota(I32, (cols, LANES), 1)
        for r in range(4):
            choose = jnp.where((source == target + heads * r) & (target < heads), 1.0, 0.0).astype(F32)
            nsend_ref[r, : 3 * buckets, :] = jnp.dot(
                picked, choose, preferred_element_type=F32, precision=lax.Precision.HIGHEST
            )
        for copy in sn_out + out_out[1:]:
            copy.start()

        def finish(i):
            total = rank_stage(i, 0)
            cols = slice(i * pw, (i + 1) * pw)
            gq_ref[:, cols] = total[:, :pw]
            gk_ref[:, cols] = total[:, pw : 2 * pw]
            gv_ref[:, cols] = total[:, 2 * pw : 3 * pw]
            go_ref[cols, :] = total[:, 3 * pw :].T

        for r in order[:-1]:
            side_stage(1, r)
        for copy in sn_out:
            copy.wait()
        nsend_ref[1] = nsend_ref[0] + nrecv_ref[0] + nrecv_ref[1] + nrecv_ref[2]
        sx_out.start()
        xf_last[1].start()
        side_stage(1, 0)
        finish(0)
        for r in range(ranks - 2, 0, -2):
            rank_stage(1, r)
        sx_out.wait()
        nsend_ref[2] = nsend_ref[1] + sxrecv_ref[...]
        for r in range(1, ranks):
            sz_out[r].start()
        total = ffn_stage(0)
        full, rest = split_quarter(ff)
        for m, ref in enumerate((fg_ref, fu_ref, fd_ref)):
            ref[:full, :] = total[:, m * full : (m + 1) * full].T
            if rest:
                ref[full:, :] = total[:, 3 * full + m * rest : 3 * full + (m + 1) * rest].T
        total = nsend_ref[2]
        for r in range(1, ranks):
            sz_out[r].wait_recv()
            total = total + szrecv_ref[r - 1]
        small_ref[...] = total
        finish(1)
        gi_out.wait()
        for copy in out_out:
            copy.wait()
        for i in range(2):
            for copy in far_out[i][0] + far_out[i][1] + xa_out[i] + za_out[i][1:]:
                copy.wait_send()
        for copy in core_out + xf_out[1:] + xf_last + zf_out[1:] + sz_out[1:]:
            copy.wait_send()


def backward(wide, buckets, ff, ga, x, gain, gain2, fsum, gm, e, ids, out, wo_all, ctx, linv, qkv, w_all, trows=64):
    slots, d = x.shape
    heads = 4
    pw = 2 * HEAD_DIM
    ranks, chunk = wide // 2, d // wide
    packed = fsum.shape[-1]
    width = heads * HEAD_DIM
    small = 3 * buckets + 2 * d // LANES
    vmem, anywhere = pl.BlockSpec(memory_space=pltpu.VMEM), pl.BlockSpec(memory_space=pl.ANY)
    shape = jax.ShapeDtypeStruct
    dma = pltpu.SemaphoreType.DMA

    def slot(u):
        return backward_slot(jnp.minimum(u, 7))

    return pl.pallas_call(
        functools.partial(backward_kernel, wide, heads, buckets, trows, ff),
        grid=(8 + slots // trows,),
        in_specs=[vmem] * 4 + [anywhere] * 7 + [
            pl.BlockSpec((pw, d), lambda u: (slot(u), 0)),
            pl.BlockSpec((slots, pw), lambda u: (0, slot(u))),
            pl.BlockSpec((slots, pw), lambda u: (0, slot(u))),
            pl.BlockSpec((3, slots, pw), lambda u: (0, 0, slot(u))),
            pl.BlockSpec((3, d, pw), lambda u: (0, 0, slot(u))),
        ],
        out_specs=[anywhere] * 2 + [vmem] * 8,
        out_shape=[
            shape((slots, d), F32),
            shape((slots, d), BF),
            shape((small, LANES), F32),
            shape((chunk, width), F32),
            shape((chunk, width), F32),
            shape((chunk, width), F32),
            shape((width, chunk), F32),
            shape((ff, chunk), F32),
            shape((ff, chunk), F32),
            shape((ff, chunk), F32),
        ],
        scratch_shapes=[
            pltpu.VMEM((slots, d), F32),
            pltpu.VMEM((ranks, chunk, packed), BF),
            pltpu.VMEM((8, 2, slots, slots), BF),
            pltpu.VMEM((3, slots, slots), I32),
            pltpu.VMEM((d, slots), BF),
            pltpu.VMEM((d, slots), BF),
            pltpu.VMEM((slots, d), F32),
            pltpu.VMEM((3 * buckets * 16, 16 * 16), F32),
            pltpu.VMEM((8, ranks, 2, chunk, 4 * pw), BF),
            pltpu.VMEM((4, ranks, 2, chunk, 4 * pw), BF),
            pltpu.VMEM((2, ranks, 2, chunk, 4 * pw), BF),
            pltpu.VMEM((2, ranks, chunk, 4 * pw), BF),
            pltpu.VMEM((2, ranks - 1, chunk, 4 * pw), BF),
            pltpu.VMEM((ranks, chunk, packed), BF),
            pltpu.VMEM((ranks - 1, chunk, packed), BF),
            pltpu.VMEM((4, small, LANES), F32),
            pltpu.VMEM((3, small, LANES), F32),
            pltpu.VMEM((small, LANES), F32),
            pltpu.VMEM((ranks - 1, small, LANES), F32),
            dma((6,)), dma((2,)), dma((4, 2)), dma((2, 2, ranks, 2)), dma((2, 2)), dma((ranks + 1, 2)), dma((ranks - 1, 2)),
            dma((2, ranks, 2)), dma((2, ranks - 1, 2)), dma((3, 2)), dma((2,)), dma((ranks - 1, 2)),
        ],
        compiler_params=pltpu.CompilerParams(
            vmem_limit_bytes=VMEM_LIMIT, collective_id=3, has_side_effects=True
        ),
        cost_estimate=pl.CostEstimate(flops=30 * slots * d * d, bytes_accessed=60 << 20, transcendentals=0),
        name="backward",
    )(ga, x, gain, gain2, fsum, gm, e, *ids, out, wo_all, ctx, linv, qkv, w_all)


def results_kernel(
    wide, narrow, buckets, heads, middle_ref, out_ref, outin_ref, gi_ref, small_ref, *rest,
):
    sources, (block_ref, go_ref, ga_ref, gf_ref, tr_ref, th_ref, tv_ref), targets = rest[:7], rest[7:14], rest[14:]
    block_ref[...] = (middle_ref[...] + (out_ref[...].astype(F32) + outin_ref[...].astype(F32))).astype(BF)
    go_ref[...] = gi_ref[...]

    @pl.when(pl.program_id(0) == 0)
    def _():
        for a, b in zip(sources, targets):
            b[...] = a[...]
        w, n = lax.axis_index("wide"), lax.axis_index("narrow")
        d = middle_ref.shape[1]
        per, own = d // (wide * narrow), buckets // wide
        start = (w * narrow + n) * per
        for k, ref in enumerate((ga_ref, gf_ref)):
            row = small_ref[pl.ds(3 * buckets + k * (d // LANES) + start // LANES, 1), :]
            lane = lax.broadcasted_iota(I32, (per, LANES), 1)
            mine = lane == lax.broadcasted_iota(I32, (per, LANES), 0) + start % LANES
            ref[...] = jnp.sum(jnp.where(mine, jnp.broadcast_to(row, (per, LANES)), 0.0), axis=1)
        for k, ref in enumerate((tr_ref, th_ref, tv_ref)):
            ref[...] = small_ref[pl.ds(k * buckets + w * own, own), :heads]


def results(wide, narrow, buckets, heads, middle, out, outin, small, grad_input, big):
    slots, d = middle.shape
    shape = jax.ShapeDtypeStruct
    per, own = d // (wide * narrow), buckets // wide
    rows = pl.BlockSpec((slots // 4, d), lambda i: (i, 0))
    whole = lambda *sh: pl.BlockSpec(sh, lambda i: (0,) * len(sh))
    return pl.pallas_call(
        functools.partial(results_kernel, wide, narrow, buckets, heads),
        grid=(4,),
        in_specs=[rows] * 4 + [whole(*small.shape)] + [whole(*x.shape) for x in big],
        out_specs=[rows] * 2 + [whole(per)] * 2 + [whole(own, heads)] * 3 + [whole(*x.shape) for x in big],
        out_shape=[shape((slots, d), BF), shape((slots, d), F32)] + [shape((per,), F32)] * 2
        + [shape((own, heads), F32)] * 3 + [shape(x.shape, x.dtype) for x in big],
        compiler_params=pltpu.CompilerParams(vmem_limit_bytes=VMEM_LIMIT),
        name="results",
    )(middle, out, outin, grad_input, small, *big)


def shards(
    wide, narrow, hidden_in, grad_out, gain_attn, gain_ffn, w_query, w_key, w_value, w_output,
    table_rel, table_horiz, table_vert, wi_gate, wi_up, wo_ffn, counts, patch_mask,
    bucket_rel, bucket_horiz, bucket_vert,
):
    slots = bucket_rel.shape[1]
    rows, d = hidden_in.shape
    buckets, heads = table_rel.shape
    width = w_query.shape[1]
    ff = wi_gate.shape[1]
    assert rows == slots and narrow == 4 and wide >= 4 and heads * HEAD_DIM == width
    ids = (bucket_rel, bucket_horiz, bucket_vert)

    qkv, exps, context, linv, w_all, wo_all, middle, ffn_own, grad_far, wg_core, wu_core, wd_core = forward(
        counts, patch_mask, hidden_in, gain_attn, gain_ffn, (table_rel.T, table_horiz.T, table_vert.T),
        w_query, w_key, w_value, w_output, ids, grad_out, wi_gate.T, wi_up.T, wo_ffn,
    )
    out, ffn_sum, grad_middle, grad_attn, grad_gain_second = feed_forward(
        ffn_own, grad_out, grad_far, middle, gain_ffn,
        (wi_gate.T, wi_up.T, wo_ffn), (wg_core, wu_core, wd_core),
    )
    grad_input, out_in, small, gq, gk, gv, go, fg, fu, fd = backward(
        wide, buckets, ff, grad_attn, hidden_in, gain_attn, grad_gain_second,
        ffn_sum.reshape(wide // 2, 2, d // wide, -1), grad_middle, exps, ids, out,
        wo_all, context, linv, qkv, w_all,
    )
    block_out, grad_input, gain1, gain2, rel, horiz, vert, gq, gk, gv, go, fg, fu, fd = results(
        wide, narrow, buckets, heads, middle, out, out_in, small, grad_input, (gq, gk, gv, go, fg, fu, fd)
    )
    return (
        block_out, grad_input, gain1, gain2, gq, gk, gv, go, rel, horiz, vert, fg.T, fu.T, fd,
    )


def solution(mesh):
    rows, both = P(("wide", "narrow"), None), P(("wide", "narrow"))
    cols, across = P(None, "narrow"), P("narrow", None)
    grid, turned = P("wide", "narrow"), P("narrow", "wide")
    pages = P("wide", None, None)
    return jax.shard_map(
        functools.partial(shards, mesh.shape["wide"], mesh.shape["narrow"]),
        mesh=mesh,
        in_specs=(
            rows, rows, P(), P(), cols, cols, cols, across, cols, cols, cols, cols, cols, across,
            P("wide"), P("wide", None), pages, pages, pages,
        ),
        out_specs=(
            rows, rows, both, both, grid, grid, grid, turned, grid, grid, grid, grid, grid, turned,
        ),
        check_vma=False,
    )
```

```python
import functools
import math

import jax
import jax.numpy as jnp
from jax import lax
from jax.experimental import pallas as pl
from jax.experimental.pallas import tpu as pltpu
from jax.sharding import PartitionSpec as P

F32 = jnp.float32
BF = jnp.bfloat16
I32 = jnp.int32
HEAD_DIM = 64
LANES = 128
EPS = 1e-06
NT = (((1,), (1,)), ((), ()))

FIXED = 2048.0
OFFSET = 8192
MASKED = -3.0e12
VMEM_LIMIT = 60 << 20
MESH = pl.DeviceIdType.MESH


def lookup(table_row, ids):
    return jnp.take_along_axis(table_row, ids, axis=1, mode="promise_in_bounds")


def neighbours():
    w, n = lax.axis_index("wide"), lax.axis_index("narrow")
    return w, n, (w, n ^ 1), (w, n ^ 2), (w, n ^ 3), (w ^ 1, n)


def greet(devices):
    barrier = pltpu.get_barrier_semaphore()
    for device in devices:
        pl.semaphore_signal(barrier, inc=1, device_id=device, device_id_type=MESH)
    pl.semaphore_wait(barrier, len(devices))


def remote(src, dst, sems, device):
    return pltpu.make_async_remote_copy(
        src_ref=src, dst_ref=dst, send_sem=sems.at[0], recv_sem=sems.at[1], device_id=device, device_id_type=MESH
    )


def forward_kernel(
    heads, buckets, chunk,
    counts_ref, patch_ref, x_ref, gain1_ref, gain2_ref, tr_ref, th_ref, tv_ref,
    wq_ref, wk_ref, wv_ref, wo_ref, ir_ref, ih_ref, iv_ref, go_ref, wg_ref, wu_ref, wd_ref,
    qkv_to, e_ref, ctx_to, linv_to, wall_to, woall_to, middle_ref, ffn_ref, gofar_ref, wgc_ref, wuc_ref, wdc_ref,
    qkv_ref, ctx_ref, linv_ref, wall_ref, woall_ref, normed_ref, mask_ref, ids_ref, tab_ref, tabs_ref, words_ref, ebuf_ref,
    own_sem, id_sem, e_sem, core_sem, far_sem, deep_sem, wide_sem, fwd_sem, tab_sem, big_sem, leave_sem,
):
    pw = 2 * HEAD_DIM
    slots, d = x_ref.shape
    piece = d // 2
    w, n, core, far, diag, side = neighbours()
    deep = (w ^ 2, n)
    half, share = w & 1, (w >> 1) & 1
    other = 1 - half

    def source(m, pair, part=None):
        cols = pl.ds(pl.multiple_of(pair * pw, pw), pw)
        span = slice(None) if part is None else pl.ds(pl.multiple_of(part * piece, piece), piece)
        return wo_ref.at[cols, span] if m == 3 else (wq_ref, wk_ref, wv_ref)[m].at[span, cols]

    def place(m, slot, part=None):
        cols = pl.ds(pl.multiple_of(slot * pw, pw), pw)
        span = slice(None) if part is None else pl.ds(pl.multiple_of(part * piece, piece), piece)
        return woall_ref.at[cols, span] if m == 3 else wall_ref.at[m, span, cols]

    ids_in = [pltpu.make_async_copy(r.at[n], ids_ref.at[t], id_sem.at[t]) for t, r in enumerate((ir_ref, ih_ref, iv_ref))]
    own_in = [[pltpu.make_async_copy(source(m, p), place(m, p), own_sem.at[p, m]) for m in range(4)] for p in range(2)]
    for copy in own_in[0][:3] + ids_in + own_in[0][3:] + own_in[1]:
        copy.start()

    tab_ref[...] = jnp.zeros_like(tab_ref)
    for t, r in enumerate((tr_ref, th_ref, tv_ref)):
        tab_ref[t * heads : (t + 1) * heads, :buckets] = jnp.floor(r[...].astype(F32) * FIXED + 0.5)

    greet((core, far, diag, side, deep))
    far_out = [remote(source(m, half, share), place(m, 4 + half, share), far_sem.at[m], far) for m in range(4)]
    deep_out = [remote(place(m, 4 + half, share), place(m, 4 + half, share), deep_sem.at[m], deep) for m in range(4)]
    core_out = [[remote(source(m, p), place(m, 2 + p), core_sem.at[p, m], core) for m in range(4)] for p in range(2)]
    tabs_out = [remote(tab_ref, tabs_ref.at[r - 1], tab_sem.at[r - 1], dev) for r, dev in ((1, core), (2, far), (3, diag))]
    wide_out = [
        [remote(place(m, 4 + half, k), place(m, 4 + half, k), wide_sem.at[m, i], side) for i, k in enumerate((share, 1 - share))]
        for m in range(4)
    ]
    fwd_out = [
        [remote(place(m, 4 + half, k), place(m, 6 + half, k), fwd_sem.at[m, i], core) for i, k in enumerate((share, 1 - share))]
        for m in range(4)
    ]
    last_out = [remote(place(m, 4 + other), place(m, 6 + other), fwd_sem.at[m, 2], core) for m in range(4)]
    go_out = remote(go_ref, gofar_ref, big_sem.at[0], far)
    ffn_out = [
        remote(wg_ref, wgc_ref, big_sem.at[1], core),
        remote(wu_ref, wuc_ref, big_sem.at[2], core),
        remote(wd_ref, wdc_ref, big_sem.at[3], core),
    ]
    for copy in tabs_out + far_out + [go_out] + core_out[0] + core_out[1]:
        copy.start()

    x = x_ref[...].astype(F32)
    inv = lax.rsqrt(jnp.mean(x * x, axis=-1, keepdims=True) + EPS)
    normed_ref[...] = (x * inv * gain1_ref[...].astype(F32)[None]).astype(BF)
    text = slots - patch_ref.shape[1]
    shown = jnp.concatenate(
        [
            jnp.where(lax.broadcasted_iota(I32, (1, text), 1) < counts_ref[n], 1, 0),
            patch_ref[pl.ds(n, 1), :],
        ],
        axis=1,
    )
    column = jnp.broadcast_to(jnp.where(shown == 1, 0.0, MASKED), (pw, slots)).T
    lane_all = lax.broadcasted_iota(I32, (slots, pw), 1)
    mask_ref[...] = jnp.where(lane_all == 0, column, 0.0).astype(BF)
    ones = jnp.ones((slots, pw), BF)
    lane = lax.broadcasted_iota(I32, (chunk, pw), 1)
    low = lane < HEAD_DIM
    first = jnp.where(lane == 0, 1.0, 0.0).astype(BF)
    to_log2 = math.log2(math.e) / FIXED

    def pack_words(r, table):
        fixed = table.astype(I32)
        for p in range(2):
            for t in range(3):
                row = t * heads + 2 * p
                words_ref[2 * r + p, t : t + 1, :] = fixed[row + 1 : row + 2] * 65536 + fixed[row : row + 1] + OFFSET

    pack_words(0, tab_ref[...])
    for copy in ids_in:
        copy.wait()

    def e_out(parity, slot):
        return pltpu.make_async_copy(ebuf_ref.at[parity], e_ref.at[slot], e_sem.at[parity])

    def leaving(slot):
        cols = pl.ds(pl.multiple_of(slot * pw, pw), pw)
        pairs = (
            (wall_ref.at[:, :, cols], wall_to.at[:, :, cols]),
            (qkv_ref.at[:, :, cols], qkv_to.at[:, :, cols]),
            (ctx_ref.at[:, cols], ctx_to.at[:, cols]),
            (linv_ref.at[:, cols], linv_to.at[:, cols]),
        )
        return [pltpu.make_async_copy(a, b, leave_sem.at[k, slot]) for k, (a, b) in enumerate(pairs)]

    def slot_of(t):
        late = 4 + 2 * (t & 1) + jnp.where(t >= 6, other, half)
        return jnp.where(t < 4, t, late)

    plan = [[] for _ in range(16)]

    def far_arrived(m):
        far_out[m].wait_recv()
        deep_out[m].start()
        wide_out[m][0].start()
        fwd_out[m][0].start()

    def deep_arrived(m):
        deep_out[m].wait_recv()
        wide_out[m][1].start()
        fwd_out[m][1].start()

    def wide_arrived(m):
        for copy in wide_out[m]:
            copy.wait_recv()
        last_out[m].start()

    def tables_arrived():
        for r, copy in enumerate(tabs_out):
            copy.wait()
            pack_words(r + 1, tabs_ref[r])

    for p in range(2):
        plan[2 * p].extend(own_in[p][m].wait for m in range(3))
        plan[4 + 2 * p].extend(core_out[p][m].wait_recv for m in range(3))
    plan[3].append(tables_arrived)
    for m in range(4):
        plan[2 + m].append(functools.partial(far_arrived, m))
        plan[4 + m].append(functools.partial(deep_arrived, m))
    plan[7].extend(copy.start for copy in ffn_out)
    plan[10].extend(copy.wait_recv for m in range(3) for copy in fwd_out[m])
    plan[12].extend(functools.partial(wide_arrived, m) for m in range(3))
    plan[14].extend(last_out[m].wait_recv for m in range(3))
    plan[14].append(functools.partial(wide_arrived, 3))

    def events(t, c):
        for k in range(8):
            if plan[2 * k + c]:

                @pl.when(t == k)
                def _():
                    for action in plan[2 * k + c]:
                        action()

    def step(t, carry):
        slot = slot_of(t)
        events(t, 0)
        parity = t & 1

        @pl.when(t >= 2)
        def _():
            e_out(parity, slot).wait()

        cols = pl.ds(pl.multiple_of(slot * pw, pw), pw)
        weights = jnp.concatenate([wall_ref[m, :, cols] for m in range(3)], axis=1)
        joined = jnp.dot(normed_ref[...], weights, preferred_element_type=F32).astype(BF)
        for m in range(3):
            qkv_ref[m, :, cols] = joined[:, m * pw : (m + 1) * pw]
        kx = jnp.concatenate([joined[:, pw : 2 * pw], mask_ref[...]], axis=1)
        vx = jnp.concatenate([joined[:, 2 * pw :], ones], axis=1)
        words = words_ref[slot]
        for c in range(slots // chunk):
            if c == slots // chunk // 2:
                events(t, 1)
            rows = slice(c * chunk, (c + 1) * chunk)
            q2 = joined[rows, :pw] * jnp.bfloat16(FIXED)
            zero = jnp.zeros_like(q2)
            scores = []
            for sub in range(2):
                q = jnp.where(low, q2, zero) if sub == 0 else jnp.where(low, zero, q2)
                q = jnp.concatenate([q, first], axis=1)
                scores.append(lax.dot_general(q, kx, NT, preferred_element_type=F32))
            tabs = [jnp.broadcast_to(words[k : k + 1, :], (chunk, LANES)) for k in range(3)]
            parts = ([], [])
            for j in range(slots // LANES):
                sl = slice(j * LANES, (j + 1) * LANES)
                bias = (
                    lookup(tabs[0], ids_ref[0, rows, sl])
                    + lookup(tabs[1], ids_ref[1, rows, sl])
                    + lookup(tabs[2], ids_ref[2, rows, sl])
                )
                parts[0].append(scores[0][:, sl] + (bias & 0xFFFF).astype(F32))
                parts[1].append(scores[1][:, sl] + (bias >> 16).astype(F32))
            outs = []
            for sub in range(2):
                s = jnp.concatenate(parts[sub], axis=1)
                peak = jnp.max(s, axis=1, keepdims=True)
                e = jnp.exp2((s - peak) * to_log2).astype(BF)
                ebuf_ref[parity, sub, rows, :] = e
                outs.append(jnp.dot(e, vx, preferred_element_type=F32))
            linv = 1.0 / jnp.where(low, outs[0][:, pw:], outs[1][:, pw:])
            linv_ref[rows, cols] = linv
            ctx_ref[rows, cols] = (jnp.where(low, outs[0][:, :pw], outs[1][:, :pw]) * linv).astype(BF)
        e_out(parity, slot).start()
        for copy in leaving(slot):
            copy.start()
        return carry

    lax.fori_loop(0, 8, step, 0)
    for p in range(2):
        own_in[p][3].wait()
        core_out[p][3].wait_recv()
    for copy in fwd_out[3] + last_out[3:]:
        copy.wait_recv()
    wo_leaving = pltpu.make_async_copy(woall_ref, woall_to, id_sem.at[0])
    wo_leaving.start()
    middle = x_ref[...].astype(F32) + jnp.dot(ctx_ref[...], woall_ref[...], preferred_element_type=F32)
    middle_ref[...] = middle
    inv = lax.rsqrt(jnp.mean(middle * middle, axis=-1, keepdims=True) + EPS)
    ffn_ref[...] = (middle * inv * gain2_ref[...].astype(F32)[None]).astype(BF)
    for p in range(2):
        e_out(p, p).wait()
        for m in range(4):
            core_out[p][m].wait_send()
    for m in range(4):
        for copy in [far_out[m], deep_out[m], last_out[m]] + wide_out[m] + fwd_out[m]:
            copy.wait_send()
    for copy in ffn_out:
        copy.wait()
    for slot in range(8):
        for copy in leaving(slot):
            copy.wait()
    wo_leaving.wait()
    go_out.wait()


def forward(counts, patches, x, gain1, gain2, tables, wq, wk, wv, wo, ids, grad_out, wg, wu, wd, chunk=256):
    slots, d = x.shape
    heads = wq.shape[1] // HEAD_DIM
    buckets = tables[0].shape[1]
    ff = wd.shape[0]
    assert heads == 4
    vmem, anywhere = pl.BlockSpec(memory_space=pltpu.VMEM), pl.BlockSpec(memory_space=pl.ANY)
    shape = jax.ShapeDtypeStruct
    dma = pltpu.SemaphoreType.DMA
    return pl.pallas_call(
        functools.partial(forward_kernel, heads, buckets, chunk),
        in_specs=[pl.BlockSpec(memory_space=pltpu.SMEM)] + [vmem] * 7 + [anywhere] * 11,
        out_specs=[anywhere] * 6 + [vmem] * 2 + [anywhere] * 4,
        out_shape=[
            shape((3, slots, d), BF),
            shape((8, 2, slots, slots), BF),
            shape((slots, d), BF),
            shape((slots, d), F32),
            shape((3, d, d), BF),
            shape((d, d), BF),
            shape((slots, d), F32),
            shape((slots, d), BF),
            shape((slots, d), BF),
            shape((ff, d), BF),
            shape((ff, d), BF),
            shape((ff, d), BF),
        ],
        scratch_shapes=[
            pltpu.VMEM((3, slots, d), BF),
            pltpu.VMEM((slots, d), BF),
            pltpu.VMEM((slots, d), F32),
            pltpu.VMEM((3, d, d), BF),
            pltpu.VMEM((d, d), BF),
            pltpu.VMEM((slots, d), BF),
            pltpu.VMEM((slots, 2 * HEAD_DIM), BF),
            pltpu.VMEM((3, slots, slots), I32),
            pltpu.VMEM((16, LANES), F32),
            pltpu.VMEM((3, 16, LANES), F32),
            pltpu.VMEM((8, 8, LANES), I32),
            pltpu.VMEM((2, 2, slots, slots), BF),
            dma((2, 4)), dma((3,)), dma((2,)), dma((2, 4, 2)), dma((4, 2)), dma((4, 2)), dma((4, 2, 2)), dma((4, 3, 2)),
            dma((3, 2)), dma((4, 2)), dma((4, 8)),
        ],
        compiler_params=pltpu.CompilerParams(
            vmem_limit_bytes=VMEM_LIMIT, collective_id=1, has_side_effects=True
        ),
        cost_estimate=pl.CostEstimate(flops=20 * slots * d * d, bytes_accessed=40 << 20, transcendentals=16 * slots * slots),
        name="forward",
    )(counts, patches, x, gain1, gain2, *tables, wq, wk, wv, wo, *ids, grad_out, wg, wu, wd)


def gelu_parts(v):
    c, k = math.sqrt(2.0 / math.pi), 0.044715
    square = v * v
    t = jnp.tanh(c * v * (1.0 + k * square))
    up = 0.5 * (1.0 + t)
    slope = up + 0.5 * v * (1.0 - t * t) * (c * (1.0 + 3.0 * k * square))
    return v * up, slope


def split_quarter(ff):
    return ff // LANES * LANES, ff % LANES


def packed_width(ff):
    full, rest = split_quarter(ff)
    return 3 * full + -(-3 * rest // LANES) * LANES


def ffn_kernel(
    block, ff,
    x_ref, go_ref, gofar_ref, middle_ref, gain_ref, w0_ref, w1_ref, w2_ref, c0_ref, c1_ref, c2_ref,
    out_to, sum_to, gm_to, ga_to, gain_out_ref,
    out_ref, sum_ref, gm_ref, ga_ref, xall_ref, gall_ref, wgu_ref, wd_ref, xt_ref, gt_ref, act_ref, send_ref, recv_ref, own_ref, backfar_ref, backin_ref,
    in_sem, w_sem, x_sem, back_sem, dw_sem, leave_sem, end_sem,
):
    slots, d = middle_ref.shape
    halves = slots // block
    full, rest = split_quarter(ff)
    both = 2 * ff
    _, _, core, far, _, _ = neighbours()

    ins = [
        pltpu.make_async_copy(x_ref, xall_ref.at[pl.ds(0, slots), :], in_sem.at[0]),
        pltpu.make_async_copy(go_ref, gall_ref.at[pl.ds(0, slots), :], in_sem.at[1]),
        pltpu.make_async_copy(gofar_ref, gall_ref.at[pl.ds(slots, slots), :], in_sem.at[2]),
    ]
    weights = []
    for m, pair in enumerate(((w0_ref, c0_ref), (w1_ref, c1_ref), (w2_ref, c2_ref))):
        target, base = (wd_ref, 0) if m == 2 else (wgu_ref, m * both)
        for q, r in enumerate(pair):
            for k, (start, size, at) in enumerate(((0, full, q * full), (full, rest, 2 * full + q * rest))):
                if size:
                    weights.append(
                        pltpu.make_async_copy(
                            r.at[pl.ds(start, size), :], target.at[pl.ds(base + at, size), :], w_sem.at[m, q, k]
                        )
                    )
    for copy in ins[:2] + weights + ins[2:]:
        copy.start()
    greet((core, far))
    x_out = [
        remote(x_ref.at[pl.ds(i * block, block), :], xall_ref.at[pl.ds(slots + i * block, block), :], x_sem.at[i], far)
        for i in range(halves)
    ]
    for copy in x_out:
        copy.start()
    back_out = [
        remote(backfar_ref.at[pl.ds(i * block, block), :], backin_ref.at[pl.ds(i * block, block), :], back_sem.at[i], far)
        for i in range(halves)
    ]
    for copy in ins + weights:
        copy.wait()

    def step(b, carry):
        for i in range(halves):

            @pl.when(b == halves + i)
            def _():
                x_out[i].wait_recv()

        rows = pl.ds(pl.multiple_of(b * block, block), block)
        x, g = xall_ref[rows, :], gall_ref[rows, :]
        xt_ref[:, rows] = x.T
        gt_ref[:, rows] = g.T
        grown = lax.dot_general(x, wgu_ref[...], NT, preferred_element_type=F32)
        grad_hidden = lax.dot_general(g, wd_ref[...], NT, preferred_element_type=F32)
        gate, upper = grown[:, :both], grown[:, both:]
        gelu, slope = gelu_parts(gate)
        dg = (grad_hidden * upper * slope).astype(BF)
        du = (grad_hidden * gelu).astype(BF)
        hidden = (gelu * upper).astype(BF)
        act_ref[0, rows, :] = dg
        act_ref[1, rows, :] = du
        act_ref[2, rows, :] = hidden
        back = jnp.dot(jnp.concatenate([dg, du], axis=1), wgu_ref[...], preferred_element_type=F32)

        @pl.when(b < halves)
        def _():
            own_ref[rows, :] = back

        for i in range(halves):

            @pl.when(b == halves + i)
            def _():
                backfar_ref[i * block : (i + 1) * block, :] = back.astype(BF)
                back_out[i].start()

        out_ref[rows, :] = jnp.dot(hidden, wd_ref[...], preferred_element_type=F32).astype(BF)
        pltpu.make_async_copy(out_ref.at[rows, :], out_to.at[rows, :], leave_sem.at[b]).start()
        return carry

    lax.fori_loop(0, 2 * halves, step, 0)

    tile = d // 2
    used = 3 * (full + rest)
    dw_out = [
        remote(send_ref.at[pl.ds(c * tile, tile), :], recv_ref.at[pl.ds(c * tile, tile), :], dw_sem.at[c], core)
        for c in range(2)
    ]
    for c in range(2):
        rows = slice(c * tile, (c + 1) * tile)
        for m in range(3):
            left = gt_ref if m == 2 else xt_ref
            dw = jnp.dot(left[rows, :], act_ref[m], preferred_element_type=F32).astype(BF)
            for q, target in enumerate((sum_ref, send_ref)):
                target[rows, m * full : (m + 1) * full] = dw[:, q * full : (q + 1) * full]
                if rest:
                    at = 2 * full + q * rest
                    target[rows, 3 * full + m * rest : 3 * full + (m + 1) * rest] = dw[:, at : at + rest]
        for target in (sum_ref, send_ref):
            if used < target.shape[1]:
                target[rows, used:] = jnp.zeros((tile, target.shape[1] - used), BF)
        dw_out[c].start()
    leaving = []
    for c in range(2):
        rows = slice(c * tile, (c + 1) * tile)
        dw_out[c].wait_recv()
        sum_ref[rows, :] = (sum_ref[rows, :].astype(F32) + recv_ref[rows, :].astype(F32)).astype(BF)
        at = pl.ds(c * tile, tile)
        leaving.append(pltpu.make_async_copy(sum_ref.at[at, :], sum_to.at[at, :], end_sem.at[c]))
        leaving[-1].start()

    gains = 0.0
    for i in range(halves):
        rows, at = slice(i * block, (i + 1) * block), pl.ds(i * block, block)
        back_out[i].wait_recv()
        middle = middle_ref[rows, :]
        inv = lax.rsqrt(jnp.mean(middle * middle, axis=-1, keepdims=True) + EPS)
        upstream = own_ref[rows, :] + backin_ref[rows, :].astype(F32)
        lifted = upstream * gain_ref[...].astype(F32)[None]
        inner = jnp.mean(lifted * middle, axis=-1, keepdims=True)
        gains = gains + jnp.sum(upstream * middle * inv, axis=0, keepdims=True)
        gm = gall_ref[rows, :].astype(F32) + inv * lifted - middle * (inv * inv * inv * inner)
        gm_ref[rows, :] = gm
        ga_ref[rows, :] = gm.astype(BF)
        for k, (a, b) in enumerate(((gm_ref, gm_to), (ga_ref, ga_to))):
            leaving.append(pltpu.make_async_copy(a.at[at, :], b.at[at, :], end_sem.at[2 + 2 * i + k]))
            leaving[-1].start()
    gain_out_ref[...] = gains
    for copy in x_out + back_out + dw_out:
        copy.wait_send()
    for b in range(2 * halves):
        at = pl.ds(b * block, block)
        pltpu.make_async_copy(out_ref.at[at, :], out_to.at[at, :], leave_sem.at[b]).wait()
    for copy in leaving:
        copy.wait()


def feed_forward(x, go, gofar, middle, gain, own, other, block=256):
    slots, d = x.shape
    ff = own[0].shape[0]
    vmem, anywhere = pl.BlockSpec(memory_space=pltpu.VMEM), pl.BlockSpec(memory_space=pl.ANY)
    shape = jax.ShapeDtypeStruct
    dma = pltpu.SemaphoreType.DMA
    halves = slots // block
    packed = packed_width(ff)
    return pl.pallas_call(
        functools.partial(ffn_kernel, block, ff),
        in_specs=[anywhere] * 3 + [vmem] * 2 + [anywhere] * 6,
        out_specs=[anywhere] * 4 + [vmem],
        out_shape=[
            shape((2 * slots, d), BF),
            shape((d, packed), BF),
            shape((slots, d), F32),
            shape((slots, d), BF),
            shape((1, d), F32),
        ],
        scratch_shapes=[
            pltpu.VMEM((2 * slots, d), BF),
            pltpu.VMEM((d, packed), BF),
            pltpu.VMEM((slots, d), F32),
            pltpu.VMEM((slots, d), BF),
            pltpu.VMEM((2 * slots, d), BF),
            pltpu.VMEM((2 * slots, d), BF),
            pltpu.VMEM((4 * ff, d), BF),
            pltpu.VMEM((2 * ff, d), BF),
            pltpu.VMEM((d, 2 * slots), BF),
            pltpu.VMEM((d, 2 * slots), BF),
            pltpu.VMEM((3, 2 * slots, 2 * ff), BF),
            pltpu.VMEM((d, packed), BF),
            pltpu.VMEM((d, packed), BF),
            pltpu.VMEM((slots, d), F32),
            pltpu.VMEM((slots, d), BF),
            pltpu.VMEM((slots, d), BF),
            dma((3,)), dma((3, 2, 2)), dma((halves, 2)), dma((halves, 2)), dma((2, 2)),
            dma((2 * halves,)), dma((2 + 2 * halves,)),
        ],
        compiler_params=pltpu.CompilerParams(
            vmem_limit_bytes=VMEM_LIMIT, collective_id=2, has_side_effects=True
        ),
        cost_estimate=pl.CostEstimate(flops=36 * slots * d * ff, bytes_accessed=40 << 20, transcendentals=4 * slots * ff),
        name="feed_forward",
    )(x, go, gofar, middle, gain, *own, *other)


def backward_slot(k):
    return jnp.where(k < 4, 6 - 2 * (k & 1) + (k >> 1), 6 - 2 * (k >> 1) + (k & 1))


def backward_kernel(
    wide, heads, buckets, trows, ff,
    ga_ref, x_ref, gain_ref, gain2_ref, fsum_ref, gm_ref, e_ref, ir_ref, ih_ref, iv_ref, out_ref,
    wo_ref, ctx_ref, linv_ref, qkv_ref, wall_ref,
    gi_ref, outin_ref, small_ref, gq_ref, gk_ref, gv_ref, go_ref, fg_ref, fu_ref, fd_ref,
    gib_ref, fown_ref, ds_ref, ids_ref, nt_ref, gat_ref, dx_ref, acc_ref, part_ref, crecv_ref, frecv_ref, xarecv_ref, zarecv_ref,
    xfrecv_ref, zfrecv_ref, nsend_ref, nrecv_ref, parts_ref, srecv_ref,
    in_sem, e_sem, core_sem, far_sem, out_sem, xf_sem, zf_sem, xa_sem, za_sem, sn_sem, ss_sem,
):
    pw = 2 * HEAD_DIM
    slots, d = ga_ref.shape
    half_rows = slots // 2
    ranks = wide // 2
    chunk = d // wide
    steps = 8 + slots // trows
    u = pl.program_id(0)
    w, n, core, far, diag, side = neighbours()
    par, rank = w & 1, w >> 1
    opp = 1 - par
    peer = lambda r: (2 * (rank ^ r) + par, n)
    slot_of = backward_slot
    slot = slot_of(jnp.minimum(u, 7))

    ins = [pltpu.make_async_copy(r.at[n], ids_ref.at[t], in_sem.at[t]) for t, r in enumerate((ir_ref, ih_ref, iv_ref))]
    gm_in = pltpu.make_async_copy(gm_ref, gib_ref, in_sem.at[3])
    fown_in = pltpu.make_async_copy(fsum_ref.at[:, par], fown_ref, in_sem.at[4])
    gi_out = pltpu.make_async_copy(gib_ref, gi_ref, in_sem.at[5])
    core_out = [remote(part_ref.at[s], crecv_ref.at[i], core_sem.at[i], core) for i, s in enumerate((6, 7, 2, 3))]
    order = list(range(ranks - 1, 0, -2)) + list(range(ranks - 2, -1, -2))
    far_out = [
        [
            [
                remote(part_ref.at[4 + i, rank ^ r, p], frecv_ref.at[i, rank ^ r, p], far_sem.at[i, k, r], far)
                for r in range(ranks)
            ]
            for k, p in enumerate((opp, par))
        ]
        for i in range(2)
    ]
    out_out = [
        remote(
            out_ref.at[pl.ds(slots + i * half_rows, half_rows), :],
            outin_ref.at[pl.ds(i * half_rows, half_rows), :], out_sem.at[i], far,
        )
        for i in range(2)
    ]
    xf_out = [None] + [remote(fsum_ref.at[rank ^ r, opp], xfrecv_ref.at[r], xf_sem.at[r], side) for r in range(1, ranks)]
    some = chunk // 2
    xf_last = [
        remote(
            fsum_ref.at[rank, opp, pl.ds(k * some, some), :], xfrecv_ref.at[0, pl.ds(k * some, some), :],
            xf_sem.at[k * ranks], side,
        )
        for k in range(2)
    ]
    low_bit = lambda r: r & -r
    zf_out = [None] + [
        remote(xfrecv_ref.at[r], zfrecv_ref.at[r - 1], zf_sem.at[r - 1], peer(low_bit(r))) for r in range(1, ranks)
    ]
    feeds = lambda r: [r | (1 << b) for b in range(ranks.bit_length() - 1) if (1 << b) < (low_bit(r) if r else ranks)]
    xa_out = [
        [remote(part_ref.at[i, rank ^ r, opp], xarecv_ref.at[i, r], xa_sem.at[i, r], side) for r in range(ranks)]
        for i in range(2)
    ]
    za_out = [
        [None]
        + [
            remote(part_ref.at[i, rank ^ r, par], zarecv_ref.at[i, r - 1], za_sem.at[i, r - 1], peer(low_bit(r)))
            for r in range(1, ranks)
        ]
        for i in range(2)
    ]
    sn_out = [
        remote(nsend_ref.at[r], nrecv_ref.at[r - 1], sn_sem.at[r - 1], dev) for r, dev in ((1, core), (2, far), (3, diag))
    ]
    ss_out = [None] + [
        remote(parts_ref.at[w ^ k], srecv_ref.at[k - 1], ss_sem.at[k - 1], (w ^ k, n)) for k in range(1, wide)
    ]

    def at_edge(end, middle):
        edge = ((rank ^ (rank >> 1)) & 1) == 0
        pl.when(edge)(lambda: end())
        pl.when(jnp.logical_not(edge))(lambda: middle())

    def e_in(k):
        s = slot_of(k)
        return pltpu.make_async_copy(e_ref.at[s], ds_ref.at[s], e_sem.at[k & 1])

    def wide_f32(ref_value):
        return ref_value.astype(F32)

    @pl.when(u == 0)
    def _():
        e_in(0).start()
        for copy in [fown_in] + ins + [gm_in]:
            copy.start()
        greet([core, far, diag] + [(w ^ k, n) for k in range(1, wide)])
        if ranks == 4:
            xf_out[3].start()
            at_edge(xf_out[1].start, xf_out[2].start)
            at_edge(xf_out[2].start, xf_out[1].start)
        else:
            for r in range(ranks - 1, 0, -1):
                xf_out[r].start()
        out_out[0].start()
        x = x_ref[...].astype(F32)
        inv = lax.rsqrt(jnp.mean(x * x, axis=-1, keepdims=True) + EPS)
        nt_ref[...] = (x * inv * gain_ref[...].astype(F32)[None]).astype(BF).T
        gat_ref[...] = ga_ref[...].T
        dx_ref[...] = jnp.zeros_like(dx_ref)
        acc_ref[...] = jnp.zeros_like(acc_ref)
        parts_ref[...] = jnp.zeros_like(parts_ref)

    @pl.when(u < 8)
    def _():
        e_in(u).wait()

        @pl.when(u < 7)
        def _():
            e_in(u + 1).start()

        lane = lax.broadcasted_iota(I32, (slots, pw), 1)
        low = lane < HEAD_DIM
        do2 = (lax.dot_general(ga_ref[...], wo_ref[...], NT, preferred_element_type=F32) * linv_ref[...]).astype(BF)
        prod = do2.astype(F32) * ctx_ref[...].astype(F32)
        q2, k2, v2 = qkv_ref[0], qkv_ref[1], qkv_ref[2]
        vx = jnp.concatenate([v2, jnp.where(lane < 2, 1.0, 0.0).astype(BF)], axis=1)
        do_t, q_t = do2.T, q2.T
        zero = jnp.zeros_like(do2)
        dq, dk, dv = [], [], []
        for sub in range(2):
            mine = low if sub == 0 else jnp.logical_not(low)
            row = -jnp.sum(jnp.where(mine, prod, 0.0), axis=1, keepdims=True)
            head_part = row.astype(BF).astype(F32)
            extra = jnp.where(lane == 0, head_part, jnp.where(lane == 1, row - head_part, 0.0)).astype(BF)
            dox = jnp.concatenate([jnp.where(mine, do2, zero), extra], axis=1)
            t = lax.dot_general(dox, vx, NT, preferred_element_type=F32)
            e = ds_ref[slot, sub]
            ds = (e.astype(F32) * t).astype(BF)
            dv.append(jnp.dot(do_t[sub * HEAD_DIM : (sub + 1) * HEAD_DIM], e, preferred_element_type=F32))
            ds_ref[slot, sub] = ds
            dk.append(jnp.dot(q_t[sub * HEAD_DIM : (sub + 1) * HEAD_DIM], ds, preferred_element_type=F32))
            dq.append(jnp.dot(ds, k2, preferred_element_type=F32))
        joined = jnp.concatenate(
            [
                jnp.where(low, dq[0], dq[1]).astype(BF),
                jnp.concatenate(dk, axis=0).T.astype(BF),
                jnp.concatenate(dv, axis=0).T.astype(BF),
            ],
            axis=1,
        )
        weights = jnp.concatenate([wall_ref[m] for m in range(3)], axis=1)
        dx_ref[...] += lax.dot_general(joined, weights, NT, preferred_element_type=F32)
        part = jnp.dot(nt_ref[...], joined, preferred_element_type=F32).astype(BF)
        part_ref[slot, :, :, :, : 3 * pw] = part.reshape(ranks, 2, chunk, 3 * pw)
        part = jnp.dot(gat_ref[...], ctx_ref[...], preferred_element_type=F32).astype(BF)
        part_ref[slot, :, :, :, 3 * pw :] = part.reshape(ranks, 2, chunk, pw)

    @pl.when(u >= 8)
    def _():
        blk = 16
        one, zero = jnp.ones((blk, 4 * slots), BF), jnp.zeros((blk, 4 * slots), BF)

        @pl.when(u == 8)
        def _():
            for copy in ins:
                copy.wait()

        group = 4

        def sub_block(c, carry):
            starts = [pl.multiple_of((u - 8) * trows + (c * group + k) * blk, blk) for k in range(group)]
            g = jnp.concatenate(
                [
                    jnp.concatenate([ds_ref[s, sub, pl.ds(at, blk), :] for s in range(8) for sub in range(2)], axis=0)
                    for at in starts
                ],
                axis=1,
            )
            for t in range(3):
                ids = jnp.concatenate([ids_ref[t, pl.ds(at, blk), :].astype(F32).astype(BF) for at in starts], axis=1)
                hot = jnp.concatenate([jnp.where(ids == jnp.bfloat16(b), one, zero) for b in range(buckets)], axis=0)
                span = slice(t * buckets * blk, (t + 1) * buckets * blk)
                acc_ref[span, :] += lax.dot_general(hot, g, NT, preferred_element_type=F32)
            return carry

        lax.fori_loop(0, trows // (blk * group), sub_block, 0)

    def event(step):
        return lambda body: pl.when(u == step)(body)

    def core_stage(i):
        core_out[i].wait_recv()
        for p in (opp, par):
            total = wide_f32(part_ref[4 + i, :, p]) + wide_f32(crecv_ref[i, :, p])
            part_ref[4 + i, :, p] = total.astype(BF)
        for r in order:
            far_out[i][0][r].start()

    def own_sides():
        for i in range(2):
            for r in order:
                far_out[i][1][r].start()

    def far_stage(i):
        core_out[2 + i].wait_recv()
        for r in order:
            far_out[i][0][r].wait_recv()
            k = rank ^ r
            total = wide_f32(part_ref[i, k, opp]) + wide_f32(crecv_ref[2 + i, k, opp]) + wide_f32(frecv_ref[i, k, opp])
            part_ref[i, k, opp] = total.astype(BF)
            xa_out[i][r].start()

    def side_stage(i, r):
        far_out[i][1][r].wait_recv()
        xa_out[i][r].wait_recv()
        k = rank ^ r
        total = wide_f32(part_ref[i, k, par]) + wide_f32(crecv_ref[2 + i, k, par])
        total = total + wide_f32(frecv_ref[i, k, par]) + wide_f32(xarecv_ref[i, r])
        part_ref[i, k, par] = total.astype(BF)
        if r & 1:
            za_out[i][r].start()

    def rank_stage(i, r):
        total = wide_f32(part_ref[i, rank ^ r, par])
        for k in feeds(r):
            za_out[i][k].wait_recv()
            total = total + wide_f32(zarecv_ref[i, k - 1])
        if r == 0:
            return total
        part_ref[i, rank ^ r, par] = total.astype(BF)
        za_out[i][r].start()

    def ffn_stage(r):
        for copy in xf_last if r == 0 else [xf_out[r]]:
            copy.wait_recv()
        total = wide_f32(fown_ref[rank ^ r]) + wide_f32(xfrecv_ref[r])
        for k in feeds(r):
            zf_out[k].wait_recv()
            total = total + wide_f32(zfrecv_ref[k - 1])
        if r == 0:
            return total
        xfrecv_ref[r] = total.astype(BF)
        zf_out[r].start()

    def input_gradient():
        gm_in.wait()
        x = x_ref[...].astype(F32)
        inv = lax.rsqrt(jnp.mean(x * x, axis=-1, keepdims=True) + EPS)
        upstream = dx_ref[...]
        lifted = upstream * gain_ref[...].astype(F32)[None]
        inner = jnp.mean(lifted * x, axis=-1, keepdims=True)
        gib_ref[...] = gib_ref[...] + inv * lifted - x * (inv * inv * inv * inner)
        gi_out.start()
        gains = jnp.sum(upstream * x * inv, axis=0, keepdims=True)
        lanes = d // LANES
        for r in range(4):
            for j in range(lanes):
                span = slice(j * LANES, (j + 1) * LANES)
                nsend_ref[r, 3 * buckets + j : 3 * buckets + j + 1, :] = gains[:, span]
                nsend_ref[r, 3 * buckets + lanes + j : 3 * buckets + lanes + j + 1, :] = gain2_ref[:, span]

    plan = [[] for _ in range(steps)]
    for i in range(2):
        plan[2 * i].append(core_out[i].start)
        plan[2 * i + 1].append(functools.partial(core_stage, i))
        plan[4 + i].append(core_out[2 + i].start)
    plan[3].append(own_sides)
    plan[1].append(fown_in.wait)
    if ranks == 4:
        turn = lambda a, b: functools.partial(at_edge, functools.partial(ffn_stage, a), functools.partial(ffn_stage, b))
        plan[2].append(functools.partial(ffn_stage, 3))
        plan[5].append(turn(1, 2))
        plan[8].append(turn(2, 1))
    else:
        for k, r in enumerate(range(ranks - 1, 0, -1)):
            plan[3 + k * 6 // ranks].append(functools.partial(ffn_stage, r))
    plan[6].append(functools.partial(far_stage, 0))
    plan[7].append(input_gradient)
    plan[8].append(functools.partial(far_stage, 1))
    plan[8].append(xf_last[0].start)
    plan[12].extend(functools.partial(side_stage, 0, r) for r in order)
    plan[15].extend(functools.partial(rank_stage, 0, r) for r in range(ranks - 2, 0, -2))
    for k in range(steps):

        @pl.when(u == k)
        def _():
            for action in plan[k]:
                action()

    @pl.when(u == steps - 1)
    def _():
        blk, cols = 16, 16 * 16
        same = lax.broadcasted_iota(I32, (blk, cols), 0) == (lax.broadcasted_iota(I32, (blk, cols), 1) & (blk - 1))
        picked = [
            jnp.sum(jnp.where(same, acc_ref[b * blk : (b + 1) * blk, :], 0.0), axis=0, keepdims=True)
            for b in range(3 * buckets)
        ]
        picked = jnp.concatenate(picked, axis=0)
        source = lax.broadcasted_iota(I32, (cols, LANES), 0) >> 4
        target = lax.broadcasted_iota(I32, (cols, LANES), 1)
        choose = jnp.where(source == target, 1.0, 0.0).astype(F32)
        sums = jnp.dot(picked, choose, preferred_element_type=F32, precision=lax.Precision.HIGHEST)
        for r in range(4):
            nsend_ref[r, : 3 * buckets, :] = pltpu.roll(sums, LANES - heads * r, 1) if r else sums
        for copy in sn_out + out_out[1:]:
            copy.start()

        def finish(i):
            total = rank_stage(i, 0)
            cols = slice(i * pw, (i + 1) * pw)
            gq_ref[:, cols] = total[:, :pw]
            gk_ref[:, cols] = total[:, pw : 2 * pw]
            gv_ref[:, cols] = total[:, 2 * pw : 3 * pw]
            go_ref[cols, :] = total[:, 3 * pw :].T

        for r in order[:-1]:
            side_stage(1, r)
        for copy in sn_out:
            copy.wait()
        nsend_ref[1] = nsend_ref[0] + nrecv_ref[0] + nrecv_ref[1] + nrecv_ref[2]
        lanes, own = d // LANES, buckets // wide
        for k in range(wide):
            row = 3 * buckets + k * d // wide // LANES
            parts_ref[k, 0:1, :] = nsend_ref[1, row : row + 1, :]
            parts_ref[k, 1:2, :] = nsend_ref[1, row + lanes : row + lanes + 1, :]
            for t in range(3):
                at = t * buckets + k * own
                parts_ref[k, 2 + t * own : 2 + (t + 1) * own, :] = nsend_ref[1, at : at + own, :]
        for copy in ss_out[1:]:
            copy.start()
        xf_last[1].start()
        side_stage(1, 0)
        finish(0)
        for r in range(ranks - 2, 0, -2):
            rank_stage(1, r)
        total = ffn_stage(0)
        full, rest = split_quarter(ff)
        for m, ref in enumerate((fg_ref, fu_ref, fd_ref)):
            ref[:full, :] = total[:, m * full : (m + 1) * full].T
            if rest:
                ref[full:, :] = total[:, 3 * full + m * rest : 3 * full + (m + 1) * rest].T
        total = parts_ref[w]
        for k in range(1, wide):
            ss_out[k].wait_recv()
            total = total + srecv_ref[k - 1]
        small_ref[...] = total
        finish(1)
        gi_out.wait()
        for copy in out_out:
            copy.wait()
        for i in range(2):
            for copy in far_out[i][0] + far_out[i][1] + xa_out[i] + za_out[i][1:]:
                copy.wait_send()
        for copy in core_out + xf_out[1:] + xf_last + zf_out[1:] + ss_out[1:]:
            copy.wait_send()


def backward(wide, buckets, ff, ga, x, gain, gain2, fsum, gm, e, ids, out, wo_all, ctx, linv, qkv, w_all, trows=64):
    slots, d = x.shape
    heads = 4
    pw = 2 * HEAD_DIM
    ranks, chunk = wide // 2, d // wide
    packed = fsum.shape[-1]
    width = heads * HEAD_DIM
    small = 3 * buckets + 2 * d // LANES
    place = -(-(2 + 3 * (buckets // wide)) // 8) * 8
    vmem, anywhere = pl.BlockSpec(memory_space=pltpu.VMEM), pl.BlockSpec(memory_space=pl.ANY)
    shape = jax.ShapeDtypeStruct
    dma = pltpu.SemaphoreType.DMA

    def slot(u):
        return backward_slot(jnp.minimum(u, 7))

    return pl.pallas_call(
        functools.partial(backward_kernel, wide, heads, buckets, trows, ff),
        grid=(8 + slots // trows,),
        in_specs=[vmem] * 4 + [anywhere] * 7 + [
            pl.BlockSpec((pw, d), lambda u: (slot(u), 0)),
            pl.BlockSpec((slots, pw), lambda u: (0, slot(u))),
            pl.BlockSpec((slots, pw), lambda u: (0, slot(u))),
            pl.BlockSpec((3, slots, pw), lambda u: (0, 0, slot(u))),
            pl.BlockSpec((3, d, pw), lambda u: (0, 0, slot(u))),
        ],
        out_specs=[anywhere] * 2 + [vmem] * 8,
        out_shape=[
            shape((slots, d), F32),
            shape((slots, d), BF),
            shape((place, LANES), F32),
            shape((chunk, width), F32),
            shape((chunk, width), F32),
            shape((chunk, width), F32),
            shape((width, chunk), F32),
            shape((ff, chunk), F32),
            shape((ff, chunk), F32),
            shape((ff, chunk), F32),
        ],
        scratch_shapes=[
            pltpu.VMEM((slots, d), F32),
            pltpu.VMEM((ranks, chunk, packed), BF),
            pltpu.VMEM((8, 2, slots, slots), BF),
            pltpu.VMEM((3, slots, slots), I32),
            pltpu.VMEM((d, slots), BF),
            pltpu.VMEM((d, slots), BF),
            pltpu.VMEM((slots, d), F32),
            pltpu.VMEM((3 * buckets * 16, 16 * 16), F32),
            pltpu.VMEM((8, ranks, 2, chunk, 4 * pw), BF),
            pltpu.VMEM((4, ranks, 2, chunk, 4 * pw), BF),
            pltpu.VMEM((2, ranks, 2, chunk, 4 * pw), BF),
            pltpu.VMEM((2, ranks, chunk, 4 * pw), BF),
            pltpu.VMEM((2, ranks - 1, chunk, 4 * pw), BF),
            pltpu.VMEM((ranks, chunk, packed), BF),
            pltpu.VMEM((ranks - 1, chunk, packed), BF),
            pltpu.VMEM((4, small, LANES), F32),
            pltpu.VMEM((3, small, LANES), F32),
            pltpu.VMEM((wide, place, LANES), F32),
            pltpu.VMEM((wide - 1, place, LANES), F32),
            dma((6,)), dma((2,)), dma((4, 2)), dma((2, 2, ranks, 2)), dma((2, 2)), dma((ranks + 1, 2)), dma((ranks - 1, 2)),
            dma((2, ranks, 2)), dma((2, ranks - 1, 2)), dma((3, 2)), dma((wide - 1, 2)),
        ],
        compiler_params=pltpu.CompilerParams(
            vmem_limit_bytes=VMEM_LIMIT, collective_id=3, has_side_effects=True
        ),
        cost_estimate=pl.CostEstimate(flops=30 * slots * d * d, bytes_accessed=60 << 20, transcendentals=0),
        name="backward",
    )(ga, x, gain, gain2, fsum, gm, e, *ids, out, wo_all, ctx, linv, qkv, w_all)


def results_kernel(
    wide, narrow, buckets, heads, middle_ref, out_ref, outin_ref, gi_ref, small_ref, *rest,
):
    sources, (block_ref, go_ref, ga_ref, gf_ref, tr_ref, th_ref, tv_ref), targets = rest[:7], rest[7:14], rest[14:]
    block_ref[...] = (middle_ref[...] + (out_ref[...].astype(F32) + outin_ref[...].astype(F32))).astype(BF)
    go_ref[...] = gi_ref[...]

    @pl.when(pl.program_id(0) == 0)
    def _():
        for a, b in zip(sources, targets):
            b[...] = a[...]
        w, n = lax.axis_index("wide"), lax.axis_index("narrow")
        d = middle_ref.shape[1]
        per, own = d // (wide * narrow), buckets // wide
        start = (w * narrow + n) * per
        for k, ref in enumerate((ga_ref, gf_ref)):
            row = small_ref[k : k + 1, :]
            lane = lax.broadcasted_iota(I32, (per, LANES), 1)
            mine = lane == lax.broadcasted_iota(I32, (per, LANES), 0) + start % LANES
            ref[...] = jnp.sum(jnp.where(mine, jnp.broadcast_to(row, (per, LANES)), 0.0), axis=1)
        for k, ref in enumerate((tr_ref, th_ref, tv_ref)):
            ref[...] = small_ref[2 + k * own : 2 + (k + 1) * own, :heads]


def results(wide, narrow, buckets, heads, middle, out, outin, small, grad_input, big):
    slots, d = middle.shape
    shape = jax.ShapeDtypeStruct
    per, own = d // (wide * narrow), buckets // wide
    rows = pl.BlockSpec((slots // 4, d), lambda i: (i, 0))
    whole = lambda *sh: pl.BlockSpec(sh, lambda i: (0,) * len(sh))
    return pl.pallas_call(
        functools.partial(results_kernel, wide, narrow, buckets, heads),
        grid=(4,),
        in_specs=[rows] * 4 + [whole(*small.shape)] + [whole(*x.shape) for x in big],
        out_specs=[rows] * 2 + [whole(per)] * 2 + [whole(own, heads)] * 3 + [whole(*x.shape) for x in big],
        out_shape=[shape((slots, d), BF), shape((slots, d), F32)] + [shape((per,), F32)] * 2
        + [shape((own, heads), F32)] * 3 + [shape(x.shape, x.dtype) for x in big],
        compiler_params=pltpu.CompilerParams(vmem_limit_bytes=VMEM_LIMIT),
        name="results",
    )(middle, out, outin, grad_input, small, *big)


def shards(
    wide, narrow, hidden_in, grad_out, gain_attn, gain_ffn, w_query, w_key, w_value, w_output,
    table_rel, table_horiz, table_vert, wi_gate, wi_up, wo_ffn, counts, patch_mask,
    bucket_rel, bucket_horiz, bucket_vert,
):
    slots = bucket_rel.shape[1]
    rows, d = hidden_in.shape
    buckets, heads = table_rel.shape
    width = w_query.shape[1]
    ff = wi_gate.shape[1]
    assert rows == slots and narrow == 4 and wide >= 4 and heads * HEAD_DIM == width
    ids = (bucket_rel, bucket_horiz, bucket_vert)

    qkv, exps, context, linv, w_all, wo_all, middle, ffn_own, grad_far, wg_core, wu_core, wd_core = forward(
        counts, patch_mask, hidden_in, gain_attn, gain_ffn, (table_rel.T, table_horiz.T, table_vert.T),
        w_query, w_key, w_value, w_output, ids, grad_out, wi_gate.T, wi_up.T, wo_ffn,
    )
    out, ffn_sum, grad_middle, grad_attn, grad_gain_second = feed_forward(
        ffn_own, grad_out, grad_far, middle, gain_ffn,
        (wi_gate.T, wi_up.T, wo_ffn), (wg_core, wu_core, wd_core),
    )
    grad_input, out_in, small, gq, gk, gv, go, fg, fu, fd = backward(
        wide, buckets, ff, grad_attn, hidden_in, gain_attn, grad_gain_second,
        ffn_sum.reshape(wide // 2, 2, d // wide, -1), grad_middle, exps, ids, out,
        wo_all, context, linv, qkv, w_all,
    )
    block_out, grad_input, gain1, gain2, rel, horiz, vert, gq, gk, gv, go, fg, fu, fd = results(
        wide, narrow, buckets, heads, middle, out, out_in, small, grad_input, (gq, gk, gv, go, fg, fu, fd)
    )
    return (
        block_out, grad_input, gain1, gain2, gq, gk, gv, go, rel, horiz, vert, fg.T, fu.T, fd,
    )


def solution(mesh):
    rows, both = P(("wide", "narrow"), None), P(("wide", "narrow"))
    cols, across = P(None, "narrow"), P("narrow", None)
    grid, turned = P("wide", "narrow"), P("narrow", "wide")
    pages = P("wide", None, None)
    return jax.shard_map(
        functools.partial(shards, mesh.shape["wide"], mesh.shape["narrow"]),
        mesh=mesh,
        in_specs=(
            rows, rows, P(), P(), cols, cols, cols, across, cols, cols, cols, cols, cols, across,
            P("wide"), P("wide", None), pages, pages, pages,
        ),
        out_specs=(
            rows, rows, both, both, grid, grid, grid, turned, grid, grid, grid, grid, grid, turned,
        ),
        check_vma=False,
    )
```

```python
import functools
import math

import jax
import jax.numpy as jnp
from jax import lax
from jax.experimental import pallas as pl
from jax.experimental.pallas import tpu as pltpu
from jax.sharding import PartitionSpec as P

F32 = jnp.float32
BF = jnp.bfloat16
I32 = jnp.int32
HEAD_DIM = 64
LANES = 128
EPS = 1e-06
NT = (((1,), (1,)), ((), ()))

FIXED = 2048.0
OFFSET = 8192
MASKED = -3.0e12
VMEM_LIMIT = 60 << 20
MESH = pl.DeviceIdType.MESH


def lookup(table_row, ids):
    return jnp.take_along_axis(table_row, ids, axis=1, mode="promise_in_bounds")


def neighbours():
    w, n = lax.axis_index("wide"), lax.axis_index("narrow")
    return w, n, (w, n ^ 1), (w, n ^ 2), (w, n ^ 3), (w ^ 1, n)


def greet(devices):
    barrier = pltpu.get_barrier_semaphore()
    for device in devices:
        pl.semaphore_signal(barrier, inc=1, device_id=device, device_id_type=MESH)
    pl.semaphore_wait(barrier, len(devices))


def remote(src, dst, sems, device):
    return pltpu.make_async_remote_copy(
        src_ref=src, dst_ref=dst, send_sem=sems.at[0], recv_sem=sems.at[1], device_id=device, device_id_type=MESH
    )


def forward_kernel(
    heads, buckets, chunk,
    counts_ref, patch_ref, x_ref, gain1_ref, gain2_ref, tr_ref, th_ref, tv_ref,
    wq_ref, wk_ref, wv_ref, wo_ref, ir_ref, ih_ref, iv_ref, go_ref, wg_ref, wu_ref, wd_ref,
    qkv_to, e_ref, ctx_to, linv_to, wall_to, woall_to, middle_ref, ffn_ref, gofar_ref, wgc_ref, wuc_ref, wdc_ref,
    qkv_ref, ctx_ref, linv_ref, wall_ref, woall_ref, normed_ref, mask_ref, ids_ref, tab_ref, tabs_ref, words_ref, ebuf_ref,
    own_sem, id_sem, e_sem, core_sem, far_sem, deep_sem, wide_sem, fwd_sem, tab_sem, big_sem, leave_sem,
):
    pw = 2 * HEAD_DIM
    slots, d = x_ref.shape
    piece = d // 2
    w, n, core, far, diag, side = neighbours()
    deep = (w ^ 2, n)
    half, share = w & 1, (w >> 1) & 1
    other = 1 - half

    def source(m, pair, part=None):
        cols = pl.ds(pl.multiple_of(pair * pw, pw), pw)
        span = slice(None) if part is None else pl.ds(pl.multiple_of(part * piece, piece), piece)
        return wo_ref.at[cols, span] if m == 3 else (wq_ref, wk_ref, wv_ref)[m].at[span, cols]

    def place(m, slot, part=None):
        cols = pl.ds(pl.multiple_of(slot * pw, pw), pw)
        span = slice(None) if part is None else pl.ds(pl.multiple_of(part * piece, piece), piece)
        return woall_ref.at[cols, span] if m == 3 else wall_ref.at[m, span, cols]

    ids_in = [pltpu.make_async_copy(r.at[n], ids_ref.at[t], id_sem.at[t]) for t, r in enumerate((ir_ref, ih_ref, iv_ref))]
    own_in = [[pltpu.make_async_copy(source(m, p), place(m, p), own_sem.at[p, m]) for m in range(4)] for p in range(2)]
    for copy in own_in[0][:3] + ids_in + own_in[0][3:] + own_in[1]:
        copy.start()

    tab_ref[...] = jnp.zeros_like(tab_ref)
    for t, r in enumerate((tr_ref, th_ref, tv_ref)):
        tab_ref[t * heads : (t + 1) * heads, :buckets] = jnp.floor(r[...].astype(F32) * FIXED + 0.5)

    greet((core, far, diag, side, deep))
    far_out = [remote(source(m, half, share), place(m, 4 + half, share), far_sem.at[m], far) for m in range(4)]
    deep_out = [remote(place(m, 4 + half, share), place(m, 4 + half, share), deep_sem.at[m], deep) for m in range(4)]
    core_out = [[remote(source(m, p), place(m, 2 + p), core_sem.at[p, m], core) for m in range(4)] for p in range(2)]
    tabs_out = [remote(tab_ref, tabs_ref.at[r - 1], tab_sem.at[r - 1], dev) for r, dev in ((1, core), (2, far), (3, diag))]
    wide_out = [
        [remote(place(m, 4 + half, k), place(m, 4 + half, k), wide_sem.at[m, i], side) for i, k in enumerate((share, 1 - share))]
        for m in range(4)
    ]
    fwd_out = [
        [remote(place(m, 4 + half, k), place(m, 6 + half, k), fwd_sem.at[m, i], core) for i, k in enumerate((share, 1 - share))]
        for m in range(4)
    ]
    last_out = [remote(place(m, 4 + other), place(m, 6 + other), fwd_sem.at[m, 2], core) for m in range(4)]
    go_out = remote(go_ref, gofar_ref, big_sem.at[0], far)
    ffn_out = [
        remote(wg_ref, wgc_ref, big_sem.at[1], core),
        remote(wu_ref, wuc_ref, big_sem.at[2], core),
        remote(wd_ref, wdc_ref, big_sem.at[3], core),
    ]
    for copy in tabs_out + far_out + [go_out] + core_out[0] + core_out[1]:
        copy.start()

    x = x_ref[...].astype(F32)
    inv = lax.rsqrt(jnp.mean(x * x, axis=-1, keepdims=True) + EPS)
    normed_ref[...] = (x * inv * gain1_ref[...].astype(F32)[None]).astype(BF)
    text = slots - patch_ref.shape[1]
    shown = jnp.concatenate(
        [
            jnp.where(lax.broadcasted_iota(I32, (1, text), 1) < counts_ref[n], 1, 0),
            patch_ref[pl.ds(n, 1), :],
        ],
        axis=1,
    )
    column = jnp.broadcast_to(jnp.where(shown == 1, 0.0, MASKED), (pw, slots)).T
    lane_all = lax.broadcasted_iota(I32, (slots, pw), 1)
    mask_ref[...] = jnp.where(lane_all == 0, column, 0.0).astype(BF)
    ones = jnp.ones((slots, pw), BF)
    lane = lax.broadcasted_iota(I32, (chunk, pw), 1)
    low = lane < HEAD_DIM
    first = jnp.where(lane == 0, 1.0, 0.0).astype(BF)
    to_log2 = math.log2(math.e) / FIXED

    def pack_words(r, table):
        fixed = table.astype(I32)
        for p in range(2):
            for t in range(3):
                row = t * heads + 2 * p
                words_ref[2 * r + p, t : t + 1, :] = fixed[row + 1 : row + 2] * 65536 + fixed[row : row + 1] + OFFSET

    pack_words(0, tab_ref[...])
    for copy in ids_in:
        copy.wait()

    def e_out(parity, slot):
        return pltpu.make_async_copy(ebuf_ref.at[parity], e_ref.at[slot], e_sem.at[parity])

    def leaving(slot):
        cols = pl.ds(pl.multiple_of(slot * pw, pw), pw)
        pairs = (
            (wall_ref.at[:, :, cols], wall_to.at[:, :, cols]),
            (qkv_ref.at[:, :, cols], qkv_to.at[:, :, cols]),
            (ctx_ref.at[:, cols], ctx_to.at[:, cols]),
            (linv_ref.at[:, cols], linv_to.at[:, cols]),
        )
        return [pltpu.make_async_copy(a, b, leave_sem.at[k, slot]) for k, (a, b) in enumerate(pairs)]

    def slot_of(t):
        late = 4 + 2 * (t & 1) + jnp.where(t >= 6, other, half)
        return jnp.where(t < 4, t, late)

    plan = [[] for _ in range(16)]

    def far_arrived(m):
        far_out[m].wait_recv()
        deep_out[m].start()
        wide_out[m][0].start()
        fwd_out[m][0].start()

    def deep_arrived(m):
        deep_out[m].wait_recv()
        wide_out[m][1].start()
        fwd_out[m][1].start()

    def wide_arrived(m):
        for copy in wide_out[m]:
            copy.wait_recv()
        last_out[m].start()

    def tables_arrived():
        for r, copy in enumerate(tabs_out):
            copy.wait()
            pack_words(r + 1, tabs_ref[r])

    for p in range(2):
        plan[2 * p].extend(own_in[p][m].wait for m in range(3))
        plan[4 + 2 * p].extend(core_out[p][m].wait_recv for m in range(3))
    plan[3].append(tables_arrived)
    for m in range(4):
        plan[2 + m].append(functools.partial(far_arrived, m))
        plan[4 + m].append(functools.partial(deep_arrived, m))
    plan[7].extend(copy.start for copy in ffn_out)
    plan[10].extend(copy.wait_recv for m in range(3) for copy in fwd_out[m])
    plan[12].extend(functools.partial(wide_arrived, m) for m in range(3))
    plan[14].extend(last_out[m].wait_recv for m in range(3))
    plan[14].append(functools.partial(wide_arrived, 3))

    def events(t, c):
        for k in range(8):
            if plan[2 * k + c]:

                @pl.when(t == k)
                def _():
                    for action in plan[2 * k + c]:
                        action()

    def step(t, carry):
        slot = slot_of(t)
        events(t, 0)
        parity = t & 1

        @pl.when(t >= 2)
        def _():
            e_out(parity, slot).wait()

        cols = pl.ds(pl.multiple_of(slot * pw, pw), pw)
        weights = jnp.concatenate([wall_ref[m, :, cols] for m in range(3)], axis=1)
        joined = jnp.dot(normed_ref[...], weights, preferred_element_type=F32).astype(BF)
        for m in range(3):
            qkv_ref[m, :, cols] = joined[:, m * pw : (m + 1) * pw]
        kx = jnp.concatenate([joined[:, pw : 2 * pw], mask_ref[...]], axis=1)
        vx = jnp.concatenate([joined[:, 2 * pw :], ones], axis=1)
        words = words_ref[slot]
        for c in range(slots // chunk):
            if c == slots // chunk // 2:
                events(t, 1)
            rows = slice(c * chunk, (c + 1) * chunk)
            q2 = joined[rows, :pw] * jnp.bfloat16(FIXED)
            zero = jnp.zeros_like(q2)
            scores = []
            for sub in range(2):
                q = jnp.where(low, q2, zero) if sub == 0 else jnp.where(low, zero, q2)
                q = jnp.concatenate([q, first], axis=1)
                scores.append(lax.dot_general(q, kx, NT, preferred_element_type=F32))
            tabs = [jnp.broadcast_to(words[k : k + 1, :], (chunk, LANES)) for k in range(3)]
            parts = ([], [])
            for j in range(slots // LANES):
                sl = slice(j * LANES, (j + 1) * LANES)
                bias = (
                    lookup(tabs[0], ids_ref[0, rows, sl])
                    + lookup(tabs[1], ids_ref[1, rows, sl])
                    + lookup(tabs[2], ids_ref[2, rows, sl])
                )
                parts[0].append(scores[0][:, sl] + (bias & 0xFFFF).astype(F32))
                parts[1].append(scores[1][:, sl] + (bias >> 16).astype(F32))
            outs = []
            for sub in range(2):
                s = jnp.concatenate(parts[sub], axis=1)
                peak = jnp.max(s, axis=1, keepdims=True)
                e = jnp.exp2((s - peak) * to_log2).astype(BF)
                ebuf_ref[parity, sub, rows, :] = e
                outs.append(jnp.dot(e, vx, preferred_element_type=F32))
            linv = 1.0 / jnp.where(low, outs[0][:, pw:], outs[1][:, pw:])
            linv_ref[rows, cols] = linv
            ctx_ref[rows, cols] = (jnp.where(low, outs[0][:, :pw], outs[1][:, :pw]) * linv).astype(BF)
        e_out(parity, slot).start()
        for copy in leaving(slot):
            copy.start()
        return carry

    lax.fori_loop(0, 8, step, 0)
    for p in range(2):
        own_in[p][3].wait()
        core_out[p][3].wait_recv()
    for copy in fwd_out[3] + last_out[3:]:
        copy.wait_recv()
    wo_leaving = pltpu.make_async_copy(woall_ref, woall_to, id_sem.at[0])
    wo_leaving.start()
    middle = x_ref[...].astype(F32) + jnp.dot(ctx_ref[...], woall_ref[...], preferred_element_type=F32)
    middle_ref[...] = middle
    inv = lax.rsqrt(jnp.mean(middle * middle, axis=-1, keepdims=True) + EPS)
    ffn_ref[...] = (middle * inv * gain2_ref[...].astype(F32)[None]).astype(BF)
    for p in range(2):
        e_out(p, p).wait()
        for m in range(4):
            core_out[p][m].wait_send()
    for m in range(4):
        for copy in [far_out[m], deep_out[m], last_out[m]] + wide_out[m] + fwd_out[m]:
            copy.wait_send()
    for copy in ffn_out:
        copy.wait()
    for slot in range(8):
        for copy in leaving(slot):
            copy.wait()
    wo_leaving.wait()
    go_out.wait()


def forward(counts, patches, x, gain1, gain2, tables, wq, wk, wv, wo, ids, grad_out, wg, wu, wd, chunk=256):
    slots, d = x.shape
    heads = wq.shape[1] // HEAD_DIM
    buckets = tables[0].shape[1]
    ff = wd.shape[0]
    assert heads == 4
    vmem, anywhere = pl.BlockSpec(memory_space=pltpu.VMEM), pl.BlockSpec(memory_space=pl.ANY)
    shape = jax.ShapeDtypeStruct
    dma = pltpu.SemaphoreType.DMA
    return pl.pallas_call(
        functools.partial(forward_kernel, heads, buckets, chunk),
        in_specs=[pl.BlockSpec(memory_space=pltpu.SMEM)] + [vmem] * 7 + [anywhere] * 11,
        out_specs=[anywhere] * 6 + [vmem] * 2 + [anywhere] * 4,
        out_shape=[
            shape((3, slots, d), BF),
            shape((8, 2, slots, slots), BF),
            shape((slots, d), BF),
            shape((slots, d), F32),
            shape((3, d, d), BF),
            shape((d, d), BF),
            shape((slots, d), F32),
            shape((slots, d), BF),
            shape((slots, d), BF),
            shape((ff, d), BF),
            shape((ff, d), BF),
            shape((ff, d), BF),
        ],
        scratch_shapes=[
            pltpu.VMEM((3, slots, d), BF),
            pltpu.VMEM((slots, d), BF),
            pltpu.VMEM((slots, d), F32),
            pltpu.VMEM((3, d, d), BF),
            pltpu.VMEM((d, d), BF),
            pltpu.VMEM((slots, d), BF),
            pltpu.VMEM((slots, 2 * HEAD_DIM), BF),
            pltpu.VMEM((3, slots, slots), I32),
            pltpu.VMEM((16, LANES), F32),
            pltpu.VMEM((3, 16, LANES), F32),
            pltpu.VMEM((8, 8, LANES), I32),
            pltpu.VMEM((2, 2, slots, slots), BF),
            dma((2, 4)), dma((3,)), dma((2,)), dma((2, 4, 2)), dma((4, 2)), dma((4, 2)), dma((4, 2, 2)), dma((4, 3, 2)),
            dma((3, 2)), dma((4, 2)), dma((4, 8)),
        ],
        compiler_params=pltpu.CompilerParams(
            vmem_limit_bytes=VMEM_LIMIT, collective_id=1, has_side_effects=True
        ),
        cost_estimate=pl.CostEstimate(flops=20 * slots * d * d, bytes_accessed=40 << 20, transcendentals=16 * slots * slots),
        name="forward",
    )(counts, patches, x, gain1, gain2, *tables, wq, wk, wv, wo, *ids, grad_out, wg, wu, wd)


def gelu_parts(v):
    c, k = math.sqrt(2.0 / math.pi), 0.044715
    square = v * v
    t = jnp.tanh(c * v * (1.0 + k * square))
    up = 0.5 * (1.0 + t)
    slope = up + 0.5 * v * (1.0 - t * t) * (c * (1.0 + 3.0 * k * square))
    return v * up, slope


def split_quarter(ff):
    return ff // LANES * LANES, ff % LANES


def packed_width(ff):
    full, rest = split_quarter(ff)
    return 3 * full + -(-3 * rest // LANES) * LANES


def ffn_kernel(
    block, ff,
    x_ref, go_ref, gofar_ref, middle_ref, gain_ref, w0_ref, w1_ref, w2_ref, c0_ref, c1_ref, c2_ref,
    out_to, sum_to, gm_to, ga_to, gain_out_ref,
    out_ref, sum_ref, gm_ref, ga_ref, xall_ref, gall_ref, wgu_ref, wd_ref, xt_ref, gt_ref, act_ref, send_ref, recv_ref, own_ref, backfar_ref, backin_ref,
    in_sem, w_sem, x_sem, back_sem, dw_sem, leave_sem, end_sem,
):
    slots, d = middle_ref.shape
    halves = slots // block
    full, rest = split_quarter(ff)
    both = 2 * ff
    _, _, core, far, _, _ = neighbours()

    ins = [
        pltpu.make_async_copy(x_ref, xall_ref.at[pl.ds(0, slots), :], in_sem.at[0]),
        pltpu.make_async_copy(go_ref, gall_ref.at[pl.ds(0, slots), :], in_sem.at[1]),
        pltpu.make_async_copy(gofar_ref, gall_ref.at[pl.ds(slots, slots), :], in_sem.at[2]),
    ]
    weights = []
    for m, pair in enumerate(((w0_ref, c0_ref), (w1_ref, c1_ref), (w2_ref, c2_ref))):
        target, base = (wd_ref, 0) if m == 2 else (wgu_ref, m * both)
        for q, r in enumerate(pair):
            for k, (start, size, at) in enumerate(((0, full, q * full), (full, rest, 2 * full + q * rest))):
                if size:
                    weights.append(
                        pltpu.make_async_copy(
                            r.at[pl.ds(start, size), :], target.at[pl.ds(base + at, size), :], w_sem.at[m, q, k]
                        )
                    )
    for copy in ins[:2] + weights + ins[2:]:
        copy.start()
    greet((core, far))
    x_out = [
        remote(x_ref.at[pl.ds(i * block, block), :], xall_ref.at[pl.ds(slots + i * block, block), :], x_sem.at[i], far)
        for i in range(halves)
    ]
    for copy in x_out:
        copy.start()
    back_out = [
        remote(backfar_ref.at[pl.ds(i * block, block), :], backin_ref.at[pl.ds(i * block, block), :], back_sem.at[i], far)
        for i in range(halves)
    ]
    for copy in ins + weights:
        copy.wait()

    def step(b, carry):
        for i in range(halves):

            @pl.when(b == halves + i)
            def _():
                x_out[i].wait_recv()

        rows = pl.ds(pl.multiple_of(b * block, block), block)
        x, g = xall_ref[rows, :], gall_ref[rows, :]
        xt_ref[:, rows] = x.T
        gt_ref[:, rows] = g.T
        grown = lax.dot_general(x, wgu_ref[...], NT, preferred_element_type=F32)
        grad_hidden = lax.dot_general(g, wd_ref[...], NT, preferred_element_type=F32)
        gate, upper = grown[:, :both], grown[:, both:]
        gelu, slope = gelu_parts(gate)
        dg = (grad_hidden * upper * slope).astype(BF)
        du = (grad_hidden * gelu).astype(BF)
        hidden = (gelu * upper).astype(BF)
        act_ref[0, rows, :] = dg
        act_ref[1, rows, :] = du
        act_ref[2, rows, :] = hidden
        back = jnp.dot(jnp.concatenate([dg, du], axis=1), wgu_ref[...], preferred_element_type=F32)

        @pl.when(b < halves)
        def _():
            own_ref[rows, :] = back

        for i in range(halves):

            @pl.when(b == halves + i)
            def _():
                backfar_ref[i * block : (i + 1) * block, :] = back.astype(BF)
                back_out[i].start()

        out_ref[rows, :] = jnp.dot(hidden, wd_ref[...], preferred_element_type=F32).astype(BF)
        pltpu.make_async_copy(out_ref.at[rows, :], out_to.at[rows, :], leave_sem.at[b]).start()
        return carry

    lax.fori_loop(0, 2 * halves, step, 0)

    tile = d // 2
    used = 3 * (full + rest)
    dw_out = [
        remote(send_ref.at[pl.ds(c * tile, tile), :], recv_ref.at[pl.ds(c * tile, tile), :], dw_sem.at[c], core)
        for c in range(2)
    ]
    for c in range(2):
        rows = slice(c * tile, (c + 1) * tile)
        for m in range(3):
            left = gt_ref if m == 2 else xt_ref
            dw = jnp.dot(left[rows, :], act_ref[m], preferred_element_type=F32).astype(BF)
            for q, target in enumerate((sum_ref, send_ref)):
                target[rows, m * full : (m + 1) * full] = dw[:, q * full : (q + 1) * full]
                if rest:
                    at = 2 * full + q * rest
                    target[rows, 3 * full + m * rest : 3 * full + (m + 1) * rest] = dw[:, at : at + rest]
        for target in (sum_ref, send_ref):
            if used < target.shape[1]:
                target[rows, used:] = jnp.zeros((tile, target.shape[1] - used), BF)
        dw_out[c].start()
    leaving = []
    for c in range(2):
        rows = slice(c * tile, (c + 1) * tile)
        dw_out[c].wait_recv()
        sum_ref[rows, :] = (sum_ref[rows, :].astype(F32) + recv_ref[rows, :].astype(F32)).astype(BF)
        at = pl.ds(c * tile, tile)
        leaving.append(pltpu.make_async_copy(sum_ref.at[at, :], sum_to.at[at, :], end_sem.at[c]))
        leaving[-1].start()

    gains = 0.0
    for i in range(halves):
        rows, at = slice(i * block, (i + 1) * block), pl.ds(i * block, block)
        back_out[i].wait_recv()
        middle = middle_ref[rows, :]
        inv = lax.rsqrt(jnp.mean(middle * middle, axis=-1, keepdims=True) + EPS)
        upstream = own_ref[rows, :] + backin_ref[rows, :].astype(F32)
        lifted = upstream * gain_ref[...].astype(F32)[None]
        inner = jnp.mean(lifted * middle, axis=-1, keepdims=True)
        gains = gains + jnp.sum(upstream * middle * inv, axis=0, keepdims=True)
        gm = gall_ref[rows, :].astype(F32) + inv * lifted - middle * (inv * inv * inv * inner)
        gm_ref[rows, :] = gm
        ga_ref[rows, :] = gm.astype(BF)
        for k, (a, b) in enumerate(((gm_ref, gm_to), (ga_ref, ga_to))):
            leaving.append(pltpu.make_async_copy(a.at[at, :], b.at[at, :], end_sem.at[2 + 2 * i + k]))
            leaving[-1].start()
    gain_out_ref[...] = gains
    for copy in x_out + back_out + dw_out:
        copy.wait_send()
    for b in range(2 * halves):
        at = pl.ds(b * block, block)
        pltpu.make_async_copy(out_ref.at[at, :], out_to.at[at, :], leave_sem.at[b]).wait()
    for copy in leaving:
        copy.wait()


def feed_forward(x, go, gofar, middle, gain, own, other, block=256):
    slots, d = x.shape
    ff = own[0].shape[0]
    vmem, anywhere = pl.BlockSpec(memory_space=pltpu.VMEM), pl.BlockSpec(memory_space=pl.ANY)
    shape = jax.ShapeDtypeStruct
    dma = pltpu.SemaphoreType.DMA
    halves = slots // block
    packed = packed_width(ff)
    return pl.pallas_call(
        functools.partial(ffn_kernel, block, ff),
        in_specs=[anywhere] * 3 + [vmem] * 2 + [anywhere] * 6,
        out_specs=[anywhere] * 4 + [vmem],
        out_shape=[
            shape((2 * slots, d), BF),
            shape((d, packed), BF),
            shape((slots, d), F32),
            shape((slots, d), BF),
            shape((1, d), F32),
        ],
        scratch_shapes=[
            pltpu.VMEM((2 * slots, d), BF),
            pltpu.VMEM((d, packed), BF),
            pltpu.VMEM((slots, d), F32),
            pltpu.VMEM((slots, d), BF),
            pltpu.VMEM((2 * slots, d), BF),
            pltpu.VMEM((2 * slots, d), BF),
            pltpu.VMEM((4 * ff, d), BF),
            pltpu.VMEM((2 * ff, d), BF),
            pltpu.VMEM((d, 2 * slots), BF),
            pltpu.VMEM((d, 2 * slots), BF),
            pltpu.VMEM((3, 2 * slots, 2 * ff), BF),
            pltpu.VMEM((d, packed), BF),
            pltpu.VMEM((d, packed), BF),
            pltpu.VMEM((slots, d), F32),
            pltpu.VMEM((slots, d), BF),
            pltpu.VMEM((slots, d), BF),
            dma((3,)), dma((3, 2, 2)), dma((halves, 2)), dma((halves, 2)), dma((2, 2)),
            dma((2 * halves,)), dma((2 + 2 * halves,)),
        ],
        compiler_params=pltpu.CompilerParams(
            vmem_limit_bytes=VMEM_LIMIT, collective_id=2, has_side_effects=True
        ),
        cost_estimate=pl.CostEstimate(flops=36 * slots * d * ff, bytes_accessed=40 << 20, transcendentals=4 * slots * ff),
        name="feed_forward",
    )(x, go, gofar, middle, gain, *own, *other)


def backward_slot(k):
    return jnp.where(k < 4, 6 - 2 * (k & 1) + (k >> 1), 6 - 2 * (k >> 1) + (k & 1))


def backward_kernel(
    wide, heads, buckets, trows, ff,
    ga_ref, x_ref, gain_ref, gain2_ref, fsum_ref, gm_ref, e_ref, ir_ref, ih_ref, iv_ref, out_ref,
    wo_ref, ctx_ref, linv_ref, qkv_ref, wall_ref,
    gi_ref, outin_ref, small_ref, gq_ref, gk_ref, gv_ref, go_ref, fg_ref, fu_ref, fd_ref,
    gib_ref, fown_ref, ds_ref, ids_ref, nt_ref, gat_ref, dx_ref, acc_ref, part_ref, crecv_ref, frecv_ref, xarecv_ref, zarecv_ref,
    xfrecv_ref, zfrecv_ref, nsend_ref, nrecv_ref, parts_ref, srecv_ref,
    in_sem, e_sem, core_sem, far_sem, out_sem, xf_sem, zf_sem, xa_sem, za_sem, sn_sem, ss_sem,
):
    pw = 2 * HEAD_DIM
    slots, d = ga_ref.shape
    half_rows = slots // 2
    ranks = wide // 2
    chunk = d // wide
    steps = 8 + slots // trows
    u = pl.program_id(0)
    w, n, core, far, diag, side = neighbours()
    par, rank = w & 1, w >> 1
    opp = 1 - par
    peer = lambda r: (2 * (rank ^ r) + par, n)
    slot_of = backward_slot
    slot = slot_of(jnp.minimum(u, 7))

    ins = [pltpu.make_async_copy(r.at[n], ids_ref.at[t], in_sem.at[t]) for t, r in enumerate((ir_ref, ih_ref, iv_ref))]
    gm_in = pltpu.make_async_copy(gm_ref, gib_ref, in_sem.at[3])
    fown_in = pltpu.make_async_copy(fsum_ref.at[:, par], fown_ref, in_sem.at[4])
    gi_out = pltpu.make_async_copy(gib_ref, gi_ref, in_sem.at[5])
    core_out = [remote(part_ref.at[s], crecv_ref.at[i], core_sem.at[i], core) for i, s in enumerate((6, 7, 2, 3))]
    order = list(range(ranks - 1, 0, -2)) + list(range(ranks - 2, -1, -2))
    far_out = [
        [
            [
                remote(part_ref.at[4 + i, rank ^ r, p], frecv_ref.at[i, rank ^ r, p], far_sem.at[i, k, r], far)
                for r in range(ranks)
            ]
            for k, p in enumerate((opp, par))
        ]
        for i in range(2)
    ]
    out_out = [
        remote(
            out_ref.at[pl.ds(slots + i * half_rows, half_rows), :],
            outin_ref.at[pl.ds(i * half_rows, half_rows), :], out_sem.at[i], far,
        )
        for i in range(2)
    ]
    xf_out = [None] + [remote(fsum_ref.at[rank ^ r, opp], xfrecv_ref.at[r], xf_sem.at[r], side) for r in range(1, ranks)]
    some = chunk // 2
    xf_last = [
        remote(
            fsum_ref.at[rank, opp, pl.ds(k * some, some), :], xfrecv_ref.at[0, pl.ds(k * some, some), :],
            xf_sem.at[k * ranks], side,
        )
        for k in range(2)
    ]
    low_bit = lambda r: r & -r
    zf_out = [None] + [
        remote(xfrecv_ref.at[r], zfrecv_ref.at[r - 1], zf_sem.at[r - 1], peer(low_bit(r))) for r in range(1, ranks)
    ]
    feeds = lambda r: [r | (1 << b) for b in range(ranks.bit_length() - 1) if (1 << b) < (low_bit(r) if r else ranks)]
    xa_out = [
        [remote(part_ref.at[i, rank ^ r, opp], xarecv_ref.at[i, r], xa_sem.at[i, r], side) for r in range(ranks)]
        for i in range(2)
    ]
    za_out = [
        [None]
        + [
            remote(part_ref.at[i, rank ^ r, par], zarecv_ref.at[i, r - 1], za_sem.at[i, r - 1], peer(low_bit(r)))
            for r in range(1, ranks)
        ]
        for i in range(2)
    ]
    sn_out = [
        remote(nsend_ref.at[r], nrecv_ref.at[r - 1], sn_sem.at[r - 1], dev) for r, dev in ((1, core), (2, far), (3, diag))
    ]
    ss_out = [None] + [
        remote(parts_ref.at[w ^ k], srecv_ref.at[k - 1], ss_sem.at[k - 1], (w ^ k, n)) for k in range(1, wide)
    ]

    def at_edge(end, middle):
        edge = ((rank ^ (rank >> 1)) & 1) == 0
        pl.when(edge)(lambda: end())
        pl.when(jnp.logical_not(edge))(lambda: middle())

    def e_in(k):
        s = slot_of(k)
        return pltpu.make_async_copy(e_ref.at[s], ds_ref.at[s], e_sem.at[k & 1])

    def wide_f32(ref_value):
        return ref_value.astype(F32)

    @pl.when(u == 0)
    def _():
        e_in(0).start()
        for copy in [fown_in] + ins + [gm_in]:
            copy.start()
        greet([core, far, diag] + [(w ^ k, n) for k in range(1, wide)])
        if ranks == 4:
            xf_out[3].start()
            at_edge(xf_out[1].start, xf_out[2].start)
            at_edge(xf_out[2].start, xf_out[1].start)
        else:
            for r in range(ranks - 1, 0, -1):
                xf_out[r].start()
        out_out[0].start()
        x = x_ref[...].astype(F32)
        inv = lax.rsqrt(jnp.mean(x * x, axis=-1, keepdims=True) + EPS)
        nt_ref[...] = (x * inv * gain_ref[...].astype(F32)[None]).astype(BF).T
        gat_ref[...] = ga_ref[...].T
        dx_ref[...] = jnp.zeros_like(dx_ref)
        acc_ref[...] = jnp.zeros_like(acc_ref)
        parts_ref[...] = jnp.zeros_like(parts_ref)

    @pl.when(u < 8)
    def _():
        e_in(u).wait()

        @pl.when(u < 7)
        def _():
            e_in(u + 1).start()

        lane = lax.broadcasted_iota(I32, (slots, pw), 1)
        low = lane < HEAD_DIM
        do2 = (lax.dot_general(ga_ref[...], wo_ref[...], NT, preferred_element_type=F32) * linv_ref[...]).astype(BF)
        prod = do2.astype(F32) * ctx_ref[...].astype(F32)
        q2, k2, v2 = qkv_ref[0], qkv_ref[1], qkv_ref[2]
        vx = jnp.concatenate([v2, jnp.where(lane < 2, 1.0, 0.0).astype(BF)], axis=1)
        do_t, q_t = do2.T, q2.T
        zero = jnp.zeros_like(do2)
        dq, dk, dv = [], [], []
        for sub in range(2):
            mine = low if sub == 0 else jnp.logical_not(low)
            row = -jnp.sum(jnp.where(mine, prod, 0.0), axis=1, keepdims=True)
            head_part = row.astype(BF).astype(F32)
            extra = jnp.where(lane == 0, head_part, jnp.where(lane == 1, row - head_part, 0.0)).astype(BF)
            dox = jnp.concatenate([jnp.where(mine, do2, zero), extra], axis=1)
            t = lax.dot_general(dox, vx, NT, preferred_element_type=F32)
            e = ds_ref[slot, sub]
            ds = (e.astype(F32) * t).astype(BF)
            dv.append(jnp.dot(do_t[sub * HEAD_DIM : (sub + 1) * HEAD_DIM], e, preferred_element_type=F32))
            ds_ref[slot, sub] = ds
            dk.append(jnp.dot(q_t[sub * HEAD_DIM : (sub + 1) * HEAD_DIM], ds, preferred_element_type=F32))
            dq.append(jnp.dot(ds, k2, preferred_element_type=F32))
        joined = jnp.concatenate(
            [
                jnp.where(low, dq[0], dq[1]).astype(BF),
                jnp.concatenate(dk, axis=0).T.astype(BF),
                jnp.concatenate(dv, axis=0).T.astype(BF),
            ],
            axis=1,
        )
        weights = jnp.concatenate([wall_ref[m] for m in range(3)], axis=1)
        dx_ref[...] += lax.dot_general(joined, weights, NT, preferred_element_type=F32)
        part = jnp.dot(nt_ref[...], joined, preferred_element_type=F32).astype(BF)
        part_ref[slot, :, :, :, : 3 * pw] = part.reshape(ranks, 2, chunk, 3 * pw)
        part = jnp.dot(gat_ref[...], ctx_ref[...], preferred_element_type=F32).astype(BF)
        part_ref[slot, :, :, :, 3 * pw :] = part.reshape(ranks, 2, chunk, pw)

    @pl.when(u >= 8)
    def _():
        blk = 16
        one, zero = jnp.ones((blk, 4 * slots), BF), jnp.zeros((blk, 4 * slots), BF)

        @pl.when(u == 8)
        def _():
            for copy in ins:
                copy.wait()

        group = 4

        def sub_block(c, carry):
            starts = [pl.multiple_of((u - 8) * trows + (c * group + k) * blk, blk) for k in range(group)]
            g = jnp.concatenate(
                [
                    jnp.concatenate([ds_ref[s, sub, pl.ds(at, blk), :] for s in range(8) for sub in range(2)], axis=0)
                    for at in starts
                ],
                axis=1,
            )
            for t in range(3):
                ids = jnp.concatenate([ids_ref[t, pl.ds(at, blk), :].astype(F32).astype(BF) for at in starts], axis=1)
                hot = jnp.concatenate([jnp.where(ids == jnp.bfloat16(b), one, zero) for b in range(buckets)], axis=0)
                span = slice(t * buckets * blk, (t + 1) * buckets * blk)
                acc_ref[span, :] += lax.dot_general(hot, g, NT, preferred_element_type=F32)
            return carry

        lax.fori_loop(0, trows // (blk * group), sub_block, 0)

    def event(step):
        return lambda body: pl.when(u == step)(body)

    def core_stage(i):
        core_out[i].wait_recv()
        for p in (opp, par):
            total = wide_f32(part_ref[4 + i, :, p]) + wide_f32(crecv_ref[i, :, p])
            part_ref[4 + i, :, p] = total.astype(BF)
        for r in order:
            far_out[i][0][r].start()

    def own_sides():
        for i in range(2):
            for r in order:
                far_out[i][1][r].start()

    def far_stage(i):
        core_out[2 + i].wait_recv()
        for r in order:
            far_out[i][0][r].wait_recv()
            k = rank ^ r
            total = wide_f32(part_ref[i, k, opp]) + wide_f32(crecv_ref[2 + i, k, opp]) + wide_f32(frecv_ref[i, k, opp])
            part_ref[i, k, opp] = total.astype(BF)
            xa_out[i][r].start()

    def side_stage(i, r):
        far_out[i][1][r].wait_recv()
        xa_out[i][r].wait_recv()
        k = rank ^ r
        total = wide_f32(part_ref[i, k, par]) + wide_f32(crecv_ref[2 + i, k, par])
        total = total + wide_f32(frecv_ref[i, k, par]) + wide_f32(xarecv_ref[i, r])
        part_ref[i, k, par] = total.astype(BF)
        if r & 1:
            za_out[i][r].start()

    def rank_stage(i, r):
        total = wide_f32(part_ref[i, rank ^ r, par])
        for k in feeds(r):
            za_out[i][k].wait_recv()
            total = total + wide_f32(zarecv_ref[i, k - 1])
        if r == 0:
            return total
        part_ref[i, rank ^ r, par] = total.astype(BF)
        za_out[i][r].start()

    def ffn_stage(r):
        for copy in xf_last if r == 0 else [xf_out[r]]:
            copy.wait_recv()
        total = wide_f32(fown_ref[rank ^ r]) + wide_f32(xfrecv_ref[r])
        for k in feeds(r):
            zf_out[k].wait_recv()
            total = total + wide_f32(zfrecv_ref[k - 1])
        if r == 0:
            return total
        xfrecv_ref[r] = total.astype(BF)
        zf_out[r].start()

    def input_gradient():
        gm_in.wait()
        x = x_ref[...].astype(F32)
        inv = lax.rsqrt(jnp.mean(x * x, axis=-1, keepdims=True) + EPS)
        upstream = dx_ref[...]
        lifted = upstream * gain_ref[...].astype(F32)[None]
        inner = jnp.mean(lifted * x, axis=-1, keepdims=True)
        gib_ref[...] = gib_ref[...] + inv * lifted - x * (inv * inv * inv * inner)
        gi_out.start()
        gains = jnp.sum(upstream * x * inv, axis=0, keepdims=True)
        lanes = d // LANES
        for r in range(4):
            for j in range(lanes):
                span = slice(j * LANES, (j + 1) * LANES)
                nsend_ref[r, 3 * buckets + j : 3 * buckets + j + 1, :] = gains[:, span]
                nsend_ref[r, 3 * buckets + lanes + j : 3 * buckets + lanes + j + 1, :] = gain2_ref[:, span]

    plan = [[] for _ in range(steps)]
    for i in range(2):
        plan[2 * i].append(core_out[i].start)
        plan[2 * i + 1].append(functools.partial(core_stage, i))
        plan[4 + i].append(core_out[2 + i].start)
    plan[3].append(own_sides)
    plan[1].append(fown_in.wait)
    if ranks == 4:
        turn = lambda a, b: functools.partial(at_edge, functools.partial(ffn_stage, a), functools.partial(ffn_stage, b))
        plan[2].append(functools.partial(ffn_stage, 3))
        plan[5].append(turn(1, 2))
        plan[8].append(turn(2, 1))
    else:
        for k, r in enumerate(range(ranks - 1, 0, -1)):
            plan[3 + k * 6 // ranks].append(functools.partial(ffn_stage, r))
    plan[6].append(functools.partial(far_stage, 0))
    plan[7].append(input_gradient)
    plan[8].append(functools.partial(far_stage, 1))
    plan[8].append(xf_last[0].start)
    plan[12].extend(functools.partial(side_stage, 0, r) for r in order)
    plan[15].extend(functools.partial(rank_stage, 0, r) for r in range(ranks - 2, 0, -2))
    for k in range(steps):

        @pl.when(u == k)
        def _():
            for action in plan[k]:
                action()

    @pl.when(u == steps - 1)
    def _():
        blk, cols = 16, 16 * 16
        same = lax.broadcasted_iota(I32, (blk, cols), 0) == (lax.broadcasted_iota(I32, (blk, cols), 1) & (blk - 1))
        picked = [
            jnp.sum(jnp.where(same, acc_ref[b * blk : (b + 1) * blk, :], 0.0), axis=0, keepdims=True)
            for b in range(3 * buckets)
        ]
        picked = jnp.concatenate(picked, axis=0)
        source = lax.broadcasted_iota(I32, (cols, LANES), 0) >> 4
        target = lax.broadcasted_iota(I32, (cols, LANES), 1)
        choose = jnp.where(source == target, 1.0, 0.0).astype(F32)
        sums = jnp.dot(picked, choose, preferred_element_type=F32, precision=lax.Precision.HIGHEST)
        for r in range(4):
            nsend_ref[r, : 3 * buckets, :] = pltpu.roll(sums, LANES - heads * r, 1) if r else sums
        for copy in sn_out + out_out[1:]:
            copy.start()

        def finish(i):
            total = rank_stage(i, 0)
            cols = slice(i * pw, (i + 1) * pw)
            gq_ref[:, cols] = total[:, :pw]
            gk_ref[:, cols] = total[:, pw : 2 * pw]
            gv_ref[:, cols] = total[:, 2 * pw : 3 * pw]
            go_ref[cols, :] = total[:, 3 * pw :].T

        for r in order[:-1]:
            side_stage(1, r)
        for copy in sn_out:
            copy.wait()
        nsend_ref[1] = nsend_ref[0] + nrecv_ref[0] + nrecv_ref[1] + nrecv_ref[2]
        lanes, own = d // LANES, buckets // wide
        for k in range(wide):
            row = 3 * buckets + k * d // wide // LANES
            parts_ref[k, 0:1, :] = nsend_ref[1, row : row + 1, :]
            parts_ref[k, 1:2, :] = nsend_ref[1, row + lanes : row + lanes + 1, :]
            for t in range(3):
                at = t * buckets + k * own
                parts_ref[k, 2 + t * own : 2 + (t + 1) * own, :] = nsend_ref[1, at : at + own, :]
        for copy in ss_out[1:]:
            copy.start()
        xf_last[1].start()
        side_stage(1, 0)
        finish(0)
        for r in range(ranks - 2, 0, -2):
            rank_stage(1, r)
        total = ffn_stage(0)
        full, rest = split_quarter(ff)
        for m, ref in enumerate((fg_ref, fu_ref, fd_ref)):
            ref[:full, :] = total[:, m * full : (m + 1) * full].T
            if rest:
                ref[full:, :] = total[:, 3 * full + m * rest : 3 * full + (m + 1) * rest].T
        total = parts_ref[w]
        for k in range(1, wide):
            ss_out[k].wait_recv()
            total = total + srecv_ref[k - 1]
        small_ref[...] = total
        finish(1)
        gi_out.wait()
        for copy in out_out:
            copy.wait()
        for i in range(2):
            for copy in far_out[i][0] + far_out[i][1] + xa_out[i] + za_out[i][1:]:
                copy.wait_send()
        for copy in core_out + xf_out[1:] + xf_last + zf_out[1:] + ss_out[1:]:
            copy.wait_send()


def backward(wide, buckets, ff, ga, x, gain, gain2, fsum, gm, e, ids, out, wo_all, ctx, linv, qkv, w_all, trows=64):
    slots, d = x.shape
    heads = 4
    pw = 2 * HEAD_DIM
    ranks, chunk = wide // 2, d // wide
    packed = fsum.shape[-1]
    width = heads * HEAD_DIM
    small = 3 * buckets + 2 * d // LANES
    place = -(-(2 + 3 * (buckets // wide)) // 8) * 8
    vmem, anywhere = pl.BlockSpec(memory_space=pltpu.VMEM), pl.BlockSpec(memory_space=pl.ANY)
    shape = jax.ShapeDtypeStruct
    dma = pltpu.SemaphoreType.DMA

    def slot(u):
        return backward_slot(jnp.minimum(u, 7))

    return pl.pallas_call(
        functools.partial(backward_kernel, wide, heads, buckets, trows, ff),
        grid=(8 + slots // trows,),
        in_specs=[vmem] * 4 + [anywhere] * 7 + [
            pl.BlockSpec((pw, d), lambda u: (slot(u), 0)),
            pl.BlockSpec((slots, pw), lambda u: (0, slot(u))),
            pl.BlockSpec((slots, pw), lambda u: (0, slot(u))),
            pl.BlockSpec((3, slots, pw), lambda u: (0, 0, slot(u))),
            pl.BlockSpec((3, d, pw), lambda u: (0, 0, slot(u))),
        ],
        out_specs=[anywhere] * 2 + [vmem] * 8,
        out_shape=[
            shape((slots, d), F32),
            shape((slots, d), BF),
            shape((place, LANES), F32),
            shape((chunk, width), F32),
            shape((chunk, width), F32),
            shape((chunk, width), F32),
            shape((width, chunk), F32),
            shape((ff, chunk), F32),
            shape((ff, chunk), F32),
            shape((ff, chunk), F32),
        ],
        scratch_shapes=[
            pltpu.VMEM((slots, d), F32),
            pltpu.VMEM((ranks, chunk, packed), BF),
            pltpu.VMEM((8, 2, slots, slots), BF),
            pltpu.VMEM((3, slots, slots), I32),
            pltpu.VMEM((d, slots), BF),
            pltpu.VMEM((d, slots), BF),
            pltpu.VMEM((slots, d), F32),
            pltpu.VMEM((3 * buckets * 16, 16 * 16), F32),
            pltpu.VMEM((8, ranks, 2, chunk, 4 * pw), BF),
            pltpu.VMEM((4, ranks, 2, chunk, 4 * pw), BF),
            pltpu.VMEM((2, ranks, 2, chunk, 4 * pw), BF),
            pltpu.VMEM((2, ranks, chunk, 4 * pw), BF),
            pltpu.VMEM((2, ranks - 1, chunk, 4 * pw), BF),
            pltpu.VMEM((ranks, chunk, packed), BF),
            pltpu.VMEM((ranks - 1, chunk, packed), BF),
            pltpu.VMEM((4, small, LANES), F32),
            pltpu.VMEM((3, small, LANES), F32),
            pltpu.VMEM((wide, place, LANES), F32),
            pltpu.VMEM((wide - 1, place, LANES), F32),
            dma((6,)), dma((2,)), dma((4, 2)), dma((2, 2, ranks, 2)), dma((2, 2)), dma((ranks + 1, 2)), dma((ranks - 1, 2)),
            dma((2, ranks, 2)), dma((2, ranks - 1, 2)), dma((3, 2)), dma((wide - 1, 2)),
        ],
        compiler_params=pltpu.CompilerParams(
            vmem_limit_bytes=VMEM_LIMIT, collective_id=3, has_side_effects=True
        ),
        cost_estimate=pl.CostEstimate(flops=30 * slots * d * d, bytes_accessed=60 << 20, transcendentals=0),
        name="backward",
    )(ga, x, gain, gain2, fsum, gm, e, *ids, out, wo_all, ctx, linv, qkv, w_all)


def results_kernel(
    wide, narrow, buckets, heads, middle_ref, out_ref, outin_ref, gi_ref, small_ref, *rest,
):
    sources, (block_ref, go_ref, ga_ref, gf_ref, tr_ref, th_ref, tv_ref), targets = rest[:7], rest[7:14], rest[14:]
    block_ref[...] = (middle_ref[...] + (out_ref[...].astype(F32) + outin_ref[...].astype(F32))).astype(BF)
    go_ref[...] = gi_ref[...]

    @pl.when(pl.program_id(0) == 0)
    def _():
        for a, b in zip(sources, targets):
            b[...] = a[...]
        w, n = lax.axis_index("wide"), lax.axis_index("narrow")
        d = middle_ref.shape[1]
        per, own = d // (wide * narrow), buckets // wide
        start = (w * narrow + n) * per
        for k, ref in enumerate((ga_ref, gf_ref)):
            row = small_ref[k : k + 1, :]
            lane = lax.broadcasted_iota(I32, (per, LANES), 1)
            mine = lane == lax.broadcasted_iota(I32, (per, LANES), 0) + start % LANES
            ref[...] = jnp.sum(jnp.where(mine, jnp.broadcast_to(row, (per, LANES)), 0.0), axis=1)
        for k, ref in enumerate((tr_ref, th_ref, tv_ref)):
            ref[...] = small_ref[2 + k * own : 2 + (k + 1) * own, :heads]


def results(wide, narrow, buckets, heads, middle, out, outin, small, grad_input, big):
    slots, d = middle.shape
    shape = jax.ShapeDtypeStruct
    per, own = d // (wide * narrow), buckets // wide
    rows = pl.BlockSpec((slots // 2, d), lambda i: (i, 0))
    whole = lambda *sh: pl.BlockSpec(sh, lambda i: (0,) * len(sh))
    return pl.pallas_call(
        functools.partial(results_kernel, wide, narrow, buckets, heads),
        grid=(2,),
        in_specs=[rows] * 4 + [whole(*small.shape)] + [whole(*x.shape) for x in big],
        out_specs=[rows] * 2 + [whole(per)] * 2 + [whole(own, heads)] * 3 + [whole(*x.shape) for x in big],
        out_shape=[shape((slots, d), BF), shape((slots, d), F32)] + [shape((per,), F32)] * 2
        + [shape((own, heads), F32)] * 3 + [shape(x.shape, x.dtype) for x in big],
        compiler_params=pltpu.CompilerParams(vmem_limit_bytes=VMEM_LIMIT),
        name="results",
    )(middle, out, outin, grad_input, small, *big)


def shards(
    wide, narrow, hidden_in, grad_out, gain_attn, gain_ffn, w_query, w_key, w_value, w_output,
    table_rel, table_horiz, table_vert, wi_gate, wi_up, wo_ffn, counts, patch_mask,
    bucket_rel, bucket_horiz, bucket_vert,
):
    slots = bucket_rel.shape[1]
    rows, d = hidden_in.shape
    buckets, heads = table_rel.shape
    width = w_query.shape[1]
    ff = wi_gate.shape[1]
    assert rows == slots and narrow == 4 and wide >= 4 and heads * HEAD_DIM == width
    ids = (bucket_rel, bucket_horiz, bucket_vert)

    qkv, exps, context, linv, w_all, wo_all, middle, ffn_own, grad_far, wg_core, wu_core, wd_core = forward(
        counts, patch_mask, hidden_in, gain_attn, gain_ffn, (table_rel.T, table_horiz.T, table_vert.T),
        w_query, w_key, w_value, w_output, ids, grad_out, wi_gate.T, wi_up.T, wo_ffn,
    )
    out, ffn_sum, grad_middle, grad_attn, grad_gain_second = feed_forward(
        ffn_own, grad_out, grad_far, middle, gain_ffn,
        (wi_gate.T, wi_up.T, wo_ffn), (wg_core, wu_core, wd_core),
    )
    grad_input, out_in, small, gq, gk, gv, go, fg, fu, fd = backward(
        wide, buckets, ff, grad_attn, hidden_in, gain_attn, grad_gain_second,
        ffn_sum.reshape(wide // 2, 2, d // wide, -1), grad_middle, exps, ids, out,
        wo_all, context, linv, qkv, w_all,
    )
    block_out, grad_input, gain1, gain2, rel, horiz, vert, gq, gk, gv, go, fg, fu, fd = results(
        wide, narrow, buckets, heads, middle, out, out_in, small, grad_input, (gq, gk, gv, go, fg, fu, fd)
    )
    return (
        block_out, grad_input, gain1, gain2, gq, gk, gv, go, rel, horiz, vert, fg.T, fu.T, fd,
    )


def solution(mesh):
    rows, both = P(("wide", "narrow"), None), P(("wide", "narrow"))
    cols, across = P(None, "narrow"), P("narrow", None)
    grid, turned = P("wide", "narrow"), P("narrow", "wide")
    pages = P("wide", None, None)
    return jax.shard_map(
        functools.partial(shards, mesh.shape["wide"], mesh.shape["narrow"]),
        mesh=mesh,
        in_specs=(
            rows, rows, P(), P(), cols, cols, cols, across, cols, cols, cols, cols, cols, across,
            P("wide"), P("wide", None), pages, pages, pages,
        ),
        out_specs=(
            rows, rows, both, both, grid, grid, grid, turned, grid, grid, grid, grid, grid, turned,
        ),
        check_vma=False,
    )
```

```python
import functools
import math

import jax
import jax.numpy as jnp
from jax import lax
from jax.experimental import pallas as pl
from jax.experimental.pallas import tpu as pltpu
from jax.sharding import PartitionSpec as P

F32 = jnp.float32
BF = jnp.bfloat16
I32 = jnp.int32
HEAD_DIM = 64
LANES = 128
EPS = 1e-06
NT = (((1,), (1,)), ((), ()))

FIXED = 2048.0
OFFSET = 8192
MASKED = -3.0e12
VMEM_LIMIT = 60 << 20
MESH = pl.DeviceIdType.MESH


def lookup(table_row, ids):
    return jnp.take_along_axis(table_row, ids, axis=1, mode="promise_in_bounds")


def neighbours():
    w, n = lax.axis_index("wide"), lax.axis_index("narrow")
    return w, n, (w, n ^ 1), (w, n ^ 2), (w, n ^ 3), (w ^ 1, n)


def greet(devices):
    barrier = pltpu.get_barrier_semaphore()
    for device in devices:
        pl.semaphore_signal(barrier, inc=1, device_id=device, device_id_type=MESH)
    pl.semaphore_wait(barrier, len(devices))


def remote(src, dst, sems, device):
    return pltpu.make_async_remote_copy(
        src_ref=src, dst_ref=dst, send_sem=sems.at[0], recv_sem=sems.at[1], device_id=device, device_id_type=MESH
    )


def forward_kernel(
    heads, buckets, chunk,
    counts_ref, patch_ref, x_ref, gain1_ref, gain2_ref, tr_ref, th_ref, tv_ref,
    wq_ref, wk_ref, wv_ref, wo_ref, ir_ref, ih_ref, iv_ref, go_ref, wg_ref, wu_ref, wd_ref,
    qkv_to, e_ref, ctx_to, linv_to, wall_to, woall_to, middle_ref, ffn_ref, gofar_ref, wgc_ref, wuc_ref, wdc_ref,
    qkv_ref, ctx_ref, linv_ref, wall_ref, woall_ref, normed_ref, mask_ref, ids_ref, tab_ref, tabs_ref, words_ref, ebuf_ref,
    own_sem, id_sem, e_sem, core_sem, far_sem, deep_sem, wide_sem, fwd_sem, tab_sem, big_sem, leave_sem,
):
    pw = 2 * HEAD_DIM
    slots, d = x_ref.shape
    piece = d // 2
    w, n, core, far, diag, side = neighbours()
    deep = (w ^ 2, n)
    half, share = w & 1, (w >> 1) & 1
    other = 1 - half

    def source(m, pair, part=None):
        cols = pl.ds(pl.multiple_of(pair * pw, pw), pw)
        span = slice(None) if part is None else pl.ds(pl.multiple_of(part * piece, piece), piece)
        return wo_ref.at[cols, span] if m == 3 else (wq_ref, wk_ref, wv_ref)[m].at[span, cols]

    def place(m, slot, part=None):
        cols = pl.ds(pl.multiple_of(slot * pw, pw), pw)
        span = slice(None) if part is None else pl.ds(pl.multiple_of(part * piece, piece), piece)
        return woall_ref.at[cols, span] if m == 3 else wall_ref.at[m, span, cols]

    ids_in = [pltpu.make_async_copy(r.at[n], ids_ref.at[t], id_sem.at[t]) for t, r in enumerate((ir_ref, ih_ref, iv_ref))]
    own_in = [[pltpu.make_async_copy(source(m, p), place(m, p), own_sem.at[p, m]) for m in range(4)] for p in range(2)]
    for copy in own_in[0][:3] + ids_in + own_in[0][3:] + own_in[1]:
        copy.start()

    tab_ref[...] = jnp.zeros_like(tab_ref)
    for t, r in enumerate((tr_ref, th_ref, tv_ref)):
        tab_ref[t * heads : (t + 1) * heads, :buckets] = jnp.floor(r[...].astype(F32) * FIXED + 0.5)

    greet((core, far, diag, side, deep))
    far_out = [remote(source(m, half, share), place(m, 4 + half, share), far_sem.at[m], far) for m in range(4)]
    deep_out = [remote(place(m, 4 + half, share), place(m, 4 + half, share), deep_sem.at[m], deep) for m in range(4)]
    core_out = [[remote(source(m, p), place(m, 2 + p), core_sem.at[p, m], core) for m in range(4)] for p in range(2)]
    tabs_out = [remote(tab_ref, tabs_ref.at[r - 1], tab_sem.at[r - 1], dev) for r, dev in ((1, core), (2, far), (3, diag))]
    wide_out = [
        [remote(place(m, 4 + half, k), place(m, 4 + half, k), wide_sem.at[m, i], side) for i, k in enumerate((share, 1 - share))]
        for m in range(4)
    ]
    fwd_out = [
        [remote(place(m, 4 + half, k), place(m, 6 + half, k), fwd_sem.at[m, i], core) for i, k in enumerate((share, 1 - share))]
        for m in range(4)
    ]
    last_out = [remote(place(m, 4 + other), place(m, 6 + other), fwd_sem.at[m, 2], core) for m in range(4)]
    go_out = remote(go_ref, gofar_ref, big_sem.at[0], far)
    ffn_out = [
        remote(wg_ref, wgc_ref, big_sem.at[1], core),
        remote(wu_ref, wuc_ref, big_sem.at[2], core),
        remote(wd_ref, wdc_ref, big_sem.at[3], core),
    ]
    for copy in tabs_out + far_out + [go_out] + core_out[0] + core_out[1]:
        copy.start()

    x = x_ref[...].astype(F32)
    inv = lax.rsqrt(jnp.mean(x * x, axis=-1, keepdims=True) + EPS)
    normed_ref[...] = (x * inv * gain1_ref[...].astype(F32)[None]).astype(BF)
    text = slots - patch_ref.shape[1]
    shown = jnp.concatenate(
        [
            jnp.where(lax.broadcasted_iota(I32, (1, text), 1) < counts_ref[n], 1, 0),
            patch_ref[pl.ds(n, 1), :],
        ],
        axis=1,
    )
    column = jnp.broadcast_to(jnp.where(shown == 1, 0.0, MASKED), (pw, slots)).T
    lane_all = lax.broadcasted_iota(I32, (slots, pw), 1)
    mask_ref[...] = jnp.where(lane_all == 0, column, 0.0).astype(BF)
    ones = jnp.ones((slots, pw), BF)
    lane = lax.broadcasted_iota(I32, (chunk, pw), 1)
    low = lane < HEAD_DIM
    first = jnp.where(lane == 0, 1.0, 0.0).astype(BF)
    to_log2 = math.log2(math.e) / FIXED

    def pack_words(r, table):
        fixed = table.astype(I32)
        for p in range(2):
            for t in range(3):
                row = t * heads + 2 * p
                words_ref[2 * r + p, t : t + 1, :] = fixed[row + 1 : row + 2] * 65536 + fixed[row : row + 1] + OFFSET

    pack_words(0, tab_ref[...])
    for copy in ids_in:
        copy.wait()

    def e_out(parity, slot):
        return pltpu.make_async_copy(ebuf_ref.at[parity], e_ref.at[slot], e_sem.at[parity])

    def leaving(slot):
        cols = pl.ds(pl.multiple_of(slot * pw, pw), pw)
        pairs = (
            (wall_ref.at[:, :, cols], wall_to.at[:, :, cols]),
            (qkv_ref.at[:, :, cols], qkv_to.at[:, :, cols]),
            (ctx_ref.at[:, cols], ctx_to.at[:, cols]),
            (linv_ref.at[:, cols], linv_to.at[:, cols]),
        )
        return [pltpu.make_async_copy(a, b, leave_sem.at[k, slot]) for k, (a, b) in enumerate(pairs)]

    def slot_of(t):
        late = 4 + 2 * (t & 1) + jnp.where(t >= 6, other, half)
        return jnp.where(t < 4, t, late)

    plan = [[] for _ in range(16)]

    def far_arrived(m):
        far_out[m].wait_recv()
        deep_out[m].start()
        wide_out[m][0].start()
        fwd_out[m][0].start()

    def deep_arrived(m):
        deep_out[m].wait_recv()
        wide_out[m][1].start()
        fwd_out[m][1].start()

    def wide_arrived(m):
        for copy in wide_out[m]:
            copy.wait_recv()
        last_out[m].start()

    def tables_arrived():
        for r, copy in enumerate(tabs_out):
            copy.wait()
            pack_words(r + 1, tabs_ref[r])

    for p in range(2):
        plan[2 * p].extend(own_in[p][m].wait for m in range(3))
        plan[4 + 2 * p].extend(core_out[p][m].wait_recv for m in range(3))
    plan[3].append(tables_arrived)
    for m in range(4):
        plan[2 + m].append(functools.partial(far_arrived, m))
        plan[4 + m].append(functools.partial(deep_arrived, m))
    plan[7].extend(copy.start for copy in ffn_out)
    plan[10].extend(copy.wait_recv for m in range(3) for copy in fwd_out[m])
    plan[12].extend(functools.partial(wide_arrived, m) for m in range(3))
    plan[14].extend(last_out[m].wait_recv for m in range(3))
    plan[14].append(functools.partial(wide_arrived, 3))

    def events(t, c):
        for k in range(8):
            if plan[2 * k + c]:

                @pl.when(t == k)
                def _():
                    for action in plan[2 * k + c]:
                        action()

    def step(t, carry):
        slot = slot_of(t)
        events(t, 0)
        parity = t & 1

        @pl.when(t >= 2)
        def _():
            e_out(parity, slot).wait()

        cols = pl.ds(pl.multiple_of(slot * pw, pw), pw)
        weights = jnp.concatenate([wall_ref[m, :, cols] for m in range(3)], axis=1)
        joined = jnp.dot(normed_ref[...], weights, preferred_element_type=F32).astype(BF)
        for m in range(3):
            qkv_ref[m, :, cols] = joined[:, m * pw : (m + 1) * pw]
        kx = jnp.concatenate([joined[:, pw : 2 * pw], mask_ref[...]], axis=1)
        vx = jnp.concatenate([joined[:, 2 * pw :], ones], axis=1)
        words = words_ref[slot]
        for c in range(slots // chunk):
            if c == slots // chunk // 2:
                events(t, 1)
            rows = slice(c * chunk, (c + 1) * chunk)
            q2 = joined[rows, :pw] * jnp.bfloat16(FIXED)
            zero = jnp.zeros_like(q2)
            scores = []
            for sub in range(2):
                q = jnp.where(low, q2, zero) if sub == 0 else jnp.where(low, zero, q2)
                q = jnp.concatenate([q, first], axis=1)
                scores.append(lax.dot_general(q, kx, NT, preferred_element_type=F32))
            tabs = [jnp.broadcast_to(words[k : k + 1, :], (chunk, LANES)) for k in range(3)]
            parts = ([], [])
            for j in range(slots // LANES):
                sl = slice(j * LANES, (j + 1) * LANES)
                bias = (
                    lookup(tabs[0], ids_ref[0, rows, sl])
                    + lookup(tabs[1], ids_ref[1, rows, sl])
                    + lookup(tabs[2], ids_ref[2, rows, sl])
                )
                parts[0].append(scores[0][:, sl] + (bias & 0xFFFF).astype(F32))
                parts[1].append(scores[1][:, sl] + (bias >> 16).astype(F32))
            outs = []
            for sub in range(2):
                s = jnp.concatenate(parts[sub], axis=1)
                peak = jnp.max(s, axis=1, keepdims=True)
                e = jnp.exp2((s - peak) * to_log2).astype(BF)
                ebuf_ref[parity, sub, rows, :] = e
                outs.append(jnp.dot(e, vx, preferred_element_type=F32))
            linv = 1.0 / jnp.where(low, outs[0][:, pw:], outs[1][:, pw:])
            linv_ref[rows, cols] = linv
            ctx_ref[rows, cols] = (jnp.where(low, outs[0][:, :pw], outs[1][:, :pw]) * linv).astype(BF)
        e_out(parity, slot).start()
        for copy in leaving(slot):
            copy.start()
        return carry

    lax.fori_loop(0, 8, step, 0)
    for p in range(2):
        own_in[p][3].wait()
        core_out[p][3].wait_recv()
    for copy in fwd_out[3] + last_out[3:]:
        copy.wait_recv()
    wo_leaving = pltpu.make_async_copy(woall_ref, woall_to, id_sem.at[0])
    wo_leaving.start()
    middle = x_ref[...].astype(F32) + jnp.dot(ctx_ref[...], woall_ref[...], preferred_element_type=F32)
    middle_ref[...] = middle
    inv = lax.rsqrt(jnp.mean(middle * middle, axis=-1, keepdims=True) + EPS)
    ffn_ref[...] = (middle * inv * gain2_ref[...].astype(F32)[None]).astype(BF)
    for p in range(2):
        e_out(p, p).wait()
        for m in range(4):
            core_out[p][m].wait_send()
    for m in range(4):
        for copy in [far_out[m], deep_out[m], last_out[m]] + wide_out[m] + fwd_out[m]:
            copy.wait_send()
    for copy in ffn_out:
        copy.wait()
    for slot in range(8):
        for copy in leaving(slot):
            copy.wait()
    wo_leaving.wait()
    go_out.wait()


def forward(counts, patches, x, gain1, gain2, tables, wq, wk, wv, wo, ids, grad_out, wg, wu, wd, chunk=256):
    slots, d = x.shape
    heads = wq.shape[1] // HEAD_DIM
    buckets = tables[0].shape[1]
    ff = wd.shape[0]
    assert heads == 4
    vmem, anywhere = pl.BlockSpec(memory_space=pltpu.VMEM), pl.BlockSpec(memory_space=pl.ANY)
    shape = jax.ShapeDtypeStruct
    dma = pltpu.SemaphoreType.DMA
    return pl.pallas_call(
        functools.partial(forward_kernel, heads, buckets, chunk),
        in_specs=[pl.BlockSpec(memory_space=pltpu.SMEM)] + [vmem] * 7 + [anywhere] * 11,
        out_specs=[anywhere] * 6 + [vmem] * 2 + [anywhere] * 4,
        out_shape=[
            shape((3, slots, d), BF),
            shape((8, 2, slots, slots), BF),
            shape((slots, d), BF),
            shape((slots, d), F32),
            shape((3, d, d), BF),
            shape((d, d), BF),
            shape((slots, d), F32),
            shape((slots, d), BF),
            shape((slots, d), BF),
            shape((ff, d), BF),
            shape((ff, d), BF),
            shape((ff, d), BF),
        ],
        scratch_shapes=[
            pltpu.VMEM((3, slots, d), BF),
            pltpu.VMEM((slots, d), BF),
            pltpu.VMEM((slots, d), F32),
            pltpu.VMEM((3, d, d), BF),
            pltpu.VMEM((d, d), BF),
            pltpu.VMEM((slots, d), BF),
            pltpu.VMEM((slots, 2 * HEAD_DIM), BF),
            pltpu.VMEM((3, slots, slots), I32),
            pltpu.VMEM((16, LANES), F32),
            pltpu.VMEM((3, 16, LANES), F32),
            pltpu.VMEM((8, 8, LANES), I32),
            pltpu.VMEM((2, 2, slots, slots), BF),
            dma((2, 4)), dma((3,)), dma((2,)), dma((2, 4, 2)), dma((4, 2)), dma((4, 2)), dma((4, 2, 2)), dma((4, 3, 2)),
            dma((3, 2)), dma((4, 2)), dma((4, 8)),
        ],
        compiler_params=pltpu.CompilerParams(
            vmem_limit_bytes=VMEM_LIMIT, collective_id=1, has_side_effects=True
        ),
        cost_estimate=pl.CostEstimate(flops=20 * slots * d * d, bytes_accessed=40 << 20, transcendentals=16 * slots * slots),
        name="forward",
    )(counts, patches, x, gain1, gain2, *tables, wq, wk, wv, wo, *ids, grad_out, wg, wu, wd)


def gelu_parts(v):
    c, k = math.sqrt(2.0 / math.pi), 0.044715
    square = v * v
    t = jnp.tanh(c * v * (1.0 + k * square))
    up = 0.5 * (1.0 + t)
    slope = up + 0.5 * v * (1.0 - t * t) * (c * (1.0 + 3.0 * k * square))
    return v * up, slope


def split_quarter(ff):
    return ff // LANES * LANES, ff % LANES


def packed_width(ff):
    full, rest = split_quarter(ff)
    return 3 * full + -(-3 * rest // LANES) * LANES


def ffn_kernel(
    block, ff,
    x_ref, go_ref, gofar_ref, middle_ref, gain_ref, w0_ref, w1_ref, w2_ref, c0_ref, c1_ref, c2_ref,
    out_to, sum_to, gm_to, ga_to, gain_out_ref,
    out_ref, sum_ref, gm_ref, ga_ref, xall_ref, gall_ref, wgu_ref, wd_ref, xt_ref, gt_ref, act_ref, send_ref, recv_ref, own_ref, backfar_ref, backin_ref,
    in_sem, w_sem, x_sem, back_sem, dw_sem, leave_sem, end_sem,
):
    slots, d = middle_ref.shape
    halves = slots // block
    full, rest = split_quarter(ff)
    both = 2 * ff
    _, _, core, far, _, _ = neighbours()

    ins = [
        pltpu.make_async_copy(x_ref, xall_ref.at[pl.ds(0, slots), :], in_sem.at[0]),
        pltpu.make_async_copy(go_ref, gall_ref.at[pl.ds(0, slots), :], in_sem.at[1]),
        pltpu.make_async_copy(gofar_ref, gall_ref.at[pl.ds(slots, slots), :], in_sem.at[2]),
    ]
    weights = []
    for m, pair in enumerate(((w0_ref, c0_ref), (w1_ref, c1_ref), (w2_ref, c2_ref))):
        target, base = (wd_ref, 0) if m == 2 else (wgu_ref, m * both)
        for q, r in enumerate(pair):
            for k, (start, size, at) in enumerate(((0, full, q * full), (full, rest, 2 * full + q * rest))):
                if size:
                    weights.append(
                        pltpu.make_async_copy(
                            r.at[pl.ds(start, size), :], target.at[pl.ds(base + at, size), :], w_sem.at[m, q, k]
                        )
                    )
    for copy in ins[:2] + weights + ins[2:]:
        copy.start()
    greet((core, far))
    x_out = [
        remote(x_ref.at[pl.ds(i * block, block), :], xall_ref.at[pl.ds(slots + i * block, block), :], x_sem.at[i], far)
        for i in range(halves)
    ]
    for copy in x_out:
        copy.start()
    back_out = [
        remote(backfar_ref.at[pl.ds(i * block, block), :], backin_ref.at[pl.ds(i * block, block), :], back_sem.at[i], far)
        for i in range(halves)
    ]
    for copy in ins + weights:
        copy.wait()

    def step(b, carry):
        for i in range(halves):

            @pl.when(b == halves + i)
            def _():
                x_out[i].wait_recv()

        rows = pl.ds(pl.multiple_of(b * block, block), block)
        x, g = xall_ref[rows, :], gall_ref[rows, :]
        xt_ref[:, rows] = x.T
        gt_ref[:, rows] = g.T
        grown = lax.dot_general(x, wgu_ref[...], NT, preferred_element_type=F32)
        grad_hidden = lax.dot_general(g, wd_ref[...], NT, preferred_element_type=F32)
        gate, upper = grown[:, :both], grown[:, both:]
        gelu, slope = gelu_parts(gate)
        dg = (grad_hidden * upper * slope).astype(BF)
        du = (grad_hidden * gelu).astype(BF)
        hidden = (gelu * upper).astype(BF)
        act_ref[0, rows, :] = dg
        act_ref[1, rows, :] = du
        act_ref[2, rows, :] = hidden
        back = jnp.dot(jnp.concatenate([dg, du], axis=1), wgu_ref[...], preferred_element_type=F32)

        @pl.when(b < halves)
        def _():
            own_ref[rows, :] = back

        for i in range(halves):

            @pl.when(b == halves + i)
            def _():
                backfar_ref[i * block : (i + 1) * block, :] = back.astype(BF)
                back_out[i].start()

        out_ref[rows, :] = jnp.dot(hidden, wd_ref[...], preferred_element_type=F32).astype(BF)
        pltpu.make_async_copy(out_ref.at[rows, :], out_to.at[rows, :], leave_sem.at[b]).start()
        return carry

    lax.fori_loop(0, 2 * halves, step, 0)

    tile = d // 2
    used = 3 * (full + rest)
    dw_out = [
        remote(send_ref.at[pl.ds(c * tile, tile), :], recv_ref.at[pl.ds(c * tile, tile), :], dw_sem.at[c], core)
        for c in range(2)
    ]
    for c in range(2):
        rows = slice(c * tile, (c + 1) * tile)
        for m in range(3):
            left = gt_ref if m == 2 else xt_ref
            dw = jnp.dot(left[rows, :], act_ref[m], preferred_element_type=F32).astype(BF)
            for q, target in enumerate((sum_ref, send_ref)):
                target[rows, m * full : (m + 1) * full] = dw[:, q * full : (q + 1) * full]
                if rest:
                    at = 2 * full + q * rest
                    target[rows, 3 * full + m * rest : 3 * full + (m + 1) * rest] = dw[:, at : at + rest]
        for target in (sum_ref, send_ref):
            if used < target.shape[1]:
                target[rows, used:] = jnp.zeros((tile, target.shape[1] - used), BF)
        dw_out[c].start()
    leaving = []
    for c in range(2):
        rows = slice(c * tile, (c + 1) * tile)
        dw_out[c].wait_recv()
        sum_ref[rows, :] = (sum_ref[rows, :].astype(F32) + recv_ref[rows, :].astype(F32)).astype(BF)
        at = pl.ds(c * tile, tile)
        leaving.append(pltpu.make_async_copy(sum_ref.at[at, :], sum_to.at[at, :], end_sem.at[c]))
        leaving[-1].start()

    gains = 0.0
    for i in range(halves):
        rows, at = slice(i * block, (i + 1) * block), pl.ds(i * block, block)
        back_out[i].wait_recv()
        middle = middle_ref[rows, :]
        inv = lax.rsqrt(jnp.mean(middle * middle, axis=-1, keepdims=True) + EPS)
        upstream = own_ref[rows, :] + backin_ref[rows, :].astype(F32)
        lifted = upstream * gain_ref[...].astype(F32)[None]
        inner = jnp.mean(lifted * middle, axis=-1, keepdims=True)
        gains = gains + jnp.sum(upstream * middle * inv, axis=0, keepdims=True)
        gm = gall_ref[rows, :].astype(F32) + inv * lifted - middle * (inv * inv * inv * inner)
        gm_ref[rows, :] = gm
        ga_ref[rows, :] = gm.astype(BF)
        for k, (a, b) in enumerate(((gm_ref, gm_to), (ga_ref, ga_to))):
            leaving.append(pltpu.make_async_copy(a.at[at, :], b.at[at, :], end_sem.at[2 + 2 * i + k]))
            leaving[-1].start()
    gain_out_ref[...] = gains
    for copy in x_out + back_out + dw_out:
        copy.wait_send()
    for b in range(2 * halves):
        at = pl.ds(b * block, block)
        pltpu.make_async_copy(out_ref.at[at, :], out_to.at[at, :], leave_sem.at[b]).wait()
    for copy in leaving:
        copy.wait()


def feed_forward(x, go, gofar, middle, gain, own, other, block=256):
    slots, d = x.shape
    ff = own[0].shape[0]
    vmem, anywhere = pl.BlockSpec(memory_space=pltpu.VMEM), pl.BlockSpec(memory_space=pl.ANY)
    shape = jax.ShapeDtypeStruct
    dma = pltpu.SemaphoreType.DMA
    halves = slots // block
    packed = packed_width(ff)
    return pl.pallas_call(
        functools.partial(ffn_kernel, block, ff),
        in_specs=[anywhere] * 3 + [vmem] * 2 + [anywhere] * 6,
        out_specs=[anywhere] * 4 + [vmem],
        out_shape=[
            shape((2 * slots, d), BF),
            shape((d, packed), BF),
            shape((slots, d), F32),
            shape((slots, d), BF),
            shape((1, d), F32),
        ],
        scratch_shapes=[
            pltpu.VMEM((2 * slots, d), BF),
            pltpu.VMEM((d, packed), BF),
            pltpu.VMEM((slots, d), F32),
            pltpu.VMEM((slots, d), BF),
            pltpu.VMEM((2 * slots, d), BF),
            pltpu.VMEM((2 * slots, d), BF),
            pltpu.VMEM((4 * ff, d), BF),
            pltpu.VMEM((2 * ff, d), BF),
            pltpu.VMEM((d, 2 * slots), BF),
            pltpu.VMEM((d, 2 * slots), BF),
            pltpu.VMEM((3, 2 * slots, 2 * ff), BF),
            pltpu.VMEM((d, packed), BF),
            pltpu.VMEM((d, packed), BF),
            pltpu.VMEM((slots, d), F32),
            pltpu.VMEM((slots, d), BF),
            pltpu.VMEM((slots, d), BF),
            dma((3,)), dma((3, 2, 2)), dma((halves, 2)), dma((halves, 2)), dma((2, 2)),
            dma((2 * halves,)), dma((2 + 2 * halves,)),
        ],
        compiler_params=pltpu.CompilerParams(
            vmem_limit_bytes=VMEM_LIMIT, collective_id=2, has_side_effects=True
        ),
        cost_estimate=pl.CostEstimate(flops=36 * slots * d * ff, bytes_accessed=40 << 20, transcendentals=4 * slots * ff),
        name="feed_forward",
    )(x, go, gofar, middle, gain, *own, *other)


def backward_slot(k):
    return jnp.where(k < 4, 6 - 2 * (k & 1) + (k >> 1), 6 - 2 * (k >> 1) + (k & 1))


def backward_kernel(
    wide, heads, buckets, trows, ff,
    ga_ref, x_ref, gain_ref, gain2_ref, fsum_ref, gm_ref, e_ref, ir_ref, ih_ref, iv_ref, out_ref,
    wo_ref, ctx_ref, linv_ref, qkv_ref, wall_ref,
    gi_ref, outin_ref, small_ref, gq_ref, gk_ref, gv_ref, go_ref, fg_ref, fu_ref, fd_ref,
    gib_ref, fown_ref, ds_ref, ids_ref, nt_ref, gat_ref, dx_ref, acc_ref, part_ref, crecv_ref, frecv_ref, xarecv_ref, zarecv_ref,
    xfrecv_ref, zfrecv_ref, nsend_ref, nrecv_ref, parts_ref, srecv_ref,
    in_sem, e_sem, core_sem, far_sem, out_sem, xf_sem, zf_sem, xa_sem, za_sem, sn_sem, ss_sem,
):
    pw = 2 * HEAD_DIM
    slots, d = ga_ref.shape
    half_rows = slots // 2
    ranks = wide // 2
    chunk = d // wide
    steps = 8 + slots // trows
    u = pl.program_id(0)
    w, n, core, far, diag, side = neighbours()
    par, rank = w & 1, w >> 1
    opp = 1 - par
    peer = lambda r: (2 * (rank ^ r) + par, n)
    slot_of = backward_slot
    slot = slot_of(jnp.minimum(u, 7))

    ins = [pltpu.make_async_copy(r.at[n], ids_ref.at[t], in_sem.at[t]) for t, r in enumerate((ir_ref, ih_ref, iv_ref))]
    gm_in = pltpu.make_async_copy(gm_ref, gib_ref, in_sem.at[3])
    fown_in = pltpu.make_async_copy(fsum_ref.at[:, par], fown_ref, in_sem.at[4])
    gi_out = pltpu.make_async_copy(gib_ref, gi_ref, in_sem.at[5])
    core_out = [remote(part_ref.at[s], crecv_ref.at[i], core_sem.at[i], core) for i, s in enumerate((6, 7, 2, 3))]
    order = list(range(ranks - 1, 0, -2)) + list(range(ranks - 2, -1, -2))
    far_out = [
        [
            [
                remote(part_ref.at[4 + i, rank ^ r, p], frecv_ref.at[i, rank ^ r, p], far_sem.at[i, k, r], far)
                for r in range(ranks)
            ]
            for k, p in enumerate((opp, par))
        ]
        for i in range(2)
    ]
    out_out = [
        remote(
            out_ref.at[pl.ds(slots + i * half_rows, half_rows), :],
            outin_ref.at[pl.ds(i * half_rows, half_rows), :], out_sem.at[i], far,
        )
        for i in range(2)
    ]
    xf_out = [None] + [remote(fsum_ref.at[rank ^ r, opp], xfrecv_ref.at[r], xf_sem.at[r], side) for r in range(1, ranks)]
    some = chunk // 2
    xf_last = [
        remote(
            fsum_ref.at[rank, opp, pl.ds(k * some, some), :], xfrecv_ref.at[0, pl.ds(k * some, some), :],
            xf_sem.at[k * ranks], side,
        )
        for k in range(2)
    ]
    low_bit = lambda r: r & -r
    zf_out = [None] + [
        remote(xfrecv_ref.at[r], zfrecv_ref.at[r - 1], zf_sem.at[r - 1], peer(low_bit(r))) for r in range(1, ranks)
    ]
    feeds = lambda r: [r | (1 << b) for b in range(ranks.bit_length() - 1) if (1 << b) < (low_bit(r) if r else ranks)]
    xa_out = [
        [remote(part_ref.at[i, rank ^ r, opp], xarecv_ref.at[i, r], xa_sem.at[i, r], side) for r in range(ranks)]
        for i in range(2)
    ]
    za_out = [
        [None]
        + [
            remote(part_ref.at[i, rank ^ r, par], zarecv_ref.at[i, r - 1], za_sem.at[i, r - 1], peer(low_bit(r)))
            for r in range(1, ranks)
        ]
        for i in range(2)
    ]
    sn_out = [
        remote(nsend_ref.at[r], nrecv_ref.at[r - 1], sn_sem.at[r - 1], dev) for r, dev in ((1, core), (2, far), (3, diag))
    ]
    ss_out = [None] + [
        remote(parts_ref.at[w ^ k], srecv_ref.at[k - 1], ss_sem.at[k - 1], (w ^ k, n)) for k in range(1, wide)
    ]

    def at_edge(end, middle):
        edge = ((rank ^ (rank >> 1)) & 1) == 0
        pl.when(edge)(lambda: end())
        pl.when(jnp.logical_not(edge))(lambda: middle())

    def e_in(k):
        s = slot_of(k)
        return pltpu.make_async_copy(e_ref.at[s], ds_ref.at[s], e_sem.at[k & 1])

    def wide_f32(ref_value):
        return ref_value.astype(F32)

    @pl.when(u == 0)
    def _():
        e_in(0).start()
        for copy in [fown_in] + ins + [gm_in]:
            copy.start()
        greet([core, far, diag] + [(w ^ k, n) for k in range(1, wide)])
        if ranks == 4:
            xf_out[3].start()
            at_edge(xf_out[1].start, xf_out[2].start)
            at_edge(xf_out[2].start, xf_out[1].start)
        else:
            for r in range(ranks - 1, 0, -1):
                xf_out[r].start()
        out_out[0].start()
        x = x_ref[...].astype(F32)
        inv = lax.rsqrt(jnp.mean(x * x, axis=-1, keepdims=True) + EPS)
        nt_ref[...] = (x * inv * gain_ref[...].astype(F32)[None]).astype(BF).T
        gat_ref[...] = ga_ref[...].T
        dx_ref[...] = jnp.zeros_like(dx_ref)
        acc_ref[...] = jnp.zeros_like(acc_ref)
        parts_ref[...] = jnp.zeros_like(parts_ref)

    @pl.when(u < 8)
    def _():
        e_in(u).wait()

        @pl.when(u < 7)
        def _():
            e_in(u + 1).start()

        lane = lax.broadcasted_iota(I32, (slots, pw), 1)
        low = lane < HEAD_DIM
        do2 = (lax.dot_general(ga_ref[...], wo_ref[...], NT, preferred_element_type=F32) * linv_ref[...]).astype(BF)
        prod = do2.astype(F32) * ctx_ref[...].astype(F32)
        q2, k2, v2 = qkv_ref[0], qkv_ref[1], qkv_ref[2]
        vx = jnp.concatenate([v2, jnp.where(lane < 2, 1.0, 0.0).astype(BF)], axis=1)
        do_t, q_t = do2.T, q2.T
        zero = jnp.zeros_like(do2)
        dq, dk, dv = [], [], []
        for sub in range(2):
            mine = low if sub == 0 else jnp.logical_not(low)
            row = -jnp.sum(jnp.where(mine, prod, 0.0), axis=1, keepdims=True)
            head_part = row.astype(BF).astype(F32)
            extra = jnp.where(lane == 0, head_part, jnp.where(lane == 1, row - head_part, 0.0)).astype(BF)
            dox = jnp.concatenate([jnp.where(mine, do2, zero), extra], axis=1)
            t = lax.dot_general(dox, vx, NT, preferred_element_type=F32)
            e = ds_ref[slot, sub]
            ds = (e.astype(F32) * t).astype(BF)
            dv.append(jnp.dot(do_t[sub * HEAD_DIM : (sub + 1) * HEAD_DIM], e, preferred_element_type=F32))
            ds_ref[slot, sub] = ds
            dk.append(jnp.dot(q_t[sub * HEAD_DIM : (sub + 1) * HEAD_DIM], ds, preferred_element_type=F32))
            dq.append(jnp.dot(ds, k2, preferred_element_type=F32))
        joined = jnp.concatenate(
            [
                jnp.where(low, dq[0], dq[1]).astype(BF),
                jnp.concatenate(dk, axis=0).T.astype(BF),
                jnp.concatenate(dv, axis=0).T.astype(BF),
            ],
            axis=1,
        )
        weights = jnp.concatenate([wall_ref[m] for m in range(3)], axis=1)
        dx_ref[...] += lax.dot_general(joined, weights, NT, preferred_element_type=F32)
        part = jnp.dot(nt_ref[...], joined, preferred_element_type=F32).astype(BF)
        part_ref[slot, :, :, :, : 3 * pw] = part.reshape(ranks, 2, chunk, 3 * pw)
        part = jnp.dot(gat_ref[...], ctx_ref[...], preferred_element_type=F32).astype(BF)
        part_ref[slot, :, :, :, 3 * pw :] = part.reshape(ranks, 2, chunk, pw)

    @pl.when(u >= 8)
    def _():
        blk = 16
        one, zero = jnp.ones((blk, 4 * slots), BF), jnp.zeros((blk, 4 * slots), BF)

        @pl.when(u == 8)
        def _():
            for copy in ins:
                copy.wait()

        group = 4

        def sub_block(c, carry):
            starts = [pl.multiple_of((u - 8) * trows + (c * group + k) * blk, blk) for k in range(group)]
            g = jnp.concatenate(
                [
                    jnp.concatenate([ds_ref[s, sub, pl.ds(at, blk), :] for s in range(8) for sub in range(2)], axis=0)
                    for at in starts
                ],
                axis=1,
            )
            for t in range(3):
                ids = jnp.concatenate([ids_ref[t, pl.ds(at, blk), :].astype(F32).astype(BF) for at in starts], axis=1)
                hot = jnp.concatenate([jnp.where(ids == jnp.bfloat16(b), one, zero) for b in range(buckets)], axis=0)
                span = slice(t * buckets * blk, (t + 1) * buckets * blk)
                acc_ref[span, :] += lax.dot_general(hot, g, NT, preferred_element_type=F32)
            return carry

        lax.fori_loop(0, trows // (blk * group), sub_block, 0)

    def event(step):
        return lambda body: pl.when(u == step)(body)

    def core_stage(i):
        core_out[i].wait_recv()
        for p in (opp, par):
            total = wide_f32(part_ref[4 + i, :, p]) + wide_f32(crecv_ref[i, :, p])
            part_ref[4 + i, :, p] = total.astype(BF)
        for r in order:
            far_out[i][0][r].start()

    def own_sides():
        for i in range(2):
            for r in order:
                far_out[i][1][r].start()

    def far_stage(i):
        core_out[2 + i].wait_recv()
        for r in order:
            far_out[i][0][r].wait_recv()
            k = rank ^ r
            total = wide_f32(part_ref[i, k, opp]) + wide_f32(crecv_ref[2 + i, k, opp]) + wide_f32(frecv_ref[i, k, opp])
            part_ref[i, k, opp] = total.astype(BF)
            xa_out[i][r].start()

    def side_stage(i, r):
        far_out[i][1][r].wait_recv()
        xa_out[i][r].wait_recv()
        k = rank ^ r
        total = wide_f32(part_ref[i, k, par]) + wide_f32(crecv_ref[2 + i, k, par])
        total = total + wide_f32(frecv_ref[i, k, par]) + wide_f32(xarecv_ref[i, r])
        part_ref[i, k, par] = total.astype(BF)
        if r & 1:
            za_out[i][r].start()

    def rank_stage(i, r):
        total = wide_f32(part_ref[i, rank ^ r, par])
        for k in feeds(r):
            za_out[i][k].wait_recv()
            total = total + wide_f32(zarecv_ref[i, k - 1])
        if r == 0:
            return total
        part_ref[i, rank ^ r, par] = total.astype(BF)
        za_out[i][r].start()

    def ffn_stage(r):
        for copy in xf_last if r == 0 else [xf_out[r]]:
            copy.wait_recv()
        total = wide_f32(fown_ref[rank ^ r]) + wide_f32(xfrecv_ref[r])
        for k in feeds(r):
            zf_out[k].wait_recv()
            total = total + wide_f32(zfrecv_ref[k - 1])
        if r == 0:
            return total
        xfrecv_ref[r] = total.astype(BF)
        zf_out[r].start()

    def input_gradient():
        gm_in.wait()
        x = x_ref[...].astype(F32)
        inv = lax.rsqrt(jnp.mean(x * x, axis=-1, keepdims=True) + EPS)
        upstream = dx_ref[...]
        lifted = upstream * gain_ref[...].astype(F32)[None]
        inner = jnp.mean(lifted * x, axis=-1, keepdims=True)
        gib_ref[...] = gib_ref[...] + inv * lifted - x * (inv * inv * inv * inner)
        gi_out.start()
        gains = jnp.sum(upstream * x * inv, axis=0, keepdims=True)
        lanes = d // LANES
        for r in range(4):
            for j in range(lanes):
                span = slice(j * LANES, (j + 1) * LANES)
                nsend_ref[r, 3 * buckets + j : 3 * buckets + j + 1, :] = gains[:, span]
                nsend_ref[r, 3 * buckets + lanes + j : 3 * buckets + lanes + j + 1, :] = gain2_ref[:, span]

    plan = [[] for _ in range(steps)]
    for i in range(2):
        plan[2 * i].append(core_out[i].start)
        plan[2 * i + 1].append(functools.partial(core_stage, i))
        plan[4 + i].append(core_out[2 + i].start)
    plan[3].append(own_sides)
    plan[1].append(fown_in.wait)
    if ranks == 4:
        turn = lambda a, b: functools.partial(at_edge, functools.partial(ffn_stage, a), functools.partial(ffn_stage, b))
        plan[2].append(functools.partial(ffn_stage, 3))
        plan[5].append(turn(1, 2))
        plan[8].append(turn(2, 1))
    else:
        for k, r in enumerate(range(ranks - 1, 0, -1)):
            plan[3 + k * 6 // ranks].append(functools.partial(ffn_stage, r))
    plan[6].append(functools.partial(far_stage, 0))
    plan[7].append(input_gradient)
    plan[8].append(functools.partial(far_stage, 1))
    plan[8].append(xf_last[0].start)
    plan[10].extend(functools.partial(side_stage, 0, r) for r in order)
    plan[11].extend(functools.partial(rank_stage, 0, r) for r in range(ranks - 2, 0, -2))
    for k in range(steps):

        @pl.when(u == k)
        def _():
            for action in plan[k]:
                action()

    @pl.when(u == steps - 1)
    def _():
        blk, cols = 16, 16 * 16
        same = lax.broadcasted_iota(I32, (blk, cols), 0) == (lax.broadcasted_iota(I32, (blk, cols), 1) & (blk - 1))
        picked = [
            jnp.sum(jnp.where(same, acc_ref[b * blk : (b + 1) * blk, :], 0.0), axis=0, keepdims=True)
            for b in range(3 * buckets)
        ]
        picked = jnp.concatenate(picked, axis=0)
        source = lax.broadcasted_iota(I32, (cols, LANES), 0) >> 4
        target = lax.broadcasted_iota(I32, (cols, LANES), 1)
        choose = jnp.where(source == target, 1.0, 0.0).astype(F32)
        sums = jnp.dot(picked, choose, preferred_element_type=F32, precision=lax.Precision.HIGHEST)
        for r in range(4):
            nsend_ref[r, : 3 * buckets, :] = pltpu.roll(sums, LANES - heads * r, 1) if r else sums
        for copy in sn_out + out_out[1:]:
            copy.start()

        def finish(i):
            total = rank_stage(i, 0)
            cols = slice(i * pw, (i + 1) * pw)
            gq_ref[:, cols] = total[:, :pw]
            gk_ref[:, cols] = total[:, pw : 2 * pw]
            gv_ref[:, cols] = total[:, 2 * pw : 3 * pw]
            go_ref[cols, :] = total[:, 3 * pw :].T

        for r in order[:-1]:
            side_stage(1, r)
        for copy in sn_out:
            copy.wait()
        nsend_ref[1] = nsend_ref[0] + nrecv_ref[0] + nrecv_ref[1] + nrecv_ref[2]
        lanes, own = d // LANES, buckets // wide
        for k in range(wide):
            row = 3 * buckets + k * d // wide // LANES
            parts_ref[k, 0:1, :] = nsend_ref[1, row : row + 1, :]
            parts_ref[k, 1:2, :] = nsend_ref[1, row + lanes : row + lanes + 1, :]
            for t in range(3):
                at = t * buckets + k * own
                parts_ref[k, 2 + t * own : 2 + (t + 1) * own, :] = nsend_ref[1, at : at + own, :]
        for copy in ss_out[1:]:
            copy.start()
        xf_last[1].start()
        side_stage(1, 0)
        finish(0)
        for r in range(ranks - 2, 0, -2):
            rank_stage(1, r)
        total = ffn_stage(0)
        full, rest = split_quarter(ff)
        for m, ref in enumerate((fg_ref, fu_ref, fd_ref)):
            ref[:full, :] = total[:, m * full : (m + 1) * full].T
            if rest:
                ref[full:, :] = total[:, 3 * full + m * rest : 3 * full + (m + 1) * rest].T
        total = parts_ref[w]
        for k in range(1, wide):
            ss_out[k].wait_recv()
            total = total + srecv_ref[k - 1]
        small_ref[...] = total
        finish(1)
        gi_out.wait()
        for copy in out_out:
            copy.wait()
        for i in range(2):
            for copy in far_out[i][0] + far_out[i][1] + xa_out[i] + za_out[i][1:]:
                copy.wait_send()
        for copy in core_out + xf_out[1:] + xf_last + zf_out[1:] + ss_out[1:]:
            copy.wait_send()


def backward(wide, buckets, ff, ga, x, gain, gain2, fsum, gm, e, ids, out, wo_all, ctx, linv, qkv, w_all, trows=128):
    slots, d = x.shape
    heads = 4
    pw = 2 * HEAD_DIM
    ranks, chunk = wide // 2, d // wide
    packed = fsum.shape[-1]
    width = heads * HEAD_DIM
    small = 3 * buckets + 2 * d // LANES
    place = -(-(2 + 3 * (buckets // wide)) // 8) * 8
    vmem, anywhere = pl.BlockSpec(memory_space=pltpu.VMEM), pl.BlockSpec(memory_space=pl.ANY)
    shape = jax.ShapeDtypeStruct
    dma = pltpu.SemaphoreType.DMA

    def slot(u):
        return backward_slot(jnp.minimum(u, 7))

    return pl.pallas_call(
        functools.partial(backward_kernel, wide, heads, buckets, trows, ff),
        grid=(8 + slots // trows,),
        in_specs=[vmem] * 4 + [anywhere] * 7 + [
            pl.BlockSpec((pw, d), lambda u: (slot(u), 0)),
            pl.BlockSpec((slots, pw), lambda u: (0, slot(u))),
            pl.BlockSpec((slots, pw), lambda u: (0, slot(u))),
            pl.BlockSpec((3, slots, pw), lambda u: (0, 0, slot(u))),
            pl.BlockSpec((3, d, pw), lambda u: (0, 0, slot(u))),
        ],
        out_specs=[anywhere] * 2 + [vmem] * 8,
        out_shape=[
            shape((slots, d), F32),
            shape((slots, d), BF),
            shape((place, LANES), F32),
            shape((chunk, width), F32),
            shape((chunk, width), F32),
            shape((chunk, width), F32),
            shape((width, chunk), F32),
            shape((ff, chunk), F32),
            shape((ff, chunk), F32),
            shape((ff, chunk), F32),
        ],
        scratch_shapes=[
            pltpu.VMEM((slots, d), F32),
            pltpu.VMEM((ranks, chunk, packed), BF),
            pltpu.VMEM((8, 2, slots, slots), BF),
            pltpu.VMEM((3, slots, slots), I32),
            pltpu.VMEM((d, slots), BF),
            pltpu.VMEM((d, slots), BF),
            pltpu.VMEM((slots, d), F32),
            pltpu.VMEM((3 * buckets * 16, 16 * 16), F32),
            pltpu.VMEM((8, ranks, 2, chunk, 4 * pw), BF),
            pltpu.VMEM((4, ranks, 2, chunk, 4 * pw), BF),
            pltpu.VMEM((2, ranks, 2, chunk, 4 * pw), BF),
            pltpu.VMEM((2, ranks, chunk, 4 * pw), BF),
            pltpu.VMEM((2, ranks - 1, chunk, 4 * pw), BF),
            pltpu.VMEM((ranks, chunk, packed), BF),
            pltpu.VMEM((ranks - 1, chunk, packed), BF),
            pltpu.VMEM((4, small, LANES), F32),
            pltpu.VMEM((3, small, LANES), F32),
            pltpu.VMEM((wide, place, LANES), F32),
            pltpu.VMEM((wide - 1, place, LANES), F32),
            dma((6,)), dma((2,)), dma((4, 2)), dma((2, 2, ranks, 2)), dma((2, 2)), dma((ranks + 1, 2)), dma((ranks - 1, 2)),
            dma((2, ranks, 2)), dma((2, ranks - 1, 2)), dma((3, 2)), dma((wide - 1, 2)),
        ],
        compiler_params=pltpu.CompilerParams(
            vmem_limit_bytes=VMEM_LIMIT, collective_id=3, has_side_effects=True
        ),
        cost_estimate=pl.CostEstimate(flops=30 * slots * d * d, bytes_accessed=60 << 20, transcendentals=0),
        name="backward",
    )(ga, x, gain, gain2, fsum, gm, e, *ids, out, wo_all, ctx, linv, qkv, w_all)


def results_kernel(
    wide, narrow, buckets, heads, middle_ref, out_ref, outin_ref, gi_ref, small_ref, *rest,
):
    sources, (block_ref, go_ref, ga_ref, gf_ref, tr_ref, th_ref, tv_ref), targets = rest[:7], rest[7:14], rest[14:]
    block_ref[...] = (middle_ref[...] + (out_ref[...].astype(F32) + outin_ref[...].astype(F32))).astype(BF)
    go_ref[...] = gi_ref[...]

    @pl.when(pl.program_id(0) == 0)
    def _():
        for a, b in zip(sources, targets):
            b[...] = a[...]
        w, n = lax.axis_index("wide"), lax.axis_index("narrow")
        d = middle_ref.shape[1]
        per, own = d // (wide * narrow), buckets // wide
        start = (w * narrow + n) * per
        for k, ref in enumerate((ga_ref, gf_ref)):
            row = small_ref[k : k + 1, :]
            lane = lax.broadcasted_iota(I32, (per, LANES), 1)
            mine = lane == lax.broadcasted_iota(I32, (per, LANES), 0) + start % LANES
            ref[...] = jnp.sum(jnp.where(mine, jnp.broadcast_to(row, (per, LANES)), 0.0), axis=1)
        for k, ref in enumerate((tr_ref, th_ref, tv_ref)):
            ref[...] = small_ref[2 + k * own : 2 + (k + 1) * own, :heads]


def results(wide, narrow, buckets, heads, middle, out, outin, small, grad_input, big):
    slots, d = middle.shape
    shape = jax.ShapeDtypeStruct
    per, own = d // (wide * narrow), buckets // wide
    rows = pl.BlockSpec((slots // 2, d), lambda i: (i, 0))
    whole = lambda *sh: pl.BlockSpec(sh, lambda i: (0,) * len(sh))
    return pl.pallas_call(
        functools.partial(results_kernel, wide, narrow, buckets, heads),
        grid=(2,),
        in_specs=[rows] * 4 + [whole(*small.shape)] + [whole(*x.shape) for x in big],
        out_specs=[rows] * 2 + [whole(per)] * 2 + [whole(own, heads)] * 3 + [whole(*x.shape) for x in big],
        out_shape=[shape((slots, d), BF), shape((slots, d), F32)] + [shape((per,), F32)] * 2
        + [shape((own, heads), F32)] * 3 + [shape(x.shape, x.dtype) for x in big],
        compiler_params=pltpu.CompilerParams(vmem_limit_bytes=VMEM_LIMIT),
        name="results",
    )(middle, out, outin, grad_input, small, *big)


def shards(
    wide, narrow, hidden_in, grad_out, gain_attn, gain_ffn, w_query, w_key, w_value, w_output,
    table_rel, table_horiz, table_vert, wi_gate, wi_up, wo_ffn, counts, patch_mask,
    bucket_rel, bucket_horiz, bucket_vert,
):
    slots = bucket_rel.shape[1]
    rows, d = hidden_in.shape
    buckets, heads = table_rel.shape
    width = w_query.shape[1]
    ff = wi_gate.shape[1]
    assert rows == slots and narrow == 4 and wide >= 4 and heads * HEAD_DIM == width
    ids = (bucket_rel, bucket_horiz, bucket_vert)

    qkv, exps, context, linv, w_all, wo_all, middle, ffn_own, grad_far, wg_core, wu_core, wd_core = forward(
        counts, patch_mask, hidden_in, gain_attn, gain_ffn, (table_rel.T, table_horiz.T, table_vert.T),
        w_query, w_key, w_value, w_output, ids, grad_out, wi_gate.T, wi_up.T, wo_ffn,
    )
    out, ffn_sum, grad_middle, grad_attn, grad_gain_second = feed_forward(
        ffn_own, grad_out, grad_far, middle, gain_ffn,
        (wi_gate.T, wi_up.T, wo_ffn), (wg_core, wu_core, wd_core),
    )
    grad_input, out_in, small, gq, gk, gv, go, fg, fu, fd = backward(
        wide, buckets, ff, grad_attn, hidden_in, gain_attn, grad_gain_second,
        ffn_sum.reshape(wide // 2, 2, d // wide, -1), grad_middle, exps, ids, out,
        wo_all, context, linv, qkv, w_all,
    )
    block_out, grad_input, gain1, gain2, rel, horiz, vert, gq, gk, gv, go, fg, fu, fd = results(
        wide, narrow, buckets, heads, middle, out, out_in, small, grad_input, (gq, gk, gv, go, fg, fu, fd)
    )
    return (
        block_out, grad_input, gain1, gain2, gq, gk, gv, go, rel, horiz, vert, fg.T, fu.T, fd,
    )


def solution(mesh):
    rows, both = P(("wide", "narrow"), None), P(("wide", "narrow"))
    cols, across = P(None, "narrow"), P("narrow", None)
    grid, turned = P("wide", "narrow"), P("narrow", "wide")
    pages = P("wide", None, None)
    return jax.shard_map(
        functools.partial(shards, mesh.shape["wide"], mesh.shape["narrow"]),
        mesh=mesh,
        in_specs=(
            rows, rows, P(), P(), cols, cols, cols, across, cols, cols, cols, cols, cols, across,
            P("wide"), P("wide", None), pages, pages, pages,
        ),
        out_specs=(
            rows, rows, both, both, grid, grid, grid, turned, grid, grid, grid, grid, grid, turned,
        ),
        check_vma=False,
    )
```
